128 devices in a mesh: lat: 16 (over z_hi, y, core), lon: 8 (over x, z_lo).
Axes of the slice: x: 4, y: 4, z: 4 (z_hi: 2, z_lo: 2; z = z_hi * 2 + z_lo), core: 2. Of those that a mesh axis runs over, the one named last changes fastest.
Arguments:
- spectral: bfloat16 [6, 64, 640, 1280], P(None, 'lon', 'lat'), may hold values from -6 to 6
- legendre: bfloat16 [640, 1280, 256], P('lat'), may hold values from -0.15625 to 0.15625
- wave_ids: int32 [640], replicated, may hold values from 0 to 639, each once
- points: int32 [256], P('lat'), may hold values from 1024 to 2048
- tracers: bfloat16 [16, 64, 256, 2048], P(None, None, 'lat', 'lon'), may hold values from -6 to 6
- react_base: float32 [16, 16], replicated, may hold values from -0.75 to 0.75
- react_temp: float32 [16, 16], replicated, may hold values from -0.75 to 0.75
- active_ids: int32 [4], replicated, may hold values from 0 to 15, as said below
Outputs:
- tracers_new: bfloat16 [16, 64, 256, 2048], P(None, None, 'lat', 'lon')
- active: float32 [4, 64, 256, 2048], P(None, 'lon', 'lat')
The draws below stay inside these ranges and needn't reach their ends.
Inputs may be any that keep to these rules, and one draw needn't show every extreme that they name: `active_ids`: distinct tracer indices. `wave_ids`: each slot a different wavenumber.
All inputs are finite; a program needn't handle non-finite values.
Results may differ from the reference program's by a relative error of at most 0.0042.
Values may be sent and summed in bfloat16 or wider, within the bound.
A program may use at most 256 MiB of HBM per device.

```python
import jax
import jax.numpy as jnp
from jax import lax

NSPEC = 1280
MW = 640
TRACERS = 16
ACTIVE = 4
NLAT = 256
LEV = 64
NLON = 2048


def draw_active_ids(key, part):
    return jax.random.permutation(key, TRACERS)[:ACTIVE].astype(jnp.int32)


def place_ends(result, stream_key, low, high):
    place = [jax.random.randint(jax.random.fold_in(stream_key, axis), (), 0, length) for axis, length in enumerate(result.shape)]
    main_axis = result.shape.index(max(result.shape))
    next_to = place[:main_axis] + [(place[main_axis] + 1) % result.shape[main_axis]] + place[main_axis + 1:]
    return result.at[tuple(place)].set(low).at[tuple(next_to)].set(high)


def steps_of(stream_key, shape, pieces, least, top_value):
    def one(axis_at, shards_of):
        heights = jax.random.uniform(jax.random.fold_in(jax.random.fold_in(stream_key, 6), axis_at), (shards_of,), jnp.float32, least / len(pieces), top_value / len(pieces))
        return jnp.repeat(jnp.exp(heights), shape[axis_at] // shards_of).reshape((-1,) + (1,) * (len(shape) - axis_at - 1))

    factor_of = one(*pieces[0])
    for cut in pieces[1:]:
        factor_of = factor_of * one(*cut)
    return factor_of


def normal_values(rng, extent, spread, reach, cuts=(), dtype=jnp.bfloat16):
    entries = spread * jax.random.normal(rng, extent, jnp.float32)
    if cuts:
        entries = entries * steps_of(rng, extent, cuts, -0.22, 0.18)
    return jnp.clip(entries, -reach, reach).astype(dtype)


def setup_inputs(seed: int = 0) -> dict:
    key_list = jax.random.split(jax.random.key(seed), 9)
    spectral = normal_values(key_list[0], (6, LEV, MW, NSPEC), 1.0, 6.0, ((1, 8), (2, 16)))
    legendre = normal_values(key_list[1], (MW, NSPEC, NLAT), NSPEC ** -0.5, 0.15625, ((0, 16),))
    wave_ids = jax.random.permutation(key_list[2], MW).astype(jnp.int32)
    points = place_ends(jax.random.randint(key_list[3], (NLAT,), NLON // 2, NLON + 1), jax.random.fold_in(key_list[3], 1), NLON // 2, NLON).astype(jnp.int32)
    tracers = normal_values(key_list[4], (TRACERS, LEV, NLAT, NLON), 1.0, 6.0, ((2, 16), (3, 8)))
    react_base = normal_values(key_list[5], (TRACERS, TRACERS), 64 ** -0.5, 0.75, (), jnp.float32)
    react_temp = normal_values(key_list[6], (TRACERS, TRACERS), 64 ** -0.5, 0.75, (), jnp.float32)
    active_ids = draw_active_ids(jax.random.fold_in(key_list[8], 71), 0)
    return dict(spectral=spectral, legendre=legendre, wave_ids=wave_ids, points=points, tracers=tracers, react_base=react_base, react_temp=react_temp, active_ids=active_ids)


def reference(spectral, legendre, wave_ids, points, tracers, react_base, react_temp, active_ids):
    high = lax.Precision.HIGHEST
    fourier = jnp.einsum('rlmn,mnj->rlmj', spectral.astype(jnp.float32), legendre.astype(jnp.float32), precision=high)
    fourier = lax.optimization_barrier(fourier.astype(jnp.bfloat16)).astype(jnp.float32)
    parted = fourier.reshape(3, 2, LEV, MW, NLAT)
    by_row = jnp.moveaxis(parted, 4, 0)
    columns = jnp.arange(NLON).astype(jnp.int32)

    def one_row(item):
        coeffs, count = item
        product = columns[:, None] * wave_ids[None, :].astype(jnp.int32) % count
        angle = 2.0 * jnp.pi * product.astype(jnp.float32) / count.astype(jnp.float32)
        cosine = lax.optimization_barrier(jnp.cos(angle).astype(jnp.bfloat16)).astype(jnp.float32)
        sine = lax.optimization_barrier(jnp.sin(angle).astype(jnp.bfloat16)).astype(jnp.float32)
        first = jnp.einsum('flm,im->fli', coeffs[:, 0], cosine, precision=high)
        second = jnp.einsum('flm,im->fli', coeffs[:, 1], sine, precision=high)
        return first - second
    rows = lax.map(one_row, (by_row, points))
    grid = jnp.transpose(rows, (1, 2, 0, 3)) / jnp.sqrt(jnp.float32(MW))
    wind_u, wind_v, temper = (grid[0], grid[1], grid[2])
    state = tracers.astype(jnp.float32)
    padded = jnp.pad(state, ((0, 0), (0, 0), (1, 1), (1, 1)))
    east = padded[:, :, 1:-1, 2:]
    west = padded[:, :, 1:-1, :-2]
    north = padded[:, :, 2:, 1:-1]
    south = padded[:, :, :-2, 1:-1]
    moved = state - 0.1 * wind_u * (east - west) - 0.1 * wind_v * (north - south) + 0.05 * (east + west + north + south - 4.0 * state)
    base_term = jnp.einsum('st,tlji->slji', react_base, moved, precision=high)
    temp_term = jnp.einsum('st,tlji->slji', react_temp, moved, precision=high)
    mask = (columns[None, :] < points[:, None]).astype(jnp.float32)
    reacted = (moved + base_term + temper * temp_term) * mask
    active = jnp.take(reacted, active_ids, axis=0)
    return (reacted.astype(jnp.bfloat16), active)
```

```python
import functools

import jax
import jax.numpy as jnp
from jax import lax
from jax.experimental import pallas as pl
from jax.experimental.pallas import tpu as pltpu
from jax.sharding import Mesh
from jax.sharding import PartitionSpec as P

LON = ("lon_0", "lon_1")


def whole_of(value, axes, dim):
    if not axes:
        return value
    nearer = lax.all_gather(value, axes[-1], axis=dim, tiled=True)
    return whole_of(nearer, axes[:-1], dim)


def part_angles(offsets, wave_ids, points):
    product = offsets[None, :, None] * wave_ids[None, None, :] % points[:, None, None]
    angle = 2.0 * jnp.pi * product.astype(jnp.float32) / points[:, None, None].astype(jnp.float32)
    return (jnp.cos(angle), jnp.sin(angle))


def rows_of(ref, start, size, stride):
    return jnp.concatenate([ref[k, pl.ds(start, size, stride=stride), :] for k in range(2)], axis=1)


def edge_kernel(tr_ref, low_ref, high_ref, col_ref, wide, acc):
    h = pl.program_id(0)
    lane = lax.broadcasted_iota(jnp.int32, (256, 128), 1)

    @pl.when(h == 0)
    def _():
        acc[...] = jnp.zeros_like(acc)

    def level(l, carry):
        x = tr_ref[:, l].reshape(256, 256).astype(jnp.float32)
        for k in range(2):
            wide[k] = x[:, 128 * k : 128 * k + 128]
        low_ref[l] = rows_of(wide, 0, 16, 16).astype(jnp.bfloat16)
        high_ref[l] = rows_of(wide, 15, 16, 16).astype(jnp.bfloat16)
        at = h * 8 + l
        first = pltpu.roll(x[:, :128], at, 1)
        last = pltpu.roll(x[:, 128:], lax.rem(at + 65, 128), 1)
        acc[...] = jnp.where(lane == at, first, jnp.where(lane == at + 64, last, acc[...]))
        return carry

    lax.fori_loop(0, 8, level, 0)

    @pl.when(h == pl.num_programs(0) - 1)
    def _():
        col_ref[...] = acc[...].astype(jnp.bfloat16)


def edges_of(tracers):
    return pl.pallas_call(
        edge_kernel,
        grid=(8,),
        in_specs=[pl.BlockSpec((16, 8, 16, 256), lambda h: (0, h, 0, 0))],
        out_specs=[
            pl.BlockSpec((8, 16, 256), lambda h: (h, 0, 0)),
            pl.BlockSpec((8, 16, 256), lambda h: (h, 0, 0)),
            pl.BlockSpec((256, 128), lambda h: (0, 0)),
        ],
        out_shape=[
            jax.ShapeDtypeStruct((64, 16, 256), jnp.bfloat16),
            jax.ShapeDtypeStruct((64, 16, 256), jnp.bfloat16),
            jax.ShapeDtypeStruct((256, 128), jnp.bfloat16),
        ],
        scratch_shapes=[pltpu.VMEM((2, 256, 128), jnp.float32), pltpu.VMEM((256, 128), jnp.float32)],
        name="edges",
    )(tracers)


def chem_kernel(
    ids_ref, tr_ref, wind_ref, north_ref, south_ref, east_ref, west_ref, mask_ref, base_ref, temp_ref,
    out_ref, act_ref, wide, east, west, mix, moved, moved_b,
):
    h = pl.program_id(0)

    @pl.when(h == 0)
    def _():
        east[...] = east_ref[...].astype(jnp.float32)
        west[...] = west_ref[...].astype(jnp.float32)
        row = lax.broadcasted_iota(jnp.int32, (256, 16), 0)
        col = lax.broadcasted_iota(jnp.int32, (256, 16), 1)
        spread = jnp.where(row // 16 == col, 1.0, 0.0).astype(jnp.bfloat16)
        row = lax.broadcasted_iota(jnp.int32, (256, 256), 0)
        col = lax.broadcasted_iota(jnp.int32, (256, 256), 1)
        same = row % 16 == col % 16
        for k, ref in enumerate((base_ref, temp_ref)):
            rows = jnp.dot(spread, ref[...].astype(jnp.bfloat16), preferred_element_type=jnp.float32)
            full = lax.dot_general(
                rows.astype(jnp.bfloat16), spread, (((1,), (1,)), ((), ())), preferred_element_type=jnp.float32
            )
            mix[pl.ds(256 * k, 256), :] = jnp.where(same, full, 0.0).astype(jnp.bfloat16)

    for k in range(2):
        wide[k] = wind_ref[0, :, 128 * k : 128 * k + 128].astype(jnp.float32)
    lane = lax.broadcasted_iota(jnp.int32, (16, 128), 1)
    row = lax.broadcasted_iota(jnp.int32, (16, 256), 0)
    lane_low, lane_high = lane == 0, lane == 127
    row_low, row_high = row == 0, row == 15
    mask = mask_ref[...]

    def level(l, carry):
        at = h * 8 + l
        u = 0.1 * rows_of(wide, l, 16, 24)
        v = 0.1 * rows_of(wide, 8 + l, 16, 24)
        temper = rows_of(wide, 16 + l, 16, 24)
        east_w, west_w = 0.05 - u, 0.05 + u
        north_w, south_w = 0.05 - v, 0.05 + v
        north = north_ref[l].astype(jnp.float32)
        south = south_ref[l].astype(jnp.float32)
        for t in range(16):
            x = tr_ref[t, l].astype(jnp.float32)
            xl, xr = x[:, :128], x[:, 128:]
            he = pltpu.roll(east[pl.ds(16 * t, 16), :], 127 - at, 1)
            hw = pltpu.roll(west[pl.ds(16 * t, 16), :], 64 - at, 1)
            el, er = pltpu.roll(xl, 127, 1), pltpu.roll(xr, 127, 1)
            wl, wr = pltpu.roll(xl, 1, 1), pltpu.roll(xr, 1, 1)
            xe = jnp.concatenate([jnp.where(lane_high, er, el), jnp.where(lane_high, he, er)], axis=1)
            xw = jnp.concatenate([jnp.where(lane_low, hw, wl), jnp.where(lane_low, wl, wr)], axis=1)
            xn = jnp.where(row_high, north[t : t + 1, :], pltpu.roll(x, 15, 0))
            xs = jnp.where(row_low, south[t : t + 1, :], pltpu.roll(x, 1, 0))
            q = 0.8 * x + east_w * xe + west_w * xw + north_w * xn + south_w * xs
            moved[t] = q
            moved_b[pl.ds(16 * t, 16), :] = q.astype(jnp.bfloat16)
        y = jnp.dot(mix[...], moved_b[...], preferred_element_type=jnp.float32)
        for t in range(16):
            q = (moved[t] + y[16 * t : 16 * t + 16] + temper * y[256 + 16 * t : 272 + 16 * t]) * mask
            moved[t] = q
            out_ref[t, l] = q.astype(jnp.bfloat16)
        for a in range(4):
            act_ref[0, a, l] = moved[ids_ref[a]].astype(jnp.bfloat16)
        return carry

    lax.fori_loop(0, 8, level, 0)


def chemistry(tracers, winds, north, south, east, west, mask, base, temp, ids):
    whole = lambda h, i: (0, 0)
    return pl.pallas_call(
        chem_kernel,
        grid_spec=pltpu.PrefetchScalarGridSpec(
            num_scalar_prefetch=1,
            grid=(8,),
            in_specs=[
                pl.BlockSpec((16, 8, 16, 256), lambda h, i: (0, h, 0, 0)),
                pl.BlockSpec((1, 384, 256), lambda h, i: (h, 0, 0)),
                pl.BlockSpec((8, 16, 256), lambda h, i: (h, 0, 0)),
                pl.BlockSpec((8, 16, 256), lambda h, i: (h, 0, 0)),
                pl.BlockSpec((256, 128), whole),
                pl.BlockSpec((256, 128), whole),
                pl.BlockSpec((16, 256), whole),
                pl.BlockSpec((16, 16), whole),
                pl.BlockSpec((16, 16), whole),
            ],
            out_specs=[
                pl.BlockSpec((16, 8, 16, 256), lambda h, i: (0, h, 0, 0)),
                pl.BlockSpec((1, 4, 8, 16, 256), lambda h, i: (h, 0, 0, 0, 0)),
            ],
            scratch_shapes=[
                pltpu.VMEM((2, 384, 128), jnp.float32),
                pltpu.VMEM((256, 128), jnp.float32),
                pltpu.VMEM((256, 128), jnp.float32),
                pltpu.VMEM((512, 256), jnp.bfloat16),
                pltpu.VMEM((16, 16, 256), jnp.float32),
                pltpu.VMEM((256, 256), jnp.bfloat16),
            ],
        ),
        out_shape=[
            jax.ShapeDtypeStruct((16, 64, 16, 256), jnp.bfloat16),
            jax.ShapeDtypeStruct((8, 4, 8, 16, 256), jnp.bfloat16),
        ],
        name="chemistry",
    )(ids, tracers, winds, north, south, east, west, mask, base, temp)


def shifted(value, axis):
    size = lax.axis_size(axis)
    up = [(i, (i + 1) % size) for i in range(size - 1)]
    return lax.ppermute(value, axis, up)


def shifted_back(value, axis):
    size = lax.axis_size(axis)
    up = [((i + 1) % size, i) for i in range(size - 1)]
    return lax.ppermute(value, axis, up)


def body(spectral, legendre, wave_ids, points, tracers, react_base, react_temp, active_ids):
    low, high, cols = edges_of(tracers)
    south = shifted(high, "lat")
    north = shifted_back(low, "lat")
    west = shifted(cols, LON)
    east = shifted_back(cols, LON)
    fourier = lax.dot_general(
        spectral, legendre, (((3,), (1,)), ((2,), (0,))), preferred_element_type=jnp.float32
    )
    fourier = fourier.astype(jnp.bfloat16)
    banded = lax.all_to_all(fourier, "lat", split_axis=3, concat_axis=0, tiled=True)
    banded = whole_of(banded, LON, 2)
    waves = banded.shape[0]
    levels = banded.shape[2]
    lat_rows = banded.shape[3]
    tile = tracers.shape[3]
    parted = banded.reshape(waves, 3, 2, levels, lat_rows)
    stacked = jnp.concatenate([parted[:, :, 0], parted[:, :, 1]], axis=0)
    base_col = lax.axis_index(LON) * tile
    columns = base_col + jnp.arange(tile)
    width_low = 16
    count_high = tile // width_low
    high_cols = base_col + width_low * jnp.arange(count_high)
    low_cols = jnp.arange(width_low)
    cos_high, sin_high = part_angles(high_cols, wave_ids, points)
    cos_low, sin_low = part_angles(low_cols, wave_ids, points)
    cos_full = (
        cos_high[:, :, None, :] * cos_low[:, None, :, :]
        - sin_high[:, :, None, :] * sin_low[:, None, :, :]
    )
    sin_full = (
        sin_high[:, :, None, :] * cos_low[:, None, :, :]
        + cos_high[:, :, None, :] * sin_low[:, None, :, :]
    )
    cosine = cos_full.reshape(lat_rows, tile, waves).astype(jnp.bfloat16)
    sine = sin_full.reshape(lat_rows, tile, waves).astype(jnp.bfloat16)
    table = jnp.concatenate([cosine, -sine], axis=2)
    grid = jnp.einsum("mflj,jim->flji", stacked, table, preferred_element_type=jnp.float32)
    grid = grid / jnp.sqrt(jnp.float32(waves))
    winds = grid.astype(jnp.bfloat16).reshape(3, 8, 8, 16, 256)
    winds = jnp.transpose(winds, (1, 3, 0, 2, 4)).reshape(8, 384, 256)
    mask = (columns[None, :] < points[:, None]).astype(jnp.float32)
    fresh, active = chemistry(
        tracers, winds, north, south, east, west, mask, react_base, react_temp, active_ids
    )
    active = lax.all_to_all(active, LON, split_axis=0, concat_axis=0, tiled=True)
    active = jnp.transpose(active, (1, 2, 3, 0, 4)).reshape(4, 8, 16, 2048).astype(jnp.float32)
    return (fresh, active)


def solution(mesh):
    finer = Mesh(mesh.devices.reshape(mesh.shape["lat"], 4, 2), ("lat", "lon_0", "lon_1"))
    in_specs = (
        P(None, LON, "lat", None),
        P("lat", None, None),
        P(),
        P("lat"),
        P(None, None, "lat", LON),
        P(),
        P(),
        P(),
    )
    out_specs = (P(None, None, "lat", LON), P(None, LON, "lat", None))
    return jax.shard_map(body, mesh=finer, in_specs=in_specs, out_specs=out_specs, check_vma=False)
```

```python
import functools

import jax
import jax.numpy as jnp
from jax import lax
from jax.experimental import pallas as pl
from jax.experimental.pallas import tpu as pltpu
from jax.sharding import PartitionSpec as P

LON = "lon"


SRC = 16
DST = 8
MESH = pl.DeviceIdType.MESH
COS = (0.9999999888947231, -19.739204440276147, 64.93911426452443, -85.45007790017918,
       60.167101643628186, -25.965527386763885, 6.525643976222309)
SIN = (6.283185302441191, -41.34170037999709, 81.60513001863838, -76.70298898514991,
       42.02570052333535, -14.898960232258009, 3.2368479099117575)


def waves_at(product, count, inverse):
    turns = jnp.round(product * inverse)
    t = (product - turns * count) * inverse
    s = t * t
    c = COS[-1]
    for k in COS[-2::-1]:
        c = c * s + k
    d = SIN[-1]
    for k in SIN[-2::-1]:
        d = d * s + k
    return c, d * t


def spectral_kernel(
    four_ref, rowid_ref, laneid_ref, pts_ref,
    out_ref,
    tall, send_a, got_a, table, phase, coef, line, turned, send_b,
    sent_a, came_a, sent_b, came_b, own,
):
    g, h = lax.axis_index("lat"), lax.axis_index("lon")
    barrier = pltpu.get_barrier_semaphore()
    for d in range(1, SRC):
        pl.semaphore_signal(barrier, inc=1, device_id=(lax.rem(g + d, SRC), h), device_id_type=MESH)
    for d in range(1, DST):
        pl.semaphore_signal(barrier, inc=1, device_id=(g, lax.rem(h + d, DST)), device_id_type=MESH)

    for k in range(2):
        tall[k] = four_ref[:, :, 128 * k : 128 * k + 128].reshape(1920, 128).astype(jnp.float32)
    blank = jnp.zeros((8, 128), jnp.float32)

    def turn(r, carry):
        for k in range(2):
            parts = [tall[k, pl.ds(16 * f + r, 40, stride=48), :] for f in range(3)]
            block = jnp.concatenate(parts + [blank], axis=0).T.astype(jnp.bfloat16)
            for b in range(8):
                send_a[8 * k + b, r] = block[16 * b : 16 * b + 16]
        return carry

    lax.fori_loop(0, 16, turn, 0)
    pl.semaphore_wait(barrier, SRC + DST - 2)

    def copy_a(d):
        to = lax.rem(g + d, SRC)
        return pltpu.make_async_remote_copy(
            src_ref=send_a.at[to], dst_ref=got_a.at[g], send_sem=sent_a.at[d], recv_sem=came_a.at[d],
            device_id=(to, h), device_id_type=MESH,
        )

    for d in range(1, SRC):
        copy_a(d).start()
    mine = pltpu.make_async_copy(send_a.at[g], got_a.at[g], own.at[0])
    mine.start()

    shape = (128, 128)

    def tables(j, carry):
        count = jnp.full((1, 1), pts_ref[j], jnp.int32).astype(jnp.float32)
        inverse = 1.0 / count
        far = lax.broadcasted_iota(jnp.int32, (8, 128), 0).astype(jnp.float32) * 256.0
        lane = lax.broadcasted_iota(jnp.int32, shape, 1).astype(jnp.float32)
        for p in range(6):
            ids = laneid_ref[:, pl.ds(128 * p, 128)]
            c, s = waves_at(ids * far, count, inverse)
            phase[j, 0, p] = c
            phase[j, 1, p] = s
        for p in range(6):
            ids = rowid_ref[pl.ds(128 * p, 128), :]
            c, s = waves_at(ids * lane, count, inverse)
            c1, s1 = waves_at(ids * 128.0, count, inverse)
            table[j, pl.ds(128 * p, 128), pl.ds(0, 128)] = c.astype(jnp.bfloat16)
            table[j, pl.ds(768 + 128 * p, 128), pl.ds(0, 128)] = (-s).astype(jnp.bfloat16)
            table[j, pl.ds(128 * p, 128), pl.ds(128, 128)] = (c * c1 - s * s1).astype(jnp.bfloat16)
            table[j, pl.ds(768 + 128 * p, 128), pl.ds(128, 128)] = (-(s * c1 + c * s1)).astype(jnp.bfloat16)
        return carry

    lax.fori_loop(0, 16, tables, 0)

    mine.wait()
    for d in range(1, SRC):
        copy_a(d).wait_recv()

    def widen(q, carry):
        coef[pl.ds(256 * q, 256), :] = got_a[q].reshape(256, 128).astype(jnp.float32)
        return carry

    lax.fori_loop(0, SRC, widen, 0)

    def turn_of(j):
        lane = lax.broadcasted_iota(jnp.int32, (16, 128), 1)
        for p in range(6):
            held = []
            for q in range(3):
                s = 3 * p + q
                if s < SRC:
                    held.append(coef[pl.ds(256 * s + j, 16, stride=16), :])
                else:
                    held.append(None)
            for f in range(3):
                value = jnp.zeros((16, 128), jnp.float32)
                for q in range(3):
                    if held[q] is None:
                        continue
                    moved = held[q] if q == f else pltpu.roll(held[q], (40 * (q - f)) % 128, 1)
                    value = jnp.where((lane >= 40 * q) & (lane < 40 * q + 40), moved, value)
                re, im = value[:8], value[8:]
                line[f, 0, p] = re
                line[f, 1, p] = im
        for p in range(6):
            for a in range(0, DST, 2):
                parts = []
                for b in range(6):
                    row, f = a + b // 3, b % 3
                    c = phase[j, 0, p, row : row + 1, :]
                    s = phase[j, 1, p, row : row + 1, :]
                    re, im = line[f, 0, p], line[f, 1, p]
                    parts.append((re * c - im * s, re * s + im * c))
                for b in range(0, 6, 2):
                    at = 24 * a + 8 * b
                    for k in range(2):
                        pair = jnp.concatenate([parts[b][k], parts[b + 1][k]], axis=0)
                        turned[at : at + 16, 768 * k + 128 * p : 768 * k + 128 * p + 128] = pair.astype(jnp.bfloat16)
        out = jnp.dot(turned[...], table[j], preferred_element_type=jnp.float32)
        return out * (640.0 ** -0.5)

    def copy_b(d, c):
        to = lax.rem(h + d, DST)
        return pltpu.make_async_remote_copy(
            src_ref=send_b.at[c, to], dst_ref=out_ref.at[h, pl.ds(96 * c, 96), :],
            send_sem=sent_b.at[c, d], recv_sem=came_b.at[c, d], device_id=(g, to), device_id_type=MESH,
        )

    def copy_own(c):
        return pltpu.make_async_copy(send_b.at[c, h], out_ref.at[h, pl.ds(96 * c, 96), :], own.at[1 + c])

    def quad(c, carry):
        for jj in range(2):
            one = turn_of(4 * c + 2 * jj)
            two = turn_of(4 * c + 2 * jj + 1)
            for a in range(DST):
                both = jnp.concatenate([one[24 * a : 24 * a + 24], two[24 * a : 24 * a + 24]], axis=0)
                send_b[c, a, pl.ds(48 * jj, 48), :] = both.astype(jnp.bfloat16)
        for d in range(1, DST):
            copy_b(d, c).start()
        copy_own(c).start()
        return carry

    lax.fori_loop(0, 4, quad, 0)
    for d in range(1, SRC):
        copy_a(d).wait_send()

    def finish(c, carry):
        copy_own(c).wait()
        for d in range(1, DST):
            copy_b(d, c).wait()
        return carry

    lax.fori_loop(0, 4, finish, 0)


def winds_of(fourier, wave_ids, points):
    ids = jnp.zeros((6, 3, 40), jnp.float32).reshape(18, 40).at[:16].set(wave_ids.reshape(16, 40).astype(jnp.float32))
    ids = jnp.pad(ids.reshape(6, 120), ((0, 0), (0, 8))).reshape(768)
    rowid = jnp.broadcast_to(ids[:, None], (768, 128))
    laneid = jnp.broadcast_to(ids[None, :], (8, 768))
    vmem = pl.BlockSpec(memory_space=pltpu.VMEM)
    return pl.pallas_call(
        spectral_kernel,
        in_specs=[vmem, vmem, vmem, pl.BlockSpec(memory_space=pltpu.SMEM)],
        out_specs=pl.BlockSpec(memory_space=pl.ANY),
        out_shape=jax.ShapeDtypeStruct((8, 384, 256), jnp.bfloat16),
        scratch_shapes=[
            pltpu.VMEM((2, 1920, 128), jnp.float32),
            pltpu.VMEM((16, 16, 16, 128), jnp.bfloat16),
            pltpu.VMEM((16, 16, 16, 128), jnp.bfloat16),
            pltpu.VMEM((16, 1536, 256), jnp.bfloat16),
            pltpu.VMEM((16, 2, 6, 8, 128), jnp.float32),
            pltpu.VMEM((4096, 128), jnp.float32),
            pltpu.VMEM((3, 2, 6, 8, 128), jnp.float32),
            pltpu.VMEM((192, 1536), jnp.bfloat16),
            pltpu.VMEM((4, 8, 96, 256), jnp.bfloat16),
            pltpu.SemaphoreType.DMA((16,)),
            pltpu.SemaphoreType.DMA((16,)),
            pltpu.SemaphoreType.DMA((4, 8)),
            pltpu.SemaphoreType.DMA((4, 8)),
            pltpu.SemaphoreType.DMA((5,)),
        ],
        compiler_params=pltpu.CompilerParams(
            collective_id=0, has_side_effects=True, vmem_limit_bytes=60 * 1024 * 1024
        ),
        name="winds",
    )(fourier, rowid, laneid, points)


def rows_of(ref, start, size, stride):
    return jnp.concatenate([ref[k, pl.ds(start, size, stride=stride), :] for k in range(2)], axis=1)


def edge_kernel(tr_ref, low_ref, high_ref, col_ref, wide, acc):
    h = pl.program_id(0)
    lane = lax.broadcasted_iota(jnp.int32, (256, 128), 1)

    @pl.when(h == 0)
    def _():
        acc[...] = jnp.zeros_like(acc)

    def level(l, carry):
        x = tr_ref[:, l].reshape(256, 256).astype(jnp.float32)
        for k in range(2):
            wide[k] = x[:, 128 * k : 128 * k + 128]
        low_ref[l] = rows_of(wide, 0, 16, 16).astype(jnp.bfloat16)
        high_ref[l] = rows_of(wide, 15, 16, 16).astype(jnp.bfloat16)
        at = h * 8 + l
        first = pltpu.roll(x[:, :128], at, 1)
        last = pltpu.roll(x[:, 128:], lax.rem(at + 65, 128), 1)
        acc[...] = jnp.where(lane == at, first, jnp.where(lane == at + 64, last, acc[...]))
        return carry

    lax.fori_loop(0, 8, level, 0)

    @pl.when(h == pl.num_programs(0) - 1)
    def _():
        col_ref[...] = acc[...].astype(jnp.bfloat16)


def edges_of(tracers):
    return pl.pallas_call(
        edge_kernel,
        grid=(8,),
        in_specs=[pl.BlockSpec((16, 8, 16, 256), lambda h: (0, h, 0, 0))],
        out_specs=[
            pl.BlockSpec((8, 16, 256), lambda h: (h, 0, 0)),
            pl.BlockSpec((8, 16, 256), lambda h: (h, 0, 0)),
            pl.BlockSpec((256, 128), lambda h: (0, 0)),
        ],
        out_shape=[
            jax.ShapeDtypeStruct((64, 16, 256), jnp.bfloat16),
            jax.ShapeDtypeStruct((64, 16, 256), jnp.bfloat16),
            jax.ShapeDtypeStruct((256, 128), jnp.bfloat16),
        ],
        scratch_shapes=[pltpu.VMEM((2, 256, 128), jnp.float32), pltpu.VMEM((256, 128), jnp.float32)],
        name="edges",
    )(tracers)


def chem_kernel(
    ids_ref, tr_ref, wind_ref, north_ref, south_ref, east_ref, west_ref, mask_ref, base_ref, temp_ref,
    out_ref, act_ref, wide, east, west, mix, moved, moved_b,
):
    h = pl.program_id(0)

    @pl.when(h == 0)
    def _():
        east[...] = east_ref[...].astype(jnp.float32)
        west[...] = west_ref[...].astype(jnp.float32)
        row = lax.broadcasted_iota(jnp.int32, (256, 16), 0)
        col = lax.broadcasted_iota(jnp.int32, (256, 16), 1)
        spread = jnp.where(row // 16 == col, 1.0, 0.0).astype(jnp.bfloat16)
        row = lax.broadcasted_iota(jnp.int32, (256, 256), 0)
        col = lax.broadcasted_iota(jnp.int32, (256, 256), 1)
        same = row % 16 == col % 16
        for k, ref in enumerate((base_ref, temp_ref)):
            rows = jnp.dot(spread, ref[...].astype(jnp.bfloat16), preferred_element_type=jnp.float32)
            full = lax.dot_general(
                rows.astype(jnp.bfloat16), spread, (((1,), (1,)), ((), ())), preferred_element_type=jnp.float32
            )
            mix[pl.ds(256 * k, 256), :] = jnp.where(same, full, 0.0).astype(jnp.bfloat16)

    for k in range(2):
        wide[k] = wind_ref[0, :, 128 * k : 128 * k + 128].astype(jnp.float32)
    lane = lax.broadcasted_iota(jnp.int32, (16, 128), 1)
    row = lax.broadcasted_iota(jnp.int32, (16, 256), 0)
    lane_low, lane_high = lane == 0, lane == 127
    row_low, row_high = row == 0, row == 15
    mask = mask_ref[...]

    def level(l, carry):
        at = h * 8 + l
        u = 0.1 * rows_of(wide, l, 16, 24)
        v = 0.1 * rows_of(wide, 8 + l, 16, 24)
        temper = rows_of(wide, 16 + l, 16, 24)
        east_w, west_w = 0.05 - u, 0.05 + u
        north_w, south_w = 0.05 - v, 0.05 + v
        north = north_ref[l].astype(jnp.float32)
        south = south_ref[l].astype(jnp.float32)
        for t in range(16):
            x = tr_ref[t, l].astype(jnp.float32)
            xl, xr = x[:, :128], x[:, 128:]
            he = pltpu.roll(east[pl.ds(16 * t, 16), :], 127 - at, 1)
            hw = pltpu.roll(west[pl.ds(16 * t, 16), :], 64 - at, 1)
            el, er = pltpu.roll(xl, 127, 1), pltpu.roll(xr, 127, 1)
            wl, wr = pltpu.roll(xl, 1, 1), pltpu.roll(xr, 1, 1)
            xe = jnp.concatenate([jnp.where(lane_high, er, el), jnp.where(lane_high, he, er)], axis=1)
            xw = jnp.concatenate([jnp.where(lane_low, hw, wl), jnp.where(lane_low, wl, wr)], axis=1)
            xn = jnp.where(row_high, north[t : t + 1, :], pltpu.roll(x, 15, 0))
            xs = jnp.where(row_low, south[t : t + 1, :], pltpu.roll(x, 1, 0))
            q = 0.8 * x + east_w * xe + west_w * xw + north_w * xn + south_w * xs
            moved[t] = q
            moved_b[pl.ds(16 * t, 16), :] = q.astype(jnp.bfloat16)
        y = jnp.dot(mix[...], moved_b[...], preferred_element_type=jnp.float32)
        for t in range(16):
            q = (moved[t] + y[16 * t : 16 * t + 16] + temper * y[256 + 16 * t : 272 + 16 * t]) * mask
            moved[t] = q
            out_ref[t, l] = q.astype(jnp.bfloat16)
        for a in range(4):
            act_ref[0, a, l] = moved[ids_ref[a]].astype(jnp.bfloat16)
        return carry

    lax.fori_loop(0, 8, level, 0)


def chemistry(tracers, winds, north, south, east, west, mask, base, temp, ids):
    whole = lambda h, i: (0, 0)
    return pl.pallas_call(
        chem_kernel,
        grid_spec=pltpu.PrefetchScalarGridSpec(
            num_scalar_prefetch=1,
            grid=(8,),
            in_specs=[
                pl.BlockSpec((16, 8, 16, 256), lambda h, i: (0, h, 0, 0)),
                pl.BlockSpec((1, 384, 256), lambda h, i: (h, 0, 0)),
                pl.BlockSpec((8, 16, 256), lambda h, i: (h, 0, 0)),
                pl.BlockSpec((8, 16, 256), lambda h, i: (h, 0, 0)),
                pl.BlockSpec((256, 128), whole),
                pl.BlockSpec((256, 128), whole),
                pl.BlockSpec((16, 256), whole),
                pl.BlockSpec((16, 16), whole),
                pl.BlockSpec((16, 16), whole),
            ],
            out_specs=[
                pl.BlockSpec((16, 8, 16, 256), lambda h, i: (0, h, 0, 0)),
                pl.BlockSpec((1, 4, 8, 16, 256), lambda h, i: (h, 0, 0, 0, 0)),
            ],
            scratch_shapes=[
                pltpu.VMEM((2, 384, 128), jnp.float32),
                pltpu.VMEM((256, 128), jnp.float32),
                pltpu.VMEM((256, 128), jnp.float32),
                pltpu.VMEM((512, 256), jnp.bfloat16),
                pltpu.VMEM((16, 16, 256), jnp.float32),
                pltpu.VMEM((256, 256), jnp.bfloat16),
            ],
        ),
        out_shape=[
            jax.ShapeDtypeStruct((16, 64, 16, 256), jnp.bfloat16),
            jax.ShapeDtypeStruct((8, 4, 8, 16, 256), jnp.bfloat16),
        ],
        name="chemistry",
    )(ids, tracers, winds, north, south, east, west, mask, base, temp)


def shifted(value, axis):
    size = lax.axis_size(axis)
    up = [(i, (i + 1) % size) for i in range(size - 1)]
    return lax.ppermute(value, axis, up)


def shifted_back(value, axis):
    size = lax.axis_size(axis)
    up = [((i + 1) % size, i) for i in range(size - 1)]
    return lax.ppermute(value, axis, up)


def body(spectral, legendre, wave_ids, points, tracers, react_base, react_temp, active_ids):
    low, high, cols = edges_of(tracers)
    south = shifted(high, "lat")
    north = shifted_back(low, "lat")
    west = shifted(cols, LON)
    east = shifted_back(cols, LON)
    fourier = lax.dot_general(
        spectral, legendre, (((3,), (1,)), ((2,), (0,))), preferred_element_type=jnp.float32
    )
    fourier = fourier.astype(jnp.bfloat16)
    winds = winds_of(fourier.reshape(40, 48, 256), wave_ids, points)
    columns = lax.axis_index("lon") * 256 + jnp.arange(256)
    mask = (columns[None, :] < points[:, None]).astype(jnp.float32)
    fresh, active = chemistry(
        tracers, winds, north, south, east, west, mask, react_base, react_temp, active_ids
    )
    active = lax.all_to_all(active, LON, split_axis=0, concat_axis=0, tiled=True)
    active = jnp.transpose(active, (1, 2, 3, 0, 4)).reshape(4, 8, 16, 2048).astype(jnp.float32)
    return (fresh, active)


def solution(mesh):
    in_specs = (
        P(None, LON, "lat", None),
        P("lat", None, None),
        P(),
        P("lat"),
        P(None, None, "lat", LON),
        P(),
        P(),
        P(),
    )
    out_specs = (P(None, None, "lat", LON), P(None, LON, "lat", None))
    return jax.shard_map(body, mesh=mesh, in_specs=in_specs, out_specs=out_specs, check_vma=False)
```

```python
import functools

import jax
import jax.numpy as jnp
from jax import lax
from jax.experimental import pallas as pl
from jax.experimental.pallas import tpu as pltpu
from jax.sharding import PartitionSpec as P

LON = "lon"


SRC = 16
DST = 8
MESH = pl.DeviceIdType.MESH
COS = (0.9999992006931535, -19.7389777615569, 64.92855937725766, -85.27036091136767,
       58.78399626476764, -21.059548245283555)
SIN = (6.283184911477688, -41.3415879428884, 81.59989458670537, -76.61384581975258,
       41.339653019987985, -12.465497972860707)


def waves_at(product, count, inverse):
    turns = jnp.round(product * inverse)
    t = (product - turns * count) * inverse
    s = t * t
    c = COS[-1]
    for k in COS[-2::-1]:
        c = c * s + k
    d = SIN[-1]
    for k in SIN[-2::-1]:
        d = d * s + k
    return c, d * t


def spectral_kernel(
    spec_ref, leg_ref, tr_ref, rowid_ref, laneid_ref, pts_ref,
    out_ref, north_ref, south_ref, east_ref, west_ref,
    spec, spread, leg, band, wide, cols, low, high, edge, empty, blank_cols,
    tall, send_a, got_a, table, phase, coef, line, turned, send_b,
    sent_a, came_a, sent_b, came_b, own, sent_h, came_h, taken, leg_in, band_in,
):
    g, h = lax.axis_index("lat"), lax.axis_index("lon")
    barrier = pltpu.get_barrier_semaphore()
    for d in range(1, SRC):
        pl.semaphore_signal(barrier, inc=1, device_id=(lax.rem(g + d, SRC), h), device_id_type=MESH)
    for d in range(1, DST):
        pl.semaphore_signal(barrier, inc=1, device_id=(g, lax.rem(h + d, DST)), device_id_type=MESH)

    def leg_copy(i):
        slot = lax.rem(i, 3)
        return pltpu.make_async_copy(leg_ref.at[pl.ds(5 * i, 5)], leg.at[slot], leg_in.at[slot])

    def band_copy(i):
        slot = lax.rem(i, 2)
        return pltpu.make_async_copy(tr_ref.at[:, pl.ds(8 * i, 8)], band.at[slot], band_in.at[slot])

    spec_copy = pltpu.make_async_copy(spec_ref, spec, taken)
    spec_copy.start()
    leg_copy(0).start()
    band_copy(0).start()
    leg_copy(1).start()
    band_copy(1).start()
    empty[...] = jnp.zeros_like(empty)
    blank_cols[...] = jnp.zeros_like(blank_cols)
    cols[...] = jnp.zeros_like(cols)
    spec_copy.wait()

    def loosen(r, carry):
        for k in range(10):
            spread[k, pl.ds(40 * r, 40), :] = spec[r, :, 128 * k : 128 * k + 128].astype(jnp.float32)
        return carry

    lax.fori_loop(0, 48, loosen, 0)
    lane = lax.broadcasted_iota(jnp.int32, (256, 128), 1)

    def step(i, carry):
        slot = lax.rem(i, 3)

        @pl.when(i < 6)
        def _():
            leg_copy(i + 2).start()

        leg_copy(i).wait()
        for w in range(5):
            m = 5 * i + w
            rows = [spread[k, pl.ds(m, 48, stride=40), :].astype(jnp.bfloat16) for k in range(10)]
            value = jnp.dot(jnp.concatenate(rows, axis=1), leg[slot, w], preferred_element_type=jnp.float32)
            for k in range(2):
                tall[k, pl.ds(48 * m, 48), :] = value[:, 128 * k : 128 * k + 128]
        side = lax.rem(i, 2)
        band_copy(i).wait()

        def level(l, carry):
            at = 8 * i + l
            x = band[side, :, l].reshape(256, 256).astype(jnp.float32)
            for k in range(2):
                wide[k] = x[:, 128 * k : 128 * k + 128]
            low[at] = rows_of(wide, 0, 16, 16).astype(jnp.bfloat16)
            high[at] = rows_of(wide, 15, 16, 16).astype(jnp.bfloat16)
            first = pltpu.roll(x[:, :128], at, 1)
            last = pltpu.roll(x[:, 128:], lax.rem(at + 65, 128), 1)
            cols[...] = jnp.where(lane == at, first, jnp.where(lane == at + 64, last, cols[...]))
            return carry

        lax.fori_loop(0, 8, level, 0)

        @pl.when(i < 6)
        def _():
            band_copy(i + 2).start()

        return carry

    lax.fori_loop(0, 8, step, 0)
    edge[...] = cols[...].astype(jnp.bfloat16)
    blank = jnp.zeros((8, 128), jnp.float32)

    def turn(r, carry):
        for k in range(2):
            parts = [tall[k, pl.ds(16 * f + r, 40, stride=48), :] for f in range(3)]
            block = jnp.concatenate(parts + [blank], axis=0).T.astype(jnp.bfloat16)
            for b in range(8):
                send_a[8 * k + b, r] = block[16 * b : 16 * b + 16]
        return carry

    lax.fori_loop(0, 16, turn, 0)
    pl.semaphore_wait(barrier, SRC + DST - 2)

    def copy_a(d):
        to = lax.rem(g + d, SRC)
        return pltpu.make_async_remote_copy(
            src_ref=send_a.at[to], dst_ref=got_a.at[g], send_sem=sent_a.at[d], recv_sem=came_a.at[d],
            device_id=(to, h), device_id_type=MESH,
        )

    for d in range(1, SRC):
        copy_a(d).start()
    mine = pltpu.make_async_copy(send_a.at[g], got_a.at[g], own.at[0])
    mine.start()

    def halo(k, src, dst, lat, lon):
        return pltpu.make_async_remote_copy(
            src_ref=src, dst_ref=dst, send_sem=sent_h.at[k], recv_sem=came_h.at[k],
            device_id=(lat, lon), device_id_type=MESH,
        )

    to_north = halo(0, high, south_ref, lax.rem(g + 1, SRC), h)
    to_south = halo(1, low, north_ref, lax.rem(g + SRC - 1, SRC), h)
    to_east = halo(2, edge, west_ref, g, lax.rem(h + 1, DST))
    to_west = halo(3, edge, east_ref, g, lax.rem(h + DST - 1, DST))
    none_south = pltpu.make_async_copy(empty, south_ref, own.at[5])
    none_north = pltpu.make_async_copy(empty, north_ref, own.at[6])
    none_west = pltpu.make_async_copy(blank_cols, west_ref, own.at[7])
    none_east = pltpu.make_async_copy(blank_cols, east_ref, own.at[8])
    sides = (
        (g < SRC - 1, to_north, g > 0, none_south),
        (g > 0, to_south, g < SRC - 1, none_north),
        (h < DST - 1, to_east, h > 0, none_west),
        (h > 0, to_west, h < DST - 1, none_east),
    )
    for sends, copy, gets, fill in sides:
        pl.when(sends)(copy.start)
        pl.when(jnp.logical_not(gets))(fill.start)

    shape = (128, 128)

    def tables(j, carry):
        count = jnp.full((1, 1), pts_ref[j], jnp.int32).astype(jnp.float32)
        inverse = 1.0 / count
        far = lax.broadcasted_iota(jnp.int32, (8, 128), 0).astype(jnp.float32) * 256.0
        lane = lax.broadcasted_iota(jnp.int32, shape, 1).astype(jnp.float32)
        for p in range(6):
            ids = laneid_ref[:, pl.ds(128 * p, 128)]
            c, s = waves_at(ids * far, count, inverse)
            phase[j, 0, p] = c
            phase[j, 1, p] = s
        for p in range(6):
            ids = rowid_ref[pl.ds(128 * p, 128), :]
            c, s = waves_at(ids * lane, count, inverse)
            c1 = jnp.broadcast_to(c[:, 64:65], shape)
            s1 = jnp.broadcast_to(s[:, 64:65], shape)
            c1, s1 = c1 * c1 - s1 * s1, 2.0 * c1 * s1
            table[j, pl.ds(128 * p, 128), pl.ds(0, 128)] = c.astype(jnp.bfloat16)
            table[j, pl.ds(768 + 128 * p, 128), pl.ds(0, 128)] = (-s).astype(jnp.bfloat16)
            table[j, pl.ds(128 * p, 128), pl.ds(128, 128)] = (c * c1 - s * s1).astype(jnp.bfloat16)
            table[j, pl.ds(768 + 128 * p, 128), pl.ds(128, 128)] = (-(s * c1 + c * s1)).astype(jnp.bfloat16)
        return carry

    lax.fori_loop(0, 16, tables, 0)

    mine.wait()
    for d in range(1, SRC):
        copy_a(d).wait_recv()

    def widen(q, carry):
        coef[pl.ds(256 * q, 256), :] = got_a[q].reshape(256, 128).astype(jnp.float32)
        return carry

    lax.fori_loop(0, SRC, widen, 0)

    def turn_of(j):
        lane = lax.broadcasted_iota(jnp.int32, (16, 128), 1)
        for p in range(6):
            held = []
            for q in range(3):
                s = 3 * p + q
                if s < SRC:
                    held.append(coef[pl.ds(256 * s + j, 16, stride=16), :])
                else:
                    held.append(None)
            for f in range(3):
                value = jnp.zeros((16, 128), jnp.float32)
                for q in range(3):
                    if held[q] is None:
                        continue
                    moved = held[q] if q == f else pltpu.roll(held[q], (40 * (q - f)) % 128, 1)
                    value = jnp.where((lane >= 40 * q) & (lane < 40 * q + 40), moved, value)
                re, im = value[:8], value[8:]
                line[f, 0, p] = re
                line[f, 1, p] = im
        for p in range(6):
            for a in range(0, DST, 2):
                parts = []
                for b in range(6):
                    row, f = a + b // 3, b % 3
                    c = phase[j, 0, p, row : row + 1, :]
                    s = phase[j, 1, p, row : row + 1, :]
                    re, im = line[f, 0, p], line[f, 1, p]
                    parts.append((re * c - im * s, re * s + im * c))
                for b in range(0, 6, 2):
                    at = 24 * a + 8 * b
                    for k in range(2):
                        pair = jnp.concatenate([parts[b][k], parts[b + 1][k]], axis=0)
                        turned[at : at + 16, 768 * k + 128 * p : 768 * k + 128 * p + 128] = pair.astype(jnp.bfloat16)
        out = jnp.dot(turned[...], table[j], preferred_element_type=jnp.float32)
        return out * (640.0 ** -0.5)

    def copy_b(d, c):
        to = lax.rem(h + d, DST)
        return pltpu.make_async_remote_copy(
            src_ref=send_b.at[c, to], dst_ref=out_ref.at[h, pl.ds(96 * c, 96), :],
            send_sem=sent_b.at[c, d], recv_sem=came_b.at[c, d], device_id=(g, to), device_id_type=MESH,
        )

    def copy_own(c):
        return pltpu.make_async_copy(send_b.at[c, h], out_ref.at[h, pl.ds(96 * c, 96), :], own.at[1 + c])

    def quad(c, carry):
        for jj in range(2):
            one = turn_of(4 * c + 2 * jj)
            two = turn_of(4 * c + 2 * jj + 1)
            for a in range(DST):
                both = jnp.concatenate([one[24 * a : 24 * a + 24], two[24 * a : 24 * a + 24]], axis=0)
                send_b[c, a, pl.ds(48 * jj, 48), :] = both.astype(jnp.bfloat16)
        for d in range(1, DST):
            copy_b(d, c).start()
        copy_own(c).start()
        return carry

    lax.fori_loop(0, 4, quad, 0)
    for d in range(1, SRC):
        copy_a(d).wait_send()

    def finish(c, carry):
        copy_own(c).wait()
        for d in range(1, DST):
            copy_b(d, c).wait()
        return carry

    lax.fori_loop(0, 4, finish, 0)
    for sends, copy, gets, fill in sides:
        pl.when(sends)(copy.wait_send)
        pl.when(gets)(copy.wait_recv)
        pl.when(jnp.logical_not(gets))(fill.wait)


def winds_of(spectral, legendre, tracers, wave_ids, points):
    ids = jnp.zeros((6, 3, 40), jnp.float32).reshape(18, 40).at[:16].set(wave_ids.reshape(16, 40).astype(jnp.float32))
    ids = jnp.pad(ids.reshape(6, 120), ((0, 0), (0, 8))).reshape(768)
    rowid = jnp.broadcast_to(ids[:, None], (768, 128))
    laneid = jnp.broadcast_to(ids[None, :], (8, 768))
    vmem = pl.BlockSpec(memory_space=pltpu.VMEM)
    hbm = pl.BlockSpec(memory_space=pl.ANY)
    return pl.pallas_call(
        spectral_kernel,
        in_specs=[hbm, hbm, hbm, vmem, vmem, pl.BlockSpec(memory_space=pltpu.SMEM)],
        out_specs=[hbm] * 5,
        out_shape=[
            jax.ShapeDtypeStruct((8, 384, 256), jnp.bfloat16),
            jax.ShapeDtypeStruct((64, 16, 256), jnp.bfloat16),
            jax.ShapeDtypeStruct((64, 16, 256), jnp.bfloat16),
            jax.ShapeDtypeStruct((256, 128), jnp.bfloat16),
            jax.ShapeDtypeStruct((256, 128), jnp.bfloat16),
        ],
        scratch_shapes=[
            pltpu.VMEM((48, 40, 1280), jnp.bfloat16),
            pltpu.VMEM((10, 1920, 128), jnp.float32),
            pltpu.VMEM((3, 5, 1280, 256), jnp.bfloat16),
            pltpu.VMEM((2, 16, 8, 16, 256), jnp.bfloat16),
            pltpu.VMEM((2, 256, 128), jnp.float32),
            pltpu.VMEM((256, 128), jnp.float32),
            pltpu.VMEM((64, 16, 256), jnp.bfloat16),
            pltpu.VMEM((64, 16, 256), jnp.bfloat16),
            pltpu.VMEM((256, 128), jnp.bfloat16),
            pltpu.VMEM((64, 16, 256), jnp.bfloat16),
            pltpu.VMEM((256, 128), jnp.bfloat16),
            pltpu.VMEM((2, 1920, 128), jnp.float32),
            pltpu.VMEM((16, 16, 16, 128), jnp.bfloat16),
            pltpu.VMEM((16, 16, 16, 128), jnp.bfloat16),
            pltpu.VMEM((16, 1536, 256), jnp.bfloat16),
            pltpu.VMEM((16, 2, 6, 8, 128), jnp.float32),
            pltpu.VMEM((4096, 128), jnp.float32),
            pltpu.VMEM((3, 2, 6, 8, 128), jnp.float32),
            pltpu.VMEM((192, 1536), jnp.bfloat16),
            pltpu.VMEM((4, 8, 96, 256), jnp.bfloat16),
            pltpu.SemaphoreType.DMA((16,)),
            pltpu.SemaphoreType.DMA((16,)),
            pltpu.SemaphoreType.DMA((4, 8)),
            pltpu.SemaphoreType.DMA((4, 8)),
            pltpu.SemaphoreType.DMA((9,)),
            pltpu.SemaphoreType.DMA((4,)),
            pltpu.SemaphoreType.DMA((4,)),
            pltpu.SemaphoreType.DMA,
            pltpu.SemaphoreType.DMA((3,)),
            pltpu.SemaphoreType.DMA((2,)),
        ],
        compiler_params=pltpu.CompilerParams(
            collective_id=0, has_side_effects=True, vmem_limit_bytes=60 * 1024 * 1024
        ),
        name="winds",
    )(spectral, legendre, tracers, rowid, laneid, points)


def rows_of(ref, start, size, stride):
    return jnp.concatenate([ref[k, pl.ds(start, size, stride=stride), :] for k in range(2)], axis=1)


def chem_kernel(
    ids_ref, tr_ref, wind_ref, north_ref, south_ref, east_ref, west_ref, mask_ref, base_ref, temp_ref,
    out_ref, act_ref, wide, east, west, mix, moved, moved_b,
):
    h = pl.program_id(0)

    @pl.when(h == 0)
    def _():
        east[...] = east_ref[...].astype(jnp.float32)
        west[...] = west_ref[...].astype(jnp.float32)
        row = lax.broadcasted_iota(jnp.int32, (256, 16), 0)
        col = lax.broadcasted_iota(jnp.int32, (256, 16), 1)
        spread = jnp.where(row // 16 == col, 1.0, 0.0).astype(jnp.bfloat16)
        row = lax.broadcasted_iota(jnp.int32, (256, 256), 0)
        col = lax.broadcasted_iota(jnp.int32, (256, 256), 1)
        same = row % 16 == col % 16
        for k, ref in enumerate((base_ref, temp_ref)):
            rows = jnp.dot(spread, ref[...].astype(jnp.bfloat16), preferred_element_type=jnp.float32)
            full = lax.dot_general(
                rows.astype(jnp.bfloat16), spread, (((1,), (1,)), ((), ())), preferred_element_type=jnp.float32
            )
            mix[pl.ds(256 * k, 256), :] = jnp.where(same, full, 0.0).astype(jnp.bfloat16)

    for k in range(2):
        wide[k] = wind_ref[0, :, 128 * k : 128 * k + 128].astype(jnp.float32)
    lane = lax.broadcasted_iota(jnp.int32, (16, 128), 1)
    row = lax.broadcasted_iota(jnp.int32, (16, 256), 0)
    lane_low, lane_high = lane == 0, lane == 127
    row_low, row_high = row == 0, row == 15
    mask = mask_ref[...]

    def level(l, carry):
        at = h * 8 + l
        u = 0.1 * rows_of(wide, l, 16, 24)
        v = 0.1 * rows_of(wide, 8 + l, 16, 24)
        temper = rows_of(wide, 16 + l, 16, 24)
        east_w, west_w = 0.05 - u, 0.05 + u
        north_w, south_w = 0.05 - v, 0.05 + v
        north = north_ref[l].astype(jnp.float32)
        south = south_ref[l].astype(jnp.float32)
        for t in range(16):
            x = tr_ref[t, l].astype(jnp.float32)
            xl, xr = x[:, :128], x[:, 128:]
            he = pltpu.roll(east[pl.ds(16 * t, 16), :], 127 - at, 1)
            hw = pltpu.roll(west[pl.ds(16 * t, 16), :], 64 - at, 1)
            el, er = pltpu.roll(xl, 127, 1), pltpu.roll(xr, 127, 1)
            wl, wr = pltpu.roll(xl, 1, 1), pltpu.roll(xr, 1, 1)
            xe = jnp.concatenate([jnp.where(lane_high, er, el), jnp.where(lane_high, he, er)], axis=1)
            xw = jnp.concatenate([jnp.where(lane_low, hw, wl), jnp.where(lane_low, wl, wr)], axis=1)
            xn = jnp.where(row_high, north[t : t + 1, :], pltpu.roll(x, 15, 0))
            xs = jnp.where(row_low, south[t : t + 1, :], pltpu.roll(x, 1, 0))
            q = 0.8 * x + east_w * xe + west_w * xw + north_w * xn + south_w * xs
            moved[t] = q
            moved_b[pl.ds(16 * t, 16), :] = q.astype(jnp.bfloat16)
        y = jnp.dot(mix[...], moved_b[...], preferred_element_type=jnp.float32)
        for t in range(16):
            q = (moved[t] + y[16 * t : 16 * t + 16] + temper * y[256 + 16 * t : 272 + 16 * t]) * mask
            moved[t] = q
            out_ref[t, l] = q.astype(jnp.bfloat16)
        for a in range(4):
            act_ref[0, a, l] = moved[ids_ref[a]].astype(jnp.bfloat16)
        return carry

    lax.fori_loop(0, 8, level, 0)


def chemistry(tracers, winds, north, south, east, west, mask, base, temp, ids):
    whole = lambda h, i: (0, 0)
    return pl.pallas_call(
        chem_kernel,
        grid_spec=pltpu.PrefetchScalarGridSpec(
            num_scalar_prefetch=1,
            grid=(8,),
            in_specs=[
                pl.BlockSpec((16, 8, 16, 256), lambda h, i: (0, h, 0, 0)),
                pl.BlockSpec((1, 384, 256), lambda h, i: (h, 0, 0)),
                pl.BlockSpec((8, 16, 256), lambda h, i: (h, 0, 0)),
                pl.BlockSpec((8, 16, 256), lambda h, i: (h, 0, 0)),
                pl.BlockSpec((256, 128), whole),
                pl.BlockSpec((256, 128), whole),
                pl.BlockSpec((16, 256), whole),
                pl.BlockSpec((16, 16), whole),
                pl.BlockSpec((16, 16), whole),
            ],
            out_specs=[
                pl.BlockSpec((16, 8, 16, 256), lambda h, i: (0, h, 0, 0)),
                pl.BlockSpec((1, 4, 8, 16, 256), lambda h, i: (h, 0, 0, 0, 0)),
            ],
            scratch_shapes=[
                pltpu.VMEM((2, 384, 128), jnp.float32),
                pltpu.VMEM((256, 128), jnp.float32),
                pltpu.VMEM((256, 128), jnp.float32),
                pltpu.VMEM((512, 256), jnp.bfloat16),
                pltpu.VMEM((16, 16, 256), jnp.float32),
                pltpu.VMEM((256, 256), jnp.bfloat16),
            ],
        ),
        out_shape=[
            jax.ShapeDtypeStruct((16, 64, 16, 256), jnp.bfloat16),
            jax.ShapeDtypeStruct((8, 4, 8, 16, 256), jnp.bfloat16),
        ],
        name="chemistry",
    )(ids, tracers, winds, north, south, east, west, mask, base, temp)


def body(spectral, legendre, wave_ids, points, tracers, react_base, react_temp, active_ids):
    winds, north, south, east, west = winds_of(
        spectral.reshape(48, 40, 1280), legendre, tracers, wave_ids, points
    )
    columns = lax.axis_index("lon") * 256 + jnp.arange(256)
    mask = (columns[None, :] < points[:, None]).astype(jnp.float32)
    fresh, active = chemistry(
        tracers, winds, north, south, east, west, mask, react_base, react_temp, active_ids
    )
    active = lax.all_to_all(active, LON, split_axis=0, concat_axis=0, tiled=True)
    active = jnp.transpose(active, (1, 2, 3, 0, 4)).reshape(4, 8, 16, 2048).astype(jnp.float32)
    return (fresh, active)


def solution(mesh):
    in_specs = (
        P(None, LON, "lat", None),
        P("lat", None, None),
        P(),
        P("lat"),
        P(None, None, "lat", LON),
        P(),
        P(),
        P(),
    )
    out_specs = (P(None, None, "lat", LON), P(None, LON, "lat", None))
    return jax.shard_map(body, mesh=mesh, in_specs=in_specs, out_specs=out_specs, check_vma=False)
```

```python
import functools

import jax
import jax.numpy as jnp
from jax import lax
from jax.experimental import pallas as pl
from jax.experimental.pallas import tpu as pltpu
from jax.sharding import PartitionSpec as P

LON = "lon"


SRC = 16
UNROLL = 4
CHUNK = 8
DST = 8
MESH = pl.DeviceIdType.MESH
COS = (0.9999992006931535, -19.7389777615569, 64.92855937725766, -85.27036091136767,
       58.78399626476764, -21.059548245283555)
SIN = (6.283184911477688, -41.3415879428884, 81.59989458670537, -76.61384581975258,
       41.339653019987985, -12.465497972860707)


def waves_at(product, count, inverse):
    turns = jnp.round(product * inverse)
    t = (product - turns * count) * inverse
    s = t * t
    c = COS[-1]
    for k in COS[-2::-1]:
        c = c * s + k
    d = SIN[-1]
    for k in SIN[-2::-1]:
        d = d * s + k
    return c, d * t


def spectral_kernel(
    spec_ref, leg_ref, tr_ref, rowid_ref, laneid_ref, pts_ref,
    out_ref, north_ref, south_ref, east_ref, west_ref,
    spec, spread, leg, band, wide, cols, low, high, edge, empty, blank_cols,
    tall, send_a, got_a, table, phase, coef, line, turned, send_b,
    sent_a, came_a, sent_b, came_b, own, sent_h, came_h, taken, leg_in, band_in,
):
    g, h = lax.axis_index("lat"), lax.axis_index("lon")
    barrier = pltpu.get_barrier_semaphore()
    for d in range(1, SRC):
        pl.semaphore_signal(barrier, inc=1, device_id=(lax.rem(g + d, SRC), h), device_id_type=MESH)
    for d in range(1, DST):
        pl.semaphore_signal(barrier, inc=1, device_id=(g, lax.rem(h + d, DST)), device_id_type=MESH)

    def leg_copy(i):
        slot = lax.rem(i, 3)
        return pltpu.make_async_copy(leg_ref.at[pl.ds(5 * i, 5)], leg.at[slot], leg_in.at[slot])

    def band_copy(i):
        slot = lax.rem(i, 2)
        return pltpu.make_async_copy(tr_ref.at[:, pl.ds(8 * i, 8)], band.at[slot], band_in.at[slot])

    spec_copy = pltpu.make_async_copy(spec_ref, spec, taken)
    spec_copy.start()
    leg_copy(0).start()
    band_copy(0).start()
    leg_copy(1).start()
    band_copy(1).start()
    empty[...] = jnp.zeros_like(empty)
    blank_cols[...] = jnp.zeros_like(blank_cols)
    cols[...] = jnp.zeros_like(cols)
    spec_copy.wait()

    def loosen(r, carry):
        for k in range(10):
            spread[k, pl.ds(40 * r, 40), :] = spec[r, :, 128 * k : 128 * k + 128].astype(jnp.float32)
        return carry

    lax.fori_loop(0, 48, loosen, 0)
    lane = lax.broadcasted_iota(jnp.int32, (256, 128), 1)

    def step(i, carry):
        slot = lax.rem(i, 3)

        @pl.when(i < 6)
        def _():
            leg_copy(i + 2).start()

        leg_copy(i).wait()
        for w in range(5):
            m = 5 * i + w
            rows = [spread[k, pl.ds(m, 48, stride=40), :].astype(jnp.bfloat16) for k in range(10)]
            value = jnp.dot(jnp.concatenate(rows, axis=1), leg[slot, w], preferred_element_type=jnp.float32)
            for k in range(2):
                tall[k, pl.ds(48 * m, 48), :] = value[:, 128 * k : 128 * k + 128]
        side = lax.rem(i, 2)
        band_copy(i).wait()

        def level(l, carry):
            at = 8 * i + l
            x = band[side, :, l].reshape(256, 256).astype(jnp.float32)
            for k in range(2):
                wide[k] = x[:, 128 * k : 128 * k + 128]
            low[at] = rows_of(wide, 0, 16, 16).astype(jnp.bfloat16)
            high[at] = rows_of(wide, 15, 16, 16).astype(jnp.bfloat16)
            first = pltpu.roll(x[:, :128], at, 1)
            last = pltpu.roll(x[:, 128:], lax.rem(at + 65, 128), 1)
            cols[...] = jnp.where(lane == at, first, jnp.where(lane == at + 64, last, cols[...]))
            return carry

        lax.fori_loop(0, 8, level, 0)

        @pl.when(i < 6)
        def _():
            band_copy(i + 2).start()

        return carry

    lax.fori_loop(0, 8, step, 0)
    edge[...] = cols[...].astype(jnp.bfloat16)
    blank = jnp.zeros((8, 128), jnp.float32)

    def turn(r, carry):
        for k in range(2):
            parts = [tall[k, pl.ds(16 * f + r, 40, stride=48), :] for f in range(3)]
            block = jnp.concatenate(parts + [blank], axis=0).T.astype(jnp.bfloat16)
            for b in range(8):
                send_a[8 * k + b, r] = block[16 * b : 16 * b + 16]
        return carry

    lax.fori_loop(0, 16, turn, 0)
    pl.semaphore_wait(barrier, SRC + DST - 2)

    def copy_a(d):
        to = lax.rem(g + d, SRC)
        return pltpu.make_async_remote_copy(
            src_ref=send_a.at[to], dst_ref=got_a.at[g], send_sem=sent_a.at[d], recv_sem=came_a.at[d],
            device_id=(to, h), device_id_type=MESH,
        )

    for d in range(1, SRC):
        copy_a(d).start()
    mine = pltpu.make_async_copy(send_a.at[g], got_a.at[g], own.at[0])
    mine.start()

    def halo(k, src, dst, lat, lon):
        return pltpu.make_async_remote_copy(
            src_ref=src, dst_ref=dst, send_sem=sent_h.at[k], recv_sem=came_h.at[k],
            device_id=(lat, lon), device_id_type=MESH,
        )

    to_north = halo(0, high, south_ref, lax.rem(g + 1, SRC), h)
    to_south = halo(1, low, north_ref, lax.rem(g + SRC - 1, SRC), h)
    to_east = halo(2, edge, west_ref, g, lax.rem(h + 1, DST))
    to_west = halo(3, edge, east_ref, g, lax.rem(h + DST - 1, DST))
    none_south = pltpu.make_async_copy(empty, south_ref, own.at[5])
    none_north = pltpu.make_async_copy(empty, north_ref, own.at[6])
    none_west = pltpu.make_async_copy(blank_cols, west_ref, own.at[7])
    none_east = pltpu.make_async_copy(blank_cols, east_ref, own.at[8])
    sides = (
        (g < SRC - 1, to_north, g > 0, none_south),
        (g > 0, to_south, g < SRC - 1, none_north),
        (h < DST - 1, to_east, h > 0, none_west),
        (h > 0, to_west, h < DST - 1, none_east),
    )
    for sends, copy, gets, fill in sides:
        pl.when(sends)(copy.start)
        pl.when(jnp.logical_not(gets))(fill.start)

    shape = (128, 128)

    def tables(j, carry):
        count = jnp.full((1, 1), pts_ref[j], jnp.int32).astype(jnp.float32)
        inverse = 1.0 / count
        far = lax.broadcasted_iota(jnp.int32, (8, 128), 0).astype(jnp.float32) * 256.0
        lane = lax.broadcasted_iota(jnp.int32, shape, 1).astype(jnp.float32)
        for p in range(6):
            ids = laneid_ref[:, pl.ds(128 * p, 128)]
            c, s = waves_at(ids * far, count, inverse)
            phase[j, 0, p] = c
            phase[j, 1, p] = s
        for p in range(6):
            ids = rowid_ref[pl.ds(128 * p, 128), :]
            c, s = waves_at(ids * lane, count, inverse)
            c1 = jnp.broadcast_to(c[:, 64:65], shape)
            s1 = jnp.broadcast_to(s[:, 64:65], shape)
            c1, s1 = c1 * c1 - s1 * s1, 2.0 * c1 * s1
            table[j, pl.ds(128 * p, 128), pl.ds(0, 128)] = c.astype(jnp.bfloat16)
            table[j, pl.ds(768 + 128 * p, 128), pl.ds(0, 128)] = (-s).astype(jnp.bfloat16)
            table[j, pl.ds(128 * p, 128), pl.ds(128, 128)] = (c * c1 - s * s1).astype(jnp.bfloat16)
            table[j, pl.ds(768 + 128 * p, 128), pl.ds(128, 128)] = (-(s * c1 + c * s1)).astype(jnp.bfloat16)
        return carry

    lax.fori_loop(0, 16, tables, 0)

    mine.wait()
    for d in range(1, SRC):
        copy_a(d).wait_recv()

    def widen(q, carry):
        coef[pl.ds(256 * q, 256), :] = got_a[q].reshape(256, 128).astype(jnp.float32)
        return carry

    lax.fori_loop(0, SRC, widen, 0)

    def turn_of(j):
        lane = lax.broadcasted_iota(jnp.int32, (16, 128), 1)
        for p in range(6):
            held = []
            for q in range(3):
                s = 3 * p + q
                if s < SRC:
                    held.append(coef[pl.ds(256 * s + j, 16, stride=16), :])
                else:
                    held.append(None)
            for f in range(3):
                value = jnp.zeros((16, 128), jnp.float32)
                for q in range(3):
                    if held[q] is None:
                        continue
                    moved = held[q] if q == f else pltpu.roll(held[q], (40 * (q - f)) % 128, 1)
                    value = jnp.where((lane >= 40 * q) & (lane < 40 * q + 40), moved, value)
                re, im = value[:8], value[8:]
                line[f, 0, p] = re
                line[f, 1, p] = im
        for p in range(6):
            for a in range(0, DST, 2):
                parts = []
                for b in range(6):
                    row, f = a + b // 3, b % 3
                    c = phase[j, 0, p, row : row + 1, :]
                    s = phase[j, 1, p, row : row + 1, :]
                    re, im = line[f, 0, p], line[f, 1, p]
                    parts.append((re * c - im * s, re * s + im * c))
                for b in range(0, 6, 2):
                    at = 24 * a + 8 * b
                    for k in range(2):
                        pair = jnp.concatenate([parts[b][k], parts[b + 1][k]], axis=0)
                        turned[at : at + 16, 768 * k + 128 * p : 768 * k + 128 * p + 128] = pair.astype(jnp.bfloat16)
        out = jnp.dot(turned[...], table[j], preferred_element_type=jnp.float32)
        return out * (640.0 ** -0.5)

    def copy_b(d, c):
        to = lax.rem(h + d, DST)
        return pltpu.make_async_remote_copy(
            src_ref=send_b.at[c, to], dst_ref=out_ref.at[h, pl.ds(96 * c, 96), :],
            send_sem=sent_b.at[c, d], recv_sem=came_b.at[c, d], device_id=(g, to), device_id_type=MESH,
        )

    def copy_own(c):
        return pltpu.make_async_copy(send_b.at[c, h], out_ref.at[h, pl.ds(96 * c, 96), :], own.at[1 + c])

    def quad(c, carry):
        for jj in range(2):
            one = turn_of(4 * c + 2 * jj)
            two = turn_of(4 * c + 2 * jj + 1)
            for a in range(DST):
                both = jnp.concatenate([one[24 * a : 24 * a + 24], two[24 * a : 24 * a + 24]], axis=0)
                send_b[c, a, pl.ds(48 * jj, 48), :] = both.astype(jnp.bfloat16)
        for d in range(1, DST):
            copy_b(d, c).start()
        copy_own(c).start()
        return carry

    lax.fori_loop(0, 4, quad, 0)
    for d in range(1, SRC):
        copy_a(d).wait_send()

    def finish(c, carry):
        copy_own(c).wait()
        for d in range(1, DST):
            copy_b(d, c).wait()
        return carry

    lax.fori_loop(0, 4, finish, 0)
    for sends, copy, gets, fill in sides:
        pl.when(sends)(copy.wait_send)
        pl.when(gets)(copy.wait_recv)
        pl.when(jnp.logical_not(gets))(fill.wait)


def winds_of(spectral, legendre, tracers, wave_ids, points):
    ids = jnp.zeros((6, 3, 40), jnp.float32).reshape(18, 40).at[:16].set(wave_ids.reshape(16, 40).astype(jnp.float32))
    ids = jnp.pad(ids.reshape(6, 120), ((0, 0), (0, 8))).reshape(768)
    rowid = jnp.broadcast_to(ids[:, None], (768, 128))
    laneid = jnp.broadcast_to(ids[None, :], (8, 768))
    vmem = pl.BlockSpec(memory_space=pltpu.VMEM)
    hbm = pl.BlockSpec(memory_space=pl.ANY)
    return pl.pallas_call(
        spectral_kernel,
        in_specs=[hbm, hbm, hbm, vmem, vmem, pl.BlockSpec(memory_space=pltpu.SMEM)],
        out_specs=[hbm] * 5,
        out_shape=[
            jax.ShapeDtypeStruct((8, 384, 256), jnp.bfloat16),
            jax.ShapeDtypeStruct((64, 16, 256), jnp.bfloat16),
            jax.ShapeDtypeStruct((64, 16, 256), jnp.bfloat16),
            jax.ShapeDtypeStruct((256, 128), jnp.bfloat16),
            jax.ShapeDtypeStruct((256, 128), jnp.bfloat16),
        ],
        scratch_shapes=[
            pltpu.VMEM((48, 40, 1280), jnp.bfloat16),
            pltpu.VMEM((10, 1920, 128), jnp.float32),
            pltpu.VMEM((3, 5, 1280, 256), jnp.bfloat16),
            pltpu.VMEM((2, 16, 8, 16, 256), jnp.bfloat16),
            pltpu.VMEM((2, 256, 128), jnp.float32),
            pltpu.VMEM((256, 128), jnp.float32),
            pltpu.VMEM((64, 16, 256), jnp.bfloat16),
            pltpu.VMEM((64, 16, 256), jnp.bfloat16),
            pltpu.VMEM((256, 128), jnp.bfloat16),
            pltpu.VMEM((64, 16, 256), jnp.bfloat16),
            pltpu.VMEM((256, 128), jnp.bfloat16),
            pltpu.VMEM((2, 1920, 128), jnp.float32),
            pltpu.VMEM((16, 16, 16, 128), jnp.bfloat16),
            pltpu.VMEM((16, 16, 16, 128), jnp.bfloat16),
            pltpu.VMEM((16, 1536, 256), jnp.bfloat16),
            pltpu.VMEM((16, 2, 6, 8, 128), jnp.float32),
            pltpu.VMEM((4096, 128), jnp.float32),
            pltpu.VMEM((3, 2, 6, 8, 128), jnp.float32),
            pltpu.VMEM((192, 1536), jnp.bfloat16),
            pltpu.VMEM((4, 8, 96, 256), jnp.bfloat16),
            pltpu.SemaphoreType.DMA((16,)),
            pltpu.SemaphoreType.DMA((16,)),
            pltpu.SemaphoreType.DMA((4, 8)),
            pltpu.SemaphoreType.DMA((4, 8)),
            pltpu.SemaphoreType.DMA((9,)),
            pltpu.SemaphoreType.DMA((4,)),
            pltpu.SemaphoreType.DMA((4,)),
            pltpu.SemaphoreType.DMA,
            pltpu.SemaphoreType.DMA((3,)),
            pltpu.SemaphoreType.DMA((2,)),
        ],
        compiler_params=pltpu.CompilerParams(
            collective_id=0, has_side_effects=True, vmem_limit_bytes=60 * 1024 * 1024
        ),
        name="winds",
    )(spectral, legendre, tracers, rowid, laneid, points)


def rows_of(ref, start, size, stride):
    return jnp.concatenate([ref[k, pl.ds(start, size, stride=stride), :] for k in range(2)], axis=1)


def chem_kernel(
    ids_ref, tr_ref, wind_ref, north_ref, south_ref, east_ref, west_ref, mask_ref, base_ref, temp_ref, *rest
):
    out_ref, got_ref, wide, east, west, mix, *kept = rest
    towers, moved, moved_b = kept[:2], kept[2:4], kept[4:6]
    chosen, sent, came, own = kept[6:]
    step = pl.program_id(0)
    g, tile = lax.axis_index("lat"), lax.axis_index("lon")
    h = lax.rem(tile + 1 + step, DST)
    levels = out_ref.shape[1]
    barrier = pltpu.get_barrier_semaphore()

    def send(d):
        to = lax.rem(tile + d, DST)
        return pltpu.make_async_remote_copy(
            src_ref=chosen.at[to], dst_ref=got_ref.at[tile], send_sem=sent.at[d], recv_sem=came.at[d],
            device_id=(g, to), device_id_type=MESH,
        )

    @pl.when(step == 0)
    def _():
        for d in range(1, DST):
            pl.semaphore_signal(barrier, inc=1, device_id=(g, lax.rem(tile + d, DST)), device_id_type=MESH)
        east[...] = east_ref[...].astype(jnp.float32)
        west[...] = west_ref[...].astype(jnp.float32)
        row = lax.broadcasted_iota(jnp.int32, (256, 16), 0)
        col = lax.broadcasted_iota(jnp.int32, (256, 16), 1)
        spread = jnp.where(row // 16 == col, 1.0, 0.0).astype(jnp.bfloat16)
        row = lax.broadcasted_iota(jnp.int32, (256, 256), 0)
        col = lax.broadcasted_iota(jnp.int32, (256, 256), 1)
        same = row % 16 == col % 16
        for k, ref in enumerate((base_ref, temp_ref)):
            rows = jnp.dot(spread, ref[...].astype(jnp.bfloat16), preferred_element_type=jnp.float32)
            full = lax.dot_general(
                rows.astype(jnp.bfloat16), spread, (((1,), (1,)), ((), ())), preferred_element_type=jnp.float32
            )
            full = jnp.where(same, full, 0.0).astype(jnp.bfloat16)
            for c in range(0, 16, CHUNK):
                mix[pl.ds(32 * c + 16 * CHUNK * k, 16 * CHUNK), :] = full[16 * c : 16 * (c + CHUNK)]

    for k in range(2):
        wide[k] = wind_ref[0, :, 128 * k : 128 * k + 128].astype(jnp.float32)
    lane = lax.broadcasted_iota(jnp.int32, (16, 128), 1)
    mask = mask_ref[...]

    def advect(l, kept, kept_b, tower):
        at = h * 8 + l
        local = l
        u = 0.1 * rows_of(wide, local, 16, 24)
        v = 0.1 * rows_of(wide, 8 + local, 16, 24)
        east_w, west_w = (0.05 - u) * mask, (0.05 + u) * mask
        north_w, south_w = (0.05 - v) * mask, (0.05 + v) * mask
        own_w = 0.8 * mask
        for k in range(2):
            half = slice(128 * k, 128 * k + 128)
            tower[k, pl.ds(0, 16, stride=36), :] = south_ref[l, :, half].astype(jnp.float32)
            tower[k, pl.ds(34, 16, stride=36), :] = north_ref[l, :, half].astype(jnp.float32)
        for t in range(16):
            x = tr_ref[t, l].astype(jnp.float32)
            xl, xr = x[:, :128], x[:, 128:]
            for k, part_x in enumerate((xl, xr)):
                tower[k, pl.ds(36 * t + 2, 16, stride=2), :] = part_x
            he = pltpu.roll(east[pl.ds(16 * t, 16), :], 127 - at, 1)
            hw = pltpu.roll(west[pl.ds(16 * t, 16), :], 64 - at, 1)
            el, er = pltpu.roll(xl, 127, 1), pltpu.roll(xr, 127, 1)
            wl, wr = pltpu.roll(xl, 1, 1), pltpu.roll(xr, 1, 1)
            xe = jnp.concatenate([jnp.where(lane == 127, er, el), jnp.where(lane == 127, he, er)], axis=1)
            xw = jnp.concatenate([jnp.where(lane == 0, hw, wl), jnp.where(lane == 0, wl, wr)], axis=1)
            xn = rows_of(tower, 36 * t + 4, 16, 2)
            xs = rows_of(tower, 36 * t, 16, 2)
            q = own_w * x + east_w * xe + west_w * xw + north_w * xn + south_w * xs
            kept[t] = q
            kept_b[pl.ds(16 * t, 16), :] = q.astype(jnp.bfloat16)

    def settle(l, kept, kept_b):
        temper = rows_of(wide, 16 + l, 16, 24)
        for c in range(0, 16, CHUNK):
            y = jnp.dot(mix[pl.ds(32 * c, 32 * CHUNK), :], kept_b[...], preferred_element_type=jnp.float32)
            for t in range(CHUNK):
                base, heat = y[16 * t : 16 * t + 16], y[16 * (CHUNK + t) : 16 * (CHUNK + t) + 16]
                q = kept[c + t] + base + temper * heat
                kept[c + t] = q
                out_ref[c + t, l] = q.astype(jnp.bfloat16)
        for a in range(4):
            chosen[h, a, l] = kept[ids_ref[a]].astype(jnp.bfloat16)

    def several(i, carry):
        pend = None
        for k in range(UNROLL):
            l = UNROLL * i + k
            now = (l, moved[k % 2], moved_b[k % 2])
            advect(*now, towers[k % 2])
            if pend is not None:
                settle(*pend)
            pend = now
        settle(*pend)
        return carry

    lax.fori_loop(0, levels // UNROLL, several, 0)

    @pl.when(step == 0)
    def _():
        pl.semaphore_wait(barrier, DST - 1)

    @pl.when(step < DST - 1)
    def _():
        send(step + 1).start()

    @pl.when(step == DST - 1)
    def _():
        mine = pltpu.make_async_copy(chosen.at[tile], got_ref.at[tile], own)
        mine.start()
        mine.wait()
        for d in range(1, DST):
            send(d).wait()


def chemistry(tracers, winds, north, south, east, west, mask, base, temp, ids):
    whole = lambda s, i: (0, 0)
    source = lambda s: lax.rem(lax.axis_index("lon") + 1 + s, DST)
    hbm = pl.BlockSpec(memory_space=pl.ANY)
    return pl.pallas_call(
        chem_kernel,
        grid_spec=pltpu.PrefetchScalarGridSpec(
            num_scalar_prefetch=1,
            grid=(8,),
            in_specs=[
                pl.BlockSpec((16, 8, 16, 256), lambda s, i: (0, source(s), 0, 0)),
                pl.BlockSpec((1, 384, 256), lambda s, i: (source(s), 0, 0)),
                pl.BlockSpec((8, 16, 256), lambda s, i: (source(s), 0, 0)),
                pl.BlockSpec((8, 16, 256), lambda s, i: (source(s), 0, 0)),
                pl.BlockSpec((256, 128), whole),
                pl.BlockSpec((256, 128), whole),
                pl.BlockSpec((16, 256), whole),
                pl.BlockSpec((16, 16), whole),
                pl.BlockSpec((16, 16), whole),
            ],
            out_specs=[pl.BlockSpec((16, 8, 16, 256), lambda s, i: (0, source(s), 0, 0)), hbm],
            scratch_shapes=[
                pltpu.VMEM((2, 384, 128), jnp.float32),
                pltpu.VMEM((256, 128), jnp.float32),
                pltpu.VMEM((256, 128), jnp.float32),
                pltpu.VMEM((512, 256), jnp.bfloat16),
                pltpu.VMEM((2, 576, 128), jnp.float32),
                pltpu.VMEM((2, 576, 128), jnp.float32),
                pltpu.VMEM((16, 16, 256), jnp.float32),
                pltpu.VMEM((16, 16, 256), jnp.float32),
                pltpu.VMEM((256, 256), jnp.bfloat16),
                pltpu.VMEM((256, 256), jnp.bfloat16),
                pltpu.VMEM((8, 4, 8, 16, 256), jnp.bfloat16),
                pltpu.SemaphoreType.DMA((8,)),
                pltpu.SemaphoreType.DMA((8,)),
                pltpu.SemaphoreType.DMA,
            ],
        ),
        out_shape=[
            jax.ShapeDtypeStruct((16, 64, 16, 256), jnp.bfloat16),
            jax.ShapeDtypeStruct((8, 4, 8, 16, 256), jnp.bfloat16),
        ],
        compiler_params=pltpu.CompilerParams(collective_id=1, has_side_effects=True),
        name="chemistry",
    )(ids, tracers, winds, north, south, east, west, mask, base, temp)


def body(spectral, legendre, wave_ids, points, tracers, react_base, react_temp, active_ids):
    winds, north, south, east, west = winds_of(
        spectral.reshape(48, 40, 1280), legendre, tracers, wave_ids, points
    )
    columns = lax.axis_index("lon") * 256 + jnp.arange(256)
    mask = (columns[None, :] < points[:, None]).astype(jnp.float32)
    fresh, active = chemistry(
        tracers, winds, north, south, east, west, mask, react_base, react_temp, active_ids
    )
    active = jnp.transpose(active, (1, 2, 3, 0, 4)).reshape(4, 8, 16, 2048).astype(jnp.float32)
    return (fresh, active)


def solution(mesh):
    in_specs = (
        P(None, LON, "lat", None),
        P("lat", None, None),
        P(),
        P("lat"),
        P(None, None, "lat", LON),
        P(),
        P(),
        P(),
    )
    out_specs = (P(None, None, "lat", LON), P(None, LON, "lat", None))
    return jax.shard_map(body, mesh=mesh, in_specs=in_specs, out_specs=out_specs, check_vma=False)
```

```python
import functools

import jax
import jax.numpy as jnp
from jax import lax
from jax.experimental import pallas as pl
from jax.experimental.pallas import tpu as pltpu
from jax.sharding import PartitionSpec as P

LON = "lon"


SRC = 16
UNROLL = 4
CHUNK = 8
DST = 8
MESH = pl.DeviceIdType.MESH
TILES = ((2, 1), (2, 0), (1, 1), (3, 0), (3, 1), (1, 0), (0, 1))
BANDS = (
    (1, 2, 0), (1, 2, 1), (0, 1, 0), (1, 0, 0), (0, 3, 1), (1, 1, 0), (0, 2, 0), (1, 3, 1),
    (0, 1, 1), (1, 0, 1), (0, 3, 0), (1, 1, 1), (0, 2, 1), (1, 3, 0), (0, 0, 1),
)
COS = (0.9999992006931535, -19.7389777615569, 64.92855937725766, -85.27036091136767,
       58.78399626476764, -21.059548245283555)
SIN = (6.283184911477688, -41.3415879428884, 81.59989458670537, -76.61384581975258,
       41.339653019987985, -12.465497972860707)


def tile_at(h, dx, dz, back=False):
    dx = (4 - dx) % 4 if back else dx
    return lax.rem(h // 2 + dx, 4) * 2 + lax.rem(lax.rem(h, 2) + dz, 2)


def band_at(g, dz, dy, dc):
    high = lax.rem(g // 8 + dz, 2)
    return high * 8 + lax.rem(lax.rem(g // 2, 4) + dy, 4) * 2 + lax.rem(lax.rem(g, 2) + dc, 2)


def tile_of_step(h, s):
    power = (1 + 3 * lax.rem(s, 2)) * (1 + 15 * lax.rem(s // 2, 2)) * (1 + 255 * (s // 4))
    code = sum(dx * 4**k for k, (dx, dz) in enumerate(TILES))
    return lax.rem(h // 2 + lax.rem(code // power, 4), 4) * 2 + lax.rem(lax.rem(h, 2) + 1 + s, 2)


def waves_at(product, count, inverse):
    turns = jnp.round(product * inverse)
    t = (product - turns * count) * inverse
    s = t * t
    c = COS[-1]
    for k in COS[-2::-1]:
        c = c * s + k
    d = SIN[-1]
    for k in SIN[-2::-1]:
        d = d * s + k
    return c, d * t


def spectral_kernel(
    spec_ref, leg_ref, tr_ref, ids_ref, pts_ref,
    out_ref, north_ref, south_ref, east_ref, west_ref,
    spec, spread, leg, band, wide_0, wide_1, wide_2, wide_3, cols, low, high, edge, empty, blank_cols,
    rowid, laneid, tall, send_a, got_a, table, phase, coef, line, turned, send_b,
    sent_a, came_a, sent_b, came_b, own, sent_h, came_h, taken, leg_in, band_in,
):
    g, h = lax.axis_index("lat"), lax.axis_index("lon")
    barrier = pltpu.get_barrier_semaphore()
    for d in range(1, SRC):
        pl.semaphore_signal(barrier, inc=1, device_id=(lax.rem(g + d, SRC), h), device_id_type=MESH)
    for d in range(1, DST):
        pl.semaphore_signal(barrier, inc=1, device_id=(g, lax.rem(h + d, DST)), device_id_type=MESH)

    wide = (wide_0, wide_1, wide_2, wide_3)

    def leg_copy(i):
        slot = lax.rem(i, 3)
        return pltpu.make_async_copy(leg_ref.at[pl.ds(5 * i, 5)], leg.at[slot], leg_in.at[slot])

    def band_copy(i):
        slot = lax.rem(i, 2)
        return pltpu.make_async_copy(tr_ref.at[:, pl.ds(8 * i, 8)], band.at[slot], band_in.at[slot])

    spec_copy = pltpu.make_async_copy(spec_ref, spec, taken)
    spec_copy.start()
    leg_copy(0).start()
    band_copy(0).start()
    leg_copy(1).start()
    band_copy(1).start()
    leg_copy(2).start()
    for p in range(6):
        ids = jnp.broadcast_to(ids_ref[p : p + 1, :], (128, 128)).astype(jnp.float32)
        laneid[:, 128 * p : 128 * p + 128] = ids[:8]
        rowid[128 * p : 128 * p + 128, :] = ids.T
    empty[...] = jnp.zeros_like(empty)
    blank_cols[...] = jnp.zeros_like(blank_cols)
    cols[...] = jnp.zeros_like(cols)
    spec_copy.wait()

    def loosen(i, carry):
        for r in range(4):
            for k in range(10):
                part = spec[4 * i + r, :, 128 * k : 128 * k + 128]
                spread[k, pl.ds(160 * i + 40 * r, 40), :] = part.astype(jnp.float32)
        return carry

    lax.fori_loop(0, 12, loosen, 0)
    lane = lax.broadcasted_iota(jnp.int32, (256, 128), 1)

    shape = (128, 128)

    def tables(j, carry):
        count = jnp.full((1, 1), pts_ref[j], jnp.int32).astype(jnp.float32)
        inverse = 1.0 / count
        far = lax.broadcasted_iota(jnp.int32, (8, 128), 0).astype(jnp.float32) * 256.0
        lane = lax.broadcasted_iota(jnp.int32, shape, 1).astype(jnp.float32)
        for p in range(6):
            ids = laneid[:, pl.ds(128 * p, 128)]
            c, s = waves_at(ids * far, count, inverse)
            phase[j, 0, p] = c
            phase[j, 1, p] = s
        for p in range(6):
            ids = rowid[pl.ds(128 * p, 128), :]
            c, s = waves_at(ids * lane, count, inverse)
            c1 = jnp.broadcast_to(c[:, 64:65], shape)
            s1 = jnp.broadcast_to(s[:, 64:65], shape)
            c1, s1 = c1 * c1 - s1 * s1, 2.0 * c1 * s1
            table[j, pl.ds(128 * p, 128), pl.ds(0, 128)] = c.astype(jnp.bfloat16)
            table[j, pl.ds(768 + 128 * p, 128), pl.ds(0, 128)] = (-s).astype(jnp.bfloat16)
            table[j, pl.ds(128 * p, 128), pl.ds(128, 128)] = (c * c1 - s * s1).astype(jnp.bfloat16)
            table[j, pl.ds(768 + 128 * p, 128), pl.ds(128, 128)] = (-(s * c1 + c * s1)).astype(jnp.bfloat16)
        return carry

    def step(i, carry):
        slot = lax.rem(i, 3)
        leg_copy(i).wait()
        tables(i, 0)
        for w in range(5):
            m = 5 * i + w
            rows = [spread[k, pl.ds(m, 48, stride=40), :].astype(jnp.bfloat16) for k in range(10)]
            value = jnp.dot(jnp.concatenate(rows, axis=1), leg[slot, w], preferred_element_type=jnp.float32)
            for k in range(2):
                tall[k, pl.ds(48 * m, 48), :] = value[:, 128 * k : 128 * k + 128]

        @pl.when(i < 5)
        def _():
            leg_copy(i + 3).start()

        side = lax.rem(i, 2)
        band_copy(i).wait()

        def level(l, carry):
            kept = cols[...]
            for n in range(4):
                at = 8 * i + 4 * l + n
                x = band[side, :, 4 * l + n].reshape(256, 256).astype(jnp.float32)
                for k in range(2):
                    wide[n][k] = x[:, 128 * k : 128 * k + 128]
                low[at] = rows_of(wide[n], 0, 16, 16).astype(jnp.bfloat16)
                high[at] = rows_of(wide[n], 15, 16, 16).astype(jnp.bfloat16)
                first = pltpu.roll(x[:, :128], at, 1)
                last = pltpu.roll(x[:, 128:], lax.rem(at + 65, 128), 1)
                kept = jnp.where(lane == at, first, jnp.where(lane == at + 64, last, kept))
            cols[...] = kept
            return carry

        lax.fori_loop(0, 2, level, 0)

        @pl.when(i < 6)
        def _():
            band_copy(i + 2).start()

        return carry

    lax.fori_loop(0, 8, step, 0)
    edge[...] = cols[...].astype(jnp.bfloat16)
    blank = jnp.zeros((8, 128), jnp.float32)

    def turn(r, carry):
        for k in range(2):
            parts = [tall[k, pl.ds(16 * f + r, 40, stride=48), :] for f in range(3)]
            block = jnp.concatenate(parts + [blank], axis=0).T.astype(jnp.bfloat16)
            for b in range(8):
                send_a[8 * k + b, r] = block[16 * b : 16 * b + 16]
        return carry

    lax.fori_loop(0, 16, turn, 0)
    pl.semaphore_wait(barrier, SRC + DST - 2)

    def copy_a(d):
        to = band_at(g, *BANDS[d - 1])
        return pltpu.make_async_remote_copy(
            src_ref=send_a.at[to], dst_ref=got_a.at[g], send_sem=sent_a.at[d], recv_sem=came_a.at[d],
            device_id=(to, h), device_id_type=MESH,
        )

    for d in range(1, SRC):
        copy_a(d).start()
    mine = pltpu.make_async_copy(send_a.at[g], got_a.at[g], own.at[0])
    mine.start()

    def halo(k, src, dst, lat, lon):
        return pltpu.make_async_remote_copy(
            src_ref=src, dst_ref=dst, send_sem=sent_h.at[k], recv_sem=came_h.at[k],
            device_id=(lat, lon), device_id_type=MESH,
        )

    to_north = halo(0, high, south_ref, lax.rem(g + 1, SRC), h)
    to_south = halo(1, low, north_ref, lax.rem(g + SRC - 1, SRC), h)
    to_east = halo(2, edge, west_ref, g, lax.rem(h + 1, DST))
    to_west = halo(3, edge, east_ref, g, lax.rem(h + DST - 1, DST))
    none_south = pltpu.make_async_copy(empty, south_ref, own.at[5])
    none_north = pltpu.make_async_copy(empty, north_ref, own.at[6])
    none_west = pltpu.make_async_copy(blank_cols, west_ref, own.at[7])
    none_east = pltpu.make_async_copy(blank_cols, east_ref, own.at[8])
    sides = (
        (g < SRC - 1, to_north, g > 0, none_south),
        (g > 0, to_south, g < SRC - 1, none_north),
        (h < DST - 1, to_east, h > 0, none_west),
        (h > 0, to_west, h < DST - 1, none_east),
    )
    for sends, copy, gets, fill in sides:
        pl.when(sends)(copy.start)
        pl.when(jnp.logical_not(gets))(fill.start)

    lax.fori_loop(8, 16, tables, 0)

    mine.wait()
    for d in range(1, SRC):
        copy_a(d).wait_recv()

    def widen(q, carry):
        coef[pl.ds(256 * q, 256), :] = got_a[q].reshape(256, 128).astype(jnp.float32)
        return carry

    lax.fori_loop(0, SRC, widen, 0)

    def turn_of(j):
        lane = lax.broadcasted_iota(jnp.int32, (16, 128), 1)
        for p in range(6):
            held = []
            for q in range(3):
                s = 3 * p + q
                if s < SRC:
                    held.append(coef[pl.ds(256 * s + j, 16, stride=16), :])
                else:
                    held.append(None)
            for f in range(3):
                value = jnp.zeros((16, 128), jnp.float32)
                for q in range(3):
                    if held[q] is None:
                        continue
                    moved = held[q] if q == f else pltpu.roll(held[q], (40 * (q - f)) % 128, 1)
                    value = jnp.where((lane >= 40 * q) & (lane < 40 * q + 40), moved, value)
                re, im = value[:8], value[8:]
                line[f, 0, p] = re
                line[f, 1, p] = im
        for p in range(6):
            for a in range(0, DST, 2):
                parts = []
                for b in range(6):
                    row, f = a + b // 3, b % 3
                    c = phase[j, 0, p, row : row + 1, :]
                    s = phase[j, 1, p, row : row + 1, :]
                    re, im = line[f, 0, p], line[f, 1, p]
                    parts.append((re * c - im * s, re * s + im * c))
                for b in range(0, 6, 2):
                    at = 24 * a + 8 * b
                    for k in range(2):
                        pair = jnp.concatenate([parts[b][k], parts[b + 1][k]], axis=0)
                        turned[at : at + 16, 768 * k + 128 * p : 768 * k + 128 * p + 128] = pair.astype(jnp.bfloat16)
        out = jnp.dot(turned[...], table[j], preferred_element_type=jnp.float32)
        return out * (640.0 ** -0.5)

    def copy_b(d, c):
        to = tile_at(h, *TILES[d - 1])
        return pltpu.make_async_remote_copy(
            src_ref=send_b.at[c, to], dst_ref=out_ref.at[h, pl.ds(96 * c, 96), :],
            send_sem=sent_b.at[c, d], recv_sem=came_b.at[c, d], device_id=(g, to), device_id_type=MESH,
        )

    def copy_own(c):
        return pltpu.make_async_copy(send_b.at[c, h], out_ref.at[h, pl.ds(96 * c, 96), :], own.at[1 + c])

    def quad(c, carry):
        for jj in range(2):
            one = turn_of(4 * c + 2 * jj)
            two = turn_of(4 * c + 2 * jj + 1)
            for a in range(DST):
                both = jnp.concatenate([one[24 * a : 24 * a + 24], two[24 * a : 24 * a + 24]], axis=0)
                send_b[c, a, pl.ds(48 * jj, 48), :] = both.astype(jnp.bfloat16)
        for d in range(1, DST):
            copy_b(d, c).start()
        copy_own(c).start()
        return carry

    lax.fori_loop(0, 4, quad, 0)
    for d in range(1, SRC):
        copy_a(d).wait_send()

    def finish(c, carry):
        copy_own(c).wait()
        for d in range(1, DST):
            copy_b(d, c).wait()
        return carry

    lax.fori_loop(0, 4, finish, 0)
    for sends, copy, gets, fill in sides:
        pl.when(sends)(copy.wait_send)
        pl.when(gets)(copy.wait_recv)
        pl.when(jnp.logical_not(gets))(fill.wait)


def winds_of(spectral, legendre, tracers, wave_ids, points):
    ids = jnp.pad(wave_ids.reshape(16, 40), ((0, 2), (0, 0)))
    ids = jnp.pad(ids.reshape(6, 120), ((0, 2), (0, 8)))
    vmem = pl.BlockSpec(memory_space=pltpu.VMEM)
    hbm = pl.BlockSpec(memory_space=pl.ANY)
    return pl.pallas_call(
        spectral_kernel,
        in_specs=[hbm, hbm, hbm, vmem, pl.BlockSpec(memory_space=pltpu.SMEM)],
        out_specs=[hbm] * 5,
        out_shape=[
            jax.ShapeDtypeStruct((8, 384, 256), jnp.bfloat16),
            jax.ShapeDtypeStruct((64, 16, 256), jnp.bfloat16),
            jax.ShapeDtypeStruct((64, 16, 256), jnp.bfloat16),
            jax.ShapeDtypeStruct((256, 128), jnp.bfloat16),
            jax.ShapeDtypeStruct((256, 128), jnp.bfloat16),
        ],
        scratch_shapes=[
            pltpu.VMEM((48, 40, 1280), jnp.bfloat16),
            pltpu.VMEM((10, 1920, 128), jnp.float32),
            pltpu.VMEM((3, 5, 1280, 256), jnp.bfloat16),
            pltpu.VMEM((2, 16, 8, 16, 256), jnp.bfloat16),
            pltpu.VMEM((2, 256, 128), jnp.float32),
            pltpu.VMEM((2, 256, 128), jnp.float32),
            pltpu.VMEM((2, 256, 128), jnp.float32),
            pltpu.VMEM((2, 256, 128), jnp.float32),
            pltpu.VMEM((256, 128), jnp.float32),
            pltpu.VMEM((64, 16, 256), jnp.bfloat16),
            pltpu.VMEM((64, 16, 256), jnp.bfloat16),
            pltpu.VMEM((256, 128), jnp.bfloat16),
            pltpu.VMEM((64, 16, 256), jnp.bfloat16),
            pltpu.VMEM((256, 128), jnp.bfloat16),
            pltpu.VMEM((768, 128), jnp.float32),
            pltpu.VMEM((8, 768), jnp.float32),
            pltpu.VMEM((2, 1920, 128), jnp.float32),
            pltpu.VMEM((16, 16, 16, 128), jnp.bfloat16),
            pltpu.VMEM((16, 16, 16, 128), jnp.bfloat16),
            pltpu.VMEM((16, 1536, 256), jnp.bfloat16),
            pltpu.VMEM((16, 2, 6, 8, 128), jnp.float32),
            pltpu.VMEM((4096, 128), jnp.float32),
            pltpu.VMEM((3, 2, 6, 8, 128), jnp.float32),
            pltpu.VMEM((192, 1536), jnp.bfloat16),
            pltpu.VMEM((4, 8, 96, 256), jnp.bfloat16),
            pltpu.SemaphoreType.DMA((16,)),
            pltpu.SemaphoreType.DMA((16,)),
            pltpu.SemaphoreType.DMA((4, 8)),
            pltpu.SemaphoreType.DMA((4, 8)),
            pltpu.SemaphoreType.DMA((9,)),
            pltpu.SemaphoreType.DMA((4,)),
            pltpu.SemaphoreType.DMA((4,)),
            pltpu.SemaphoreType.DMA,
            pltpu.SemaphoreType.DMA((3,)),
            pltpu.SemaphoreType.DMA((2,)),
        ],
        compiler_params=pltpu.CompilerParams(
            collective_id=0, has_side_effects=True, vmem_limit_bytes=60 * 1024 * 1024
        ),
        name="winds",
    )(spectral, legendre, tracers, ids, points)


def rows_of(ref, start, size, stride):
    return jnp.concatenate([ref[k, pl.ds(start, size, stride=stride), :] for k in range(2)], axis=1)


def chem_kernel(
    ids_ref, pts_ref, tr_ref, wind_ref, north_ref, south_ref, east_ref, west_ref, base_ref, temp_ref, *rest
):
    out_ref, got_ref, wide, east, west, mix, *kept = rest
    towers, moved, moved_b = kept[:2], kept[2:4], kept[4:6]
    chosen, sent, came, own = kept[6:]
    step = pl.program_id(0)
    g, tile = lax.axis_index("lat"), lax.axis_index("lon")
    h = tile_of_step(tile, step)
    levels = out_ref.shape[1]
    barrier = pltpu.get_barrier_semaphore()

    place = got_ref.at[:, :, :, pl.ds(pl.multiple_of(tile * 256, 256), 256)]

    def send(d):
        to = tile_of_step(tile, d - 1)
        return pltpu.make_async_remote_copy(
            src_ref=chosen.at[to], dst_ref=place, send_sem=sent.at[d], recv_sem=came.at[d],
            device_id=(g, to), device_id_type=MESH,
        )

    @pl.when(step == 0)
    def _():
        for d in range(1, DST):
            pl.semaphore_signal(barrier, inc=1, device_id=(g, lax.rem(tile + d, DST)), device_id_type=MESH)
        east[...] = east_ref[...].astype(jnp.float32)
        west[...] = west_ref[...].astype(jnp.float32)
        row = lax.broadcasted_iota(jnp.int32, (256, 16), 0)
        col = lax.broadcasted_iota(jnp.int32, (256, 16), 1)
        spread = jnp.where(row // 16 == col, 1.0, 0.0).astype(jnp.bfloat16)
        row = lax.broadcasted_iota(jnp.int32, (256, 256), 0)
        col = lax.broadcasted_iota(jnp.int32, (256, 256), 1)
        same = row % 16 == col % 16
        for k, ref in enumerate((base_ref, temp_ref)):
            rows = jnp.dot(spread, ref[...].astype(jnp.bfloat16), preferred_element_type=jnp.float32)
            full = lax.dot_general(
                rows.astype(jnp.bfloat16), spread, (((1,), (1,)), ((), ())), preferred_element_type=jnp.float32
            )
            full = jnp.where(same, full, 0.0).astype(jnp.bfloat16)
            for c in range(0, 16, CHUNK):
                mix[pl.ds(32 * c + 16 * CHUNK * k, 16 * CHUNK), :] = full[16 * c : 16 * (c + CHUNK)]

    for k in range(2):
        wide[k] = wind_ref[0, :, 128 * k : 128 * k + 128].astype(jnp.float32)
    lane = lax.broadcasted_iota(jnp.int32, (16, 128), 1)
    row = lax.broadcasted_iota(jnp.int32, (16, 256), 0)
    limit = jnp.zeros((16, 256), jnp.int32)
    for j in range(16):
        limit = jnp.where(row == j, pts_ref[j], limit)
    column = lax.broadcasted_iota(jnp.int32, (16, 256), 1) + tile * 256
    mask = jnp.where(column < limit, 1.0, 0.0)

    def advect(l, kept, kept_b, tower):
        at = h * 8 + l
        local = l
        u = 0.1 * rows_of(wide, local, 16, 24)
        v = 0.1 * rows_of(wide, 8 + local, 16, 24)
        east_w, west_w = (0.05 - u) * mask, (0.05 + u) * mask
        north_w, south_w = (0.05 - v) * mask, (0.05 + v) * mask
        own_w = 0.8 * mask
        for k in range(2):
            half = slice(128 * k, 128 * k + 128)
            tower[k, pl.ds(0, 16, stride=36), :] = south_ref[l, :, half].astype(jnp.float32)
            tower[k, pl.ds(34, 16, stride=36), :] = north_ref[l, :, half].astype(jnp.float32)
        for t in range(16):
            x = tr_ref[t, l].astype(jnp.float32)
            xl, xr = x[:, :128], x[:, 128:]
            for k, part_x in enumerate((xl, xr)):
                tower[k, pl.ds(36 * t + 2, 16, stride=2), :] = part_x
            he = pltpu.roll(east[pl.ds(16 * t, 16), :], 127 - at, 1)
            hw = pltpu.roll(west[pl.ds(16 * t, 16), :], 64 - at, 1)
            el, er = pltpu.roll(xl, 127, 1), pltpu.roll(xr, 127, 1)
            wl, wr = pltpu.roll(xl, 1, 1), pltpu.roll(xr, 1, 1)
            xe = jnp.concatenate([jnp.where(lane == 127, er, el), jnp.where(lane == 127, he, er)], axis=1)
            xw = jnp.concatenate([jnp.where(lane == 0, hw, wl), jnp.where(lane == 0, wl, wr)], axis=1)
            xn = rows_of(tower, 36 * t + 4, 16, 2)
            xs = rows_of(tower, 36 * t, 16, 2)
            q = own_w * x + east_w * xe + west_w * xw + north_w * xn + south_w * xs
            kept[t] = q
            kept_b[pl.ds(16 * t, 16), :] = q.astype(jnp.bfloat16)

    def settle(l, kept, kept_b):
        temper = rows_of(wide, 16 + l, 16, 24)
        for c in range(0, 16, CHUNK):
            y = jnp.dot(mix[pl.ds(32 * c, 32 * CHUNK), :], kept_b[...], preferred_element_type=jnp.float32)
            for t in range(CHUNK):
                base, heat = y[16 * t : 16 * t + 16], y[16 * (CHUNK + t) : 16 * (CHUNK + t) + 16]
                q = kept[c + t] + base + temper * heat
                kept[c + t] = q
                out_ref[c + t, l] = q.astype(jnp.bfloat16)
        for a in range(4):
            chosen[h, a, l] = kept[ids_ref[a]].astype(jnp.bfloat16)

    def several(i, carry):
        pend = None
        for k in range(UNROLL):
            l = UNROLL * i + k
            now = (l, moved[k % 2], moved_b[k % 2])
            advect(*now, towers[k % 2])
            if pend is not None:
                settle(*pend)
            pend = now
        settle(*pend)
        return carry

    lax.fori_loop(0, levels // UNROLL, several, 0)

    @pl.when(step == 0)
    def _():
        pl.semaphore_wait(barrier, DST - 1)

    @pl.when(step < DST - 1)
    def _():
        send(step + 1).start()

    @pl.when(step == DST - 1)
    def _():
        mine = pltpu.make_async_copy(chosen.at[tile], place, own)
        mine.start()
        mine.wait()
        for d in range(1, DST):
            send(d).wait()


def chemistry(tracers, winds, north, south, east, west, base, temp, ids, points):
    whole = lambda s, i, p: (0, 0)
    source = lambda s: tile_of_step(lax.axis_index("lon"), s)
    hbm = pl.BlockSpec(memory_space=pl.ANY)
    return pl.pallas_call(
        chem_kernel,
        grid_spec=pltpu.PrefetchScalarGridSpec(
            num_scalar_prefetch=2,
            grid=(8,),
            in_specs=[
                pl.BlockSpec((16, 8, 16, 256), lambda s, i, p: (0, source(s), 0, 0)),
                pl.BlockSpec((1, 384, 256), lambda s, i, p: (source(s), 0, 0)),
                pl.BlockSpec((8, 16, 256), lambda s, i, p: (source(s), 0, 0)),
                pl.BlockSpec((8, 16, 256), lambda s, i, p: (source(s), 0, 0)),
                pl.BlockSpec((256, 128), whole),
                pl.BlockSpec((256, 128), whole),
                pl.BlockSpec((16, 16), whole),
                pl.BlockSpec((16, 16), whole),
            ],
            out_specs=[pl.BlockSpec((16, 8, 16, 256), lambda s, i, p: (0, source(s), 0, 0)), hbm],
            scratch_shapes=[
                pltpu.VMEM((2, 384, 128), jnp.float32),
                pltpu.VMEM((256, 128), jnp.float32),
                pltpu.VMEM((256, 128), jnp.float32),
                pltpu.VMEM((512, 256), jnp.bfloat16),
                pltpu.VMEM((2, 576, 128), jnp.float32),
                pltpu.VMEM((2, 576, 128), jnp.float32),
                pltpu.VMEM((16, 16, 256), jnp.float32),
                pltpu.VMEM((16, 16, 256), jnp.float32),
                pltpu.VMEM((256, 256), jnp.bfloat16),
                pltpu.VMEM((256, 256), jnp.bfloat16),
                pltpu.VMEM((8, 4, 8, 16, 256), jnp.bfloat16),
                pltpu.SemaphoreType.DMA((8,)),
                pltpu.SemaphoreType.DMA((8,)),
                pltpu.SemaphoreType.DMA,
            ],
        ),
        out_shape=[
            jax.ShapeDtypeStruct((16, 64, 16, 256), jnp.bfloat16),
            jax.ShapeDtypeStruct((4, 8, 16, 2048), jnp.bfloat16),
        ],
        compiler_params=pltpu.CompilerParams(collective_id=1, has_side_effects=True),
        name="chemistry",
    )(ids, points, tracers, winds, north, south, east, west, base, temp)


def body(spectral, legendre, wave_ids, points, tracers, react_base, react_temp, active_ids):
    winds, north, south, east, west = winds_of(
        spectral.reshape(48, 40, 1280), legendre, tracers, wave_ids, points
    )
    fresh, active = chemistry(
        tracers, winds, north, south, east, west, react_base, react_temp, active_ids, points
    )
    return (fresh, active.astype(jnp.float32))


def solution(mesh):
    in_specs = (
        P(None, LON, "lat", None),
        P("lat", None, None),
        P(),
        P("lat"),
        P(None, None, "lat", LON),
        P(),
        P(),
        P(),
    )
    out_specs = (P(None, None, "lat", LON), P(None, LON, "lat", None))
    return jax.shard_map(body, mesh=mesh, in_specs=in_specs, out_specs=out_specs, check_vma=False)
```

```python
import functools

import jax
import jax.numpy as jnp
from jax import lax
from jax.experimental import pallas as pl
from jax.experimental.pallas import tpu as pltpu
from jax.sharding import PartitionSpec as P

LON = "lon"


SRC = 16
PLANE = 136
UNROLL = 4
CHUNK = 8
DST = 8
MESH = pl.DeviceIdType.MESH
TILES = ((2, 1), (2, 0), (1, 1), (3, 0), (3, 1), (1, 0), (0, 1))
ORDER = ((1, 0), (3, 1), (1, 1), (3, 0), (0, 1), (2, 0), (2, 1))
BANDS = (
    (1, 2, 0), (1, 2, 1), (0, 1, 0), (1, 0, 0), (0, 3, 1), (1, 1, 0), (0, 2, 0), (1, 3, 1),
    (0, 1, 1), (1, 0, 1), (0, 3, 0), (1, 1, 1), (0, 2, 1), (1, 3, 0), (0, 0, 1),
)
COS = (0.9999992006931535, -19.7389777615569, 64.92855937725766, -85.27036091136767,
       58.78399626476764, -21.059548245283555)
SIN = (6.283184911477688, -41.3415879428884, 81.59989458670537, -76.61384581975258,
       41.339653019987985, -12.465497972860707)


def tile_at(h, dx, dz, back=False):
    dx = (4 - dx) % 4 if back else dx
    return lax.rem(h // 2 + dx, 4) * 2 + lax.rem(lax.rem(h, 2) + dz, 2)


def band_at(g, dz, dy, dc):
    high = lax.rem(g // 8 + dz, 2)
    return high * 8 + lax.rem(lax.rem(g // 2, 4) + dy, 4) * 2 + lax.rem(lax.rem(g, 2) + dc, 2)


def tile_of_step(h, step):
    late = step // 14
    s = lax.rem(step, 7) * (1 - late) + 7 * late
    part = step // 7 - 2 * late + late * lax.rem(step, 2)
    two = (1 + lax.rem(s, 2)) * (1 + 3 * lax.rem(s // 2, 2)) * (1 + 15 * (s // 4))
    code_x = sum(dx * 4**k for k, (dx, dz) in enumerate(ORDER))
    code_z = sum(dz * 2**k for k, (dx, dz) in enumerate(ORDER))
    x = lax.rem(h // 2 + lax.rem(code_x // (two * two), 4), 4)
    return x * 2 + lax.rem(lax.rem(h, 2) + lax.rem(code_z // two, 2), 2), part


def waves_at(product, count, inverse):
    turns = jnp.round(product * inverse)
    t = (product - turns * count) * inverse
    s = t * t
    c = COS[-1]
    for k in COS[-2::-1]:
        c = c * s + k
    d = SIN[-1]
    for k in SIN[-2::-1]:
        d = d * s + k
    return c, d * t


def spectral_kernel(
    spec_ref, leg_ref, tr_ref, ids_ref, pts_ref,
    out_ref, north_ref, south_ref, east_ref, west_ref,
    spec, spread, leg, band, wide_0, wide_1, wide_2, wide_3, cols, low, high, edge, empty, blank_cols,
    rowid, laneid, tall, send_a, got_a, table, phase, coef, line, turned, send_b,
    sent_a, came_a, sent_b, came_b, own, sent_h, came_h, taken, leg_in, band_in,
):
    g, h = lax.axis_index("lat"), lax.axis_index("lon")
    barrier = pltpu.get_barrier_semaphore()
    for d in range(1, SRC):
        pl.semaphore_signal(barrier, inc=1, device_id=(lax.rem(g + d, SRC), h), device_id_type=MESH)
    for d in range(1, DST):
        pl.semaphore_signal(barrier, inc=1, device_id=(g, lax.rem(h + d, DST)), device_id_type=MESH)

    wide = (wide_0, wide_1, wide_2, wide_3)

    def leg_copy(i):
        slot = lax.rem(i, 3)
        return pltpu.make_async_copy(leg_ref.at[pl.ds(5 * i, 5)], leg.at[slot], leg_in.at[slot])

    def band_copy(i):
        slot = lax.rem(i, 2)
        return pltpu.make_async_copy(tr_ref.at[:, pl.ds(8 * i, 8)], band.at[slot], band_in.at[slot])

    spec_copy = pltpu.make_async_copy(spec_ref, spec, taken)
    spec_copy.start()
    leg_copy(0).start()
    band_copy(0).start()
    leg_copy(1).start()
    band_copy(1).start()
    leg_copy(2).start()
    for p in range(6):
        ids = jnp.broadcast_to(ids_ref[p : p + 1, :], (128, 128)).astype(jnp.float32)
        laneid[:, 128 * p : 128 * p + 128] = ids[:8]
        rowid[128 * p : 128 * p + 128, :] = ids.T
    tall[...] = jnp.zeros_like(tall)
    empty[...] = jnp.zeros_like(empty)
    blank_cols[...] = jnp.zeros_like(blank_cols)
    cols[...] = jnp.zeros_like(cols)
    spec_copy.wait()

    def loosen(i, carry):
        for r in range(4):
            for k in range(10):
                part = spec[4 * i + r, :, 128 * k : 128 * k + 128]
                spread[k, pl.ds(160 * i + 40 * r, 40), :] = part.astype(jnp.float32)
        return carry

    lax.fori_loop(0, 12, loosen, 0)
    lane = lax.broadcasted_iota(jnp.int32, (256, 128), 1)

    shape = (128, 128)

    def tables(j, carry):
        count = jnp.full((1, 1), pts_ref[j], jnp.int32).astype(jnp.float32)
        inverse = 1.0 / count
        far = lax.broadcasted_iota(jnp.int32, (8, 128), 0).astype(jnp.float32) * 256.0
        lane = lax.broadcasted_iota(jnp.int32, shape, 1).astype(jnp.float32)
        for p in range(6):
            ids = laneid[:, pl.ds(128 * p, 128)]
            c, s = waves_at(ids * far, count, inverse)
            phase[j, 0, p] = c
            phase[j, 1, p] = s
        for p in range(6):
            ids = rowid[pl.ds(128 * p, 128), :]
            c, s = waves_at(ids * lane, count, inverse)
            c1 = jnp.broadcast_to(c[:, 64:65], shape)
            s1 = jnp.broadcast_to(s[:, 64:65], shape)
            c1, s1 = c1 * c1 - s1 * s1, 2.0 * c1 * s1
            table[j, pl.ds(128 * p, 128), pl.ds(0, 128)] = c.astype(jnp.bfloat16)
            table[j, pl.ds(768 + 128 * p, 128), pl.ds(0, 128)] = (-s).astype(jnp.bfloat16)
            table[j, pl.ds(128 * p, 128), pl.ds(128, 128)] = (c * c1 - s * s1).astype(jnp.bfloat16)
            table[j, pl.ds(768 + 128 * p, 128), pl.ds(128, 128)] = (-(s * c1 + c * s1)).astype(jnp.bfloat16)
        return carry

    def step(i, carry):
        slot = lax.rem(i, 3)
        leg_copy(i).wait()
        tables(i, 0)
        for w in range(5):
            m = 5 * i + w
            rows = [spread[k, pl.ds(m, 48, stride=40), :].astype(jnp.bfloat16) for k in range(10)]
            value = jnp.dot(jnp.concatenate(rows, axis=1), leg[slot, w], preferred_element_type=jnp.float32)
            for k in range(2):
                for q in range(6):
                    part = value[8 * q : 8 * q + 8, 128 * k : 128 * k + 128]
                    tall[k, pl.ds(20 * q + lax.rem(m, 20), 8, stride=PLANE), :] = part

        @pl.when(i < 5)
        def _():
            leg_copy(i + 3).start()

        return carry

    def edges(i, carry):
        side = lax.rem(i, 2)
        band_copy(i).wait()

        def level(l, carry):
            kept = cols[...]
            for n in range(4):
                at = 8 * i + 4 * l + n
                x = band[side, :, 4 * l + n].reshape(256, 256).astype(jnp.float32)
                for k in range(2):
                    wide[n][k] = x[:, 128 * k : 128 * k + 128]
                low[at] = rows_of(wide[n], 0, 16, 16).astype(jnp.bfloat16)
                high[at] = rows_of(wide[n], 15, 16, 16).astype(jnp.bfloat16)
                first = pltpu.roll(x[:, :128], at, 1)
                last = pltpu.roll(x[:, 128:], lax.rem(at + 65, 128), 1)
                kept = jnp.where(lane == at, first, jnp.where(lane == at + 64, last, kept))
            cols[...] = kept
            return carry

        lax.fori_loop(0, 2, level, 0)

        @pl.when(i < 6)
        def _():
            band_copy(i + 2).start()

        return carry

    lax.fori_loop(0, 8, edges, 0)
    edge[...] = cols[...].astype(jnp.bfloat16)
    pl.semaphore_wait(barrier, SRC + DST - 2)

    def halo(k, src, dst, lat, lon):
        return pltpu.make_async_remote_copy(
            src_ref=src, dst_ref=dst, send_sem=sent_h.at[k], recv_sem=came_h.at[k],
            device_id=(lat, lon), device_id_type=MESH,
        )

    to_north = halo(0, high, south_ref, lax.rem(g + 1, SRC), h)
    to_south = halo(1, low, north_ref, lax.rem(g + SRC - 1, SRC), h)
    to_east = halo(2, edge, west_ref, g, lax.rem(h + 1, DST))
    to_west = halo(3, edge, east_ref, g, lax.rem(h + DST - 1, DST))
    none_south = pltpu.make_async_copy(empty, south_ref, own.at[5])
    none_north = pltpu.make_async_copy(empty, north_ref, own.at[6])
    none_west = pltpu.make_async_copy(blank_cols, west_ref, own.at[7])
    none_east = pltpu.make_async_copy(blank_cols, east_ref, own.at[8])
    sides = (
        (g < SRC - 1, to_north, g > 0, none_south),
        (g > 0, to_south, g < SRC - 1, none_north),
        (h < DST - 1, to_east, h > 0, none_west),
        (h > 0, to_west, h < DST - 1, none_east),
    )
    for sends, copy, gets, fill in sides:
        pl.when(sends)(copy.start)
        pl.when(jnp.logical_not(gets))(fill.start)

    def turn(half):
        def pair(i, carry):
            for k in range(2):
                blocks = [tall[k, pl.ds(PLANE * (2 * i + n), 128), :].T for n in range(2)]
                for b in range(8):
                    for rows in range(2):
                        at = 16 * b + 8 * rows
                        both = jnp.concatenate([block[at : at + 8] for block in blocks], axis=0)
                        send_a[8 * k + b, half, rows, pl.ds(16 * i, 16), :] = both.astype(jnp.bfloat16)
            return carry

        lax.fori_loop(0, 4, pair, 0)

    def copy_a(d, k):
        to = band_at(g, *BANDS[d - 1])
        src, dst = ((send_a.at[to, 0], got_a.at[g, 0]), (send_a.at[to, 1, 0], got_a.at[g, 1, 0]),
                    (send_a.at[to, 1, 1], got_a.at[g, 1, 1]))[k]
        return pltpu.make_async_remote_copy(
            src_ref=src, dst_ref=dst, send_sem=sent_a.at[k, d], recv_sem=came_a.at[k, d],
            device_id=(to, h), device_id_type=MESH,
        )

    lax.fori_loop(0, 4, step, 0)
    turn(0)
    for d in range(1, SRC):
        copy_a(d, 0).start()
    lax.fori_loop(4, 8, step, 0)
    turn(1)
    for k in (1, 2):
        for d in range(1, SRC):
            copy_a(d, k).start()
    mine = pltpu.make_async_copy(send_a.at[g], got_a.at[g], own.at[0])
    mine.start()
    lax.fori_loop(8, 12, tables, 0)
    mine.wait()

    def widen(rows):
        def one(q, carry):
            for half in range(2):
                coef[pl.ds(64 * (2 * q + half), 64), :] = got_a[q, half, rows].astype(jnp.float32)
            return carry

        lax.fori_loop(0, SRC, one, 0)

    def turn_of(j):
        lane = lax.broadcasted_iota(jnp.int32, (8, 128), 1)
        row = lax.rem(j, 8)
        for p in range(6):
            count = min(6, 2 * SRC - 6 * p)
            held = [coef[pl.ds(64 * (6 * p + q) + row, 8, stride=8), :] for q in range(count)]
            for f in range(6):
                value = jnp.zeros((8, 128), jnp.float32)
                for q in range(count):
                    moved = held[q] if q == f else pltpu.roll(held[q], (20 * (q - f)) % 128, 1)
                    value = jnp.where((lane >= 20 * q) & (lane < 20 * q + 20), moved, value)
                line[f // 2, f % 2, p] = value
        for p in range(6):
            for a in range(0, DST, 2):
                parts = []
                for b in range(6):
                    row, f = a + b // 3, b % 3
                    c = phase[j, 0, p, row : row + 1, :]
                    s = phase[j, 1, p, row : row + 1, :]
                    re, im = line[f, 0, p], line[f, 1, p]
                    parts.append((re * c - im * s, re * s + im * c))
                for b in range(0, 6, 2):
                    at = 24 * a + 8 * b
                    for k in range(2):
                        pair = jnp.concatenate([parts[b][k], parts[b + 1][k]], axis=0)
                        turned[at : at + 16, 768 * k + 128 * p : 768 * k + 128 * p + 128] = pair.astype(jnp.bfloat16)
        out = jnp.dot(turned[...], table[j], preferred_element_type=jnp.float32)
        return out * (640.0 ** -0.5)

    def copy_b(d, c):
        to = tile_at(h, *TILES[d - 1])
        return pltpu.make_async_remote_copy(
            src_ref=send_b.at[c, to], dst_ref=out_ref.at[h, pl.ds(96 * c, 96), :],
            send_sem=sent_b.at[c, d], recv_sem=came_b.at[c, d], device_id=(g, to), device_id_type=MESH,
        )

    def copy_own(c):
        return pltpu.make_async_copy(send_b.at[c, h], out_ref.at[h, pl.ds(96 * c, 96), :], own.at[1 + c])

    def quad(c, carry):
        for jj in range(2):
            one = turn_of(4 * c + 2 * jj)
            two = turn_of(4 * c + 2 * jj + 1)
            for a in range(DST):
                both = jnp.concatenate([one[24 * a : 24 * a + 24], two[24 * a : 24 * a + 24]], axis=0)
                send_b[c, a, pl.ds(48 * jj, 48), :] = both.astype(jnp.bfloat16)
        for d in range(1, DST):
            copy_b(d, c).start()
        copy_own(c).start()
        return carry

    for rows in range(2):
        for k in ((0, 1), (2,))[rows]:
            for d in range(1, SRC):
                copy_a(d, k).wait_recv()
        widen(rows)
        lax.fori_loop(2 * rows, 2 * rows + 2, quad, 0)
        if rows == 0:
            lax.fori_loop(12, 16, tables, 0)
    for k in range(3):
        for d in range(1, SRC):
            copy_a(d, k).wait_send()

    def finish(c, carry):
        copy_own(c).wait()
        for d in range(1, DST):
            copy_b(d, c).wait()
        return carry

    lax.fori_loop(0, 4, finish, 0)
    for sends, copy, gets, fill in sides:
        pl.when(sends)(copy.wait_send)
        pl.when(gets)(copy.wait_recv)
        pl.when(jnp.logical_not(gets))(fill.wait)


def winds_of(spectral, legendre, tracers, wave_ids, points):
    ids = jnp.pad(wave_ids.reshape(32, 20), ((0, 4), (0, 0)))
    ids = jnp.pad(ids.reshape(6, 120), ((0, 2), (0, 8)))
    vmem = pl.BlockSpec(memory_space=pltpu.VMEM)
    hbm = pl.BlockSpec(memory_space=pl.ANY)
    return pl.pallas_call(
        spectral_kernel,
        in_specs=[hbm, hbm, hbm, vmem, pl.BlockSpec(memory_space=pltpu.SMEM)],
        out_specs=[hbm] * 5,
        out_shape=[
            jax.ShapeDtypeStruct((8, 384, 256), jnp.bfloat16),
            jax.ShapeDtypeStruct((64, 16, 256), jnp.bfloat16),
            jax.ShapeDtypeStruct((64, 16, 256), jnp.bfloat16),
            jax.ShapeDtypeStruct((256, 128), jnp.bfloat16),
            jax.ShapeDtypeStruct((256, 128), jnp.bfloat16),
        ],
        scratch_shapes=[
            pltpu.VMEM((48, 40, 1280), jnp.bfloat16),
            pltpu.VMEM((10, 1920, 128), jnp.float32),
            pltpu.VMEM((3, 5, 1280, 256), jnp.bfloat16),
            pltpu.VMEM((2, 16, 8, 16, 256), jnp.bfloat16),
            pltpu.VMEM((2, 256, 128), jnp.float32),
            pltpu.VMEM((2, 256, 128), jnp.float32),
            pltpu.VMEM((2, 256, 128), jnp.float32),
            pltpu.VMEM((2, 256, 128), jnp.float32),
            pltpu.VMEM((256, 128), jnp.float32),
            pltpu.VMEM((64, 16, 256), jnp.bfloat16),
            pltpu.VMEM((64, 16, 256), jnp.bfloat16),
            pltpu.VMEM((256, 128), jnp.bfloat16),
            pltpu.VMEM((64, 16, 256), jnp.bfloat16),
            pltpu.VMEM((256, 128), jnp.bfloat16),
            pltpu.VMEM((768, 128), jnp.float32),
            pltpu.VMEM((8, 768), jnp.float32),
            pltpu.VMEM((2, 8 * PLANE, 128), jnp.float32),
            pltpu.VMEM((16, 2, 2, 64, 128), jnp.bfloat16),
            pltpu.VMEM((16, 2, 2, 64, 128), jnp.bfloat16),
            pltpu.VMEM((16, 1536, 256), jnp.bfloat16),
            pltpu.VMEM((16, 2, 6, 8, 128), jnp.float32),
            pltpu.VMEM((2048, 128), jnp.float32),
            pltpu.VMEM((3, 2, 6, 8, 128), jnp.float32),
            pltpu.VMEM((192, 1536), jnp.bfloat16),
            pltpu.VMEM((4, 8, 96, 256), jnp.bfloat16),
            pltpu.SemaphoreType.DMA((3, 16)),
            pltpu.SemaphoreType.DMA((3, 16)),
            pltpu.SemaphoreType.DMA((4, 8)),
            pltpu.SemaphoreType.DMA((4, 8)),
            pltpu.SemaphoreType.DMA((9,)),
            pltpu.SemaphoreType.DMA((4,)),
            pltpu.SemaphoreType.DMA((4,)),
            pltpu.SemaphoreType.DMA,
            pltpu.SemaphoreType.DMA((3,)),
            pltpu.SemaphoreType.DMA((2,)),
        ],
        compiler_params=pltpu.CompilerParams(
            collective_id=0, has_side_effects=True, vmem_limit_bytes=60 * 1024 * 1024
        ),
        name="winds",
    )(spectral, legendre, tracers, ids, points)


def rows_of(ref, start, size, stride):
    return jnp.concatenate([ref[k, pl.ds(start, size, stride=stride), :] for k in range(2)], axis=1)


def chem_kernel(
    ids_ref, pts_ref, tr_ref, wind_ref, north_ref, south_ref, east_ref, west_ref, base_ref, temp_ref, *rest
):
    out_ref, got_ref, wide, east, west, mix, *kept = rest
    towers, moved, moved_b = kept[:2], kept[2:4], kept[4:6]
    chosen, sent, came, own = kept[6:]
    step = pl.program_id(0)
    g, tile = lax.axis_index("lat"), lax.axis_index("lon")
    h, part = tile_of_step(tile, step)
    levels = out_ref.shape[1]
    barrier = pltpu.get_barrier_semaphore()

    place = got_ref.at[:, :, :, pl.ds(pl.multiple_of(tile * 256, 256), 256)]

    def send(d):
        to, some = tile_of_step(tile, d)
        rows = pl.ds(4 * some, 4)
        return pltpu.make_async_remote_copy(
            src_ref=chosen.at[to, :, rows], dst_ref=place.at[:, rows], send_sem=sent.at[d], recv_sem=came.at[d],
            device_id=(g, to), device_id_type=MESH,
        )

    @pl.when(step == 0)
    def _():
        for d in range(1, DST):
            pl.semaphore_signal(barrier, inc=1, device_id=(g, lax.rem(tile + d, DST)), device_id_type=MESH)
        east[...] = east_ref[...].astype(jnp.float32)
        west[...] = west_ref[...].astype(jnp.float32)
        row = lax.broadcasted_iota(jnp.int32, (256, 16), 0)
        col = lax.broadcasted_iota(jnp.int32, (256, 16), 1)
        spread = jnp.where(row // 16 == col, 1.0, 0.0).astype(jnp.bfloat16)
        row = lax.broadcasted_iota(jnp.int32, (256, 256), 0)
        col = lax.broadcasted_iota(jnp.int32, (256, 256), 1)
        same = row % 16 == col % 16
        for k, ref in enumerate((base_ref, temp_ref)):
            rows = jnp.dot(spread, ref[...].astype(jnp.bfloat16), preferred_element_type=jnp.float32)
            full = lax.dot_general(
                rows.astype(jnp.bfloat16), spread, (((1,), (1,)), ((), ())), preferred_element_type=jnp.float32
            )
            full = jnp.where(same, full, 0.0).astype(jnp.bfloat16)
            for c in range(0, 16, CHUNK):
                mix[pl.ds(32 * c + 16 * CHUNK * k, 16 * CHUNK), :] = full[16 * c : 16 * (c + CHUNK)]

    for k in range(2):
        wide[k] = wind_ref[0, :, 128 * k : 128 * k + 128].astype(jnp.float32)
    lane = lax.broadcasted_iota(jnp.int32, (16, 128), 1)
    row = lax.broadcasted_iota(jnp.int32, (16, 256), 0)
    limit = jnp.zeros((16, 256), jnp.int32)
    for j in range(16):
        limit = jnp.where(row == j, pts_ref[j], limit)
    column = lax.broadcasted_iota(jnp.int32, (16, 256), 1) + tile * 256
    mask = jnp.where(column < limit, 1.0, 0.0)

    def advect(l, kept, kept_b, tower):
        at = h * 8 + 4 * part + l
        local = 4 * part + l
        u = 0.1 * rows_of(wide, local, 16, 24)
        v = 0.1 * rows_of(wide, 8 + local, 16, 24)
        east_w, west_w = (0.05 - u) * mask, (0.05 + u) * mask
        north_w, south_w = (0.05 - v) * mask, (0.05 + v) * mask
        own_w = 0.8 * mask
        for k in range(2):
            half = slice(128 * k, 128 * k + 128)
            tower[k, pl.ds(0, 16, stride=36), :] = south_ref[l, :, half].astype(jnp.float32)
            tower[k, pl.ds(34, 16, stride=36), :] = north_ref[l, :, half].astype(jnp.float32)
        for t in range(16):
            x = tr_ref[t, l].astype(jnp.float32)
            xl, xr = x[:, :128], x[:, 128:]
            for k, part_x in enumerate((xl, xr)):
                tower[k, pl.ds(36 * t + 2, 16, stride=2), :] = part_x
            he = pltpu.roll(east[pl.ds(16 * t, 16), :], 127 - at, 1)
            hw = pltpu.roll(west[pl.ds(16 * t, 16), :], 64 - at, 1)
            el, er = pltpu.roll(xl, 127, 1), pltpu.roll(xr, 127, 1)
            wl, wr = pltpu.roll(xl, 1, 1), pltpu.roll(xr, 1, 1)
            xe = jnp.concatenate([jnp.where(lane == 127, er, el), jnp.where(lane == 127, he, er)], axis=1)
            xw = jnp.concatenate([jnp.where(lane == 0, hw, wl), jnp.where(lane == 0, wl, wr)], axis=1)
            xn = rows_of(tower, 36 * t + 4, 16, 2)
            xs = rows_of(tower, 36 * t, 16, 2)
            q = own_w * x + east_w * xe + west_w * xw + north_w * xn + south_w * xs
            kept[t] = q
            kept_b[pl.ds(16 * t, 16), :] = q.astype(jnp.bfloat16)

    def settle(l, kept, kept_b):
        temper = rows_of(wide, 16 + 4 * part + l, 16, 24)
        for c in range(0, 16, CHUNK):
            y = jnp.dot(mix[pl.ds(32 * c, 32 * CHUNK), :], kept_b[...], preferred_element_type=jnp.float32)
            for t in range(CHUNK):
                base, heat = y[16 * t : 16 * t + 16], y[16 * (CHUNK + t) : 16 * (CHUNK + t) + 16]
                q = kept[c + t] + base + temper * heat
                kept[c + t] = q
                out_ref[c + t, l] = q.astype(jnp.bfloat16)
        for a in range(4):
            chosen[h, a, 4 * part + l] = kept[ids_ref[a]].astype(jnp.bfloat16)

    def several(i, carry):
        pend = None
        for k in range(UNROLL):
            l = UNROLL * i + k
            now = (l, moved[k % 2], moved_b[k % 2])
            advect(*now, towers[k % 2])
            if pend is not None:
                settle(*pend)
            pend = now
        settle(*pend)
        return carry

    lax.fori_loop(0, levels // UNROLL, several, 0)

    @pl.when(step == 0)
    def _():
        pl.semaphore_wait(barrier, DST - 1)

    @pl.when(step < 14)
    def _():
        send(step).start()

    @pl.when(step == 15)
    def _():
        mine = pltpu.make_async_copy(chosen.at[tile], place, own)
        mine.start()
        mine.wait()
        for d in range(14):
            send(d).wait()


def chemistry(tracers, winds, north, south, east, west, base, temp, ids, points):
    whole = lambda s, i, p: (0, 0)
    hbm = pl.BlockSpec(memory_space=pl.ANY)

    def rows(s, i, p):
        tile, part = tile_of_step(lax.axis_index("lon"), s)
        return (2 * tile + part, 0, 0)

    def cube(s, i, p):
        return (0,) + rows(s, i, p)

    def source(s, i, p):
        return (tile_of_step(lax.axis_index("lon"), s)[0], 0, 0)

    return pl.pallas_call(
        chem_kernel,
        grid_spec=pltpu.PrefetchScalarGridSpec(
            num_scalar_prefetch=2,
            grid=(16,),
            in_specs=[
                pl.BlockSpec((16, 4, 16, 256), cube),
                pl.BlockSpec((1, 384, 256), source),
                pl.BlockSpec((4, 16, 256), rows),
                pl.BlockSpec((4, 16, 256), rows),
                pl.BlockSpec((256, 128), whole),
                pl.BlockSpec((256, 128), whole),
                pl.BlockSpec((16, 16), whole),
                pl.BlockSpec((16, 16), whole),
            ],
            out_specs=[pl.BlockSpec((16, 4, 16, 256), cube), hbm],
            scratch_shapes=[
                pltpu.VMEM((2, 384, 128), jnp.float32),
                pltpu.VMEM((256, 128), jnp.float32),
                pltpu.VMEM((256, 128), jnp.float32),
                pltpu.VMEM((512, 256), jnp.bfloat16),
                pltpu.VMEM((2, 576, 128), jnp.float32),
                pltpu.VMEM((2, 576, 128), jnp.float32),
                pltpu.VMEM((16, 16, 256), jnp.float32),
                pltpu.VMEM((16, 16, 256), jnp.float32),
                pltpu.VMEM((256, 256), jnp.bfloat16),
                pltpu.VMEM((256, 256), jnp.bfloat16),
                pltpu.VMEM((8, 4, 8, 16, 256), jnp.bfloat16),
                pltpu.SemaphoreType.DMA((14,)),
                pltpu.SemaphoreType.DMA((14,)),
                pltpu.SemaphoreType.DMA,
            ],
        ),
        out_shape=[
            jax.ShapeDtypeStruct((16, 64, 16, 256), jnp.bfloat16),
            jax.ShapeDtypeStruct((4, 8, 16, 2048), jnp.bfloat16),
        ],
        compiler_params=pltpu.CompilerParams(collective_id=1, has_side_effects=True),
        name="chemistry",
    )(ids, points, tracers, winds, north, south, east, west, base, temp)


def body(spectral, legendre, wave_ids, points, tracers, react_base, react_temp, active_ids):
    winds, north, south, east, west = winds_of(
        spectral.reshape(48, 40, 1280), legendre, tracers, wave_ids, points
    )
    fresh, active = chemistry(
        tracers, winds, north, south, east, west, react_base, react_temp, active_ids, points
    )
    return (fresh, active.astype(jnp.float32))


def solution(mesh):
    in_specs = (
        P(None, LON, "lat", None),
        P("lat", None, None),
        P(),
        P("lat"),
        P(None, None, "lat", LON),
        P(),
        P(),
        P(),
    )
    out_specs = (P(None, None, "lat", LON), P(None, LON, "lat", None))
    return jax.shard_map(body, mesh=mesh, in_specs=in_specs, out_specs=out_specs, check_vma=False)
```

```python
import functools

import jax
import jax.numpy as jnp
from jax import lax
from jax.experimental import pallas as pl
from jax.experimental.pallas import tpu as pltpu
from jax.sharding import PartitionSpec as P

LON = "lon"


SRC = 16
PLANE = 136
UNROLL = 4
CHUNK = 8
DST = 8
MESH = pl.DeviceIdType.MESH
TILES = ((2, 1), (2, 0), (1, 1), (3, 0), (3, 1), (1, 0), (0, 1))
ORDER = ((2, 0), (0, 1), (2, 1), (1, 0), (3, 1), (1, 1), (3, 0))
BANDS = (
    (1, 2, 0), (1, 2, 1), (0, 1, 0), (1, 0, 0), (0, 3, 1), (1, 1, 0), (0, 2, 0), (1, 3, 1),
    (0, 1, 1), (1, 0, 1), (0, 3, 0), (1, 1, 1), (0, 2, 1), (1, 3, 0), (0, 0, 1),
)
COS = (0.9999992006931535, -19.7389777615569, 64.92855937725766, -85.27036091136767,
       58.78399626476764, -21.059548245283555)
SIN = (6.283184911477688, -41.3415879428884, 81.59989458670537, -76.61384581975258,
       41.339653019987985, -12.465497972860707)


def tile_at(h, dx, dz, back=False):
    dx = (4 - dx) % 4 if back else dx
    return lax.rem(h // 2 + dx, 4) * 2 + lax.rem(lax.rem(h, 2) + dz, 2)


def band_at(g, dz, dy, dc):
    high = lax.rem(g // 8 + dz, 2)
    return high * 8 + lax.rem(lax.rem(g // 2, 4) + dy, 4) * 2 + lax.rem(lax.rem(g, 2) + dc, 2)


def tile_of_step(h, step):
    late = step // 14
    s = lax.rem(step, 7) * (1 - late) + 7 * late
    part = step // 7 - 2 * late + late * lax.rem(step, 2)
    two = (1 + lax.rem(s, 2)) * (1 + 3 * lax.rem(s // 2, 2)) * (1 + 15 * (s // 4))
    code_x = sum(dx * 4**k for k, (dx, dz) in enumerate(ORDER))
    code_z = sum(dz * 2**k for k, (dx, dz) in enumerate(ORDER))
    x = lax.rem(h // 2 + lax.rem(code_x // (two * two), 4), 4)
    return x * 2 + lax.rem(lax.rem(h, 2) + lax.rem(code_z // two, 2), 2), part


def waves_at(product, count, inverse):
    turns = jnp.round(product * inverse)
    t = (product - turns * count) * inverse
    s = t * t
    c = COS[-1]
    for k in COS[-2::-1]:
        c = c * s + k
    d = SIN[-1]
    for k in SIN[-2::-1]:
        d = d * s + k
    return c, d * t


def spectral_kernel(
    spec_ref, leg_ref, tr_ref, ids_ref, pts_ref,
    out_ref, north_ref, south_ref, east_ref, west_ref,
    spec, spread, leg, band, wide_0, wide_1, wide_2, wide_3, cols, low, high, edge, empty, blank_cols,
    rowid, laneid, tall, send_a, got_a, table, phase, coef, line, turned, send_b,
    sent_a, came_a, sent_b, came_b, own, sent_h, came_h, taken, leg_in, band_in,
):
    g, h = lax.axis_index("lat"), lax.axis_index("lon")
    barrier = pltpu.get_barrier_semaphore()
    for d in range(1, SRC):
        pl.semaphore_signal(barrier, inc=1, device_id=(lax.rem(g + d, SRC), h), device_id_type=MESH)
    for d in range(1, DST):
        pl.semaphore_signal(barrier, inc=1, device_id=(g, lax.rem(h + d, DST)), device_id_type=MESH)

    wide = (wide_0, wide_1, wide_2, wide_3)

    def leg_copy(i):
        slot = lax.rem(i, 5)
        return pltpu.make_async_copy(leg_ref.at[pl.ds(5 * i, 5)], leg.at[slot], leg_in.at[slot])

    def band_copy(i):
        slot = lax.rem(i, 2)
        return pltpu.make_async_copy(tr_ref.at[:, pl.ds(8 * i, 8)], band.at[slot], band_in.at[slot])

    spec_copy = pltpu.make_async_copy(spec_ref, spec, taken)
    band_copy(0).start()
    spec_copy.start()
    band_copy(1).start()
    place = lax.broadcasted_iota(jnp.int32, (8, 128), 1)
    for p in range(6):
        at, by = divmod(120 * p, 128)
        ids = jnp.broadcast_to(ids_ref[at : at + 1, :], (8, 128)).astype(jnp.float32)
        if by:
            ids = pltpu.roll(ids, 128 - by, 1)
        if 0 < by and at < 4:
            more = jnp.broadcast_to(ids_ref[at + 1 : at + 2, :], (8, 128)).astype(jnp.float32)
            ids = jnp.where(place < 128 - by, ids, pltpu.roll(more, 128 - by, 1))
        laneid[:, 128 * p : 128 * p + 128] = ids
        rowid[128 * p : 128 * p + 128, :] = jnp.broadcast_to(ids[:1], (128, 128)).T
    tall[...] = jnp.zeros_like(tall)
    empty[...] = jnp.zeros_like(empty)
    blank_cols[...] = jnp.zeros_like(blank_cols)
    cols[...] = jnp.zeros_like(cols)
    lane = lax.broadcasted_iota(jnp.int32, (256, 128), 1)

    shape = (128, 128)

    def tables(j, carry):
        count = jnp.full((1, 1), pts_ref[j], jnp.int32).astype(jnp.float32)
        inverse = 1.0 / count
        far = lax.broadcasted_iota(jnp.int32, (8, 128), 0).astype(jnp.float32) * 256.0
        lane = lax.broadcasted_iota(jnp.int32, shape, 1).astype(jnp.float32)
        for p in range(6):
            ids = laneid[:, pl.ds(128 * p, 128)]
            c, s = waves_at(ids * far, count, inverse)
            phase[j, 0, p] = c
            phase[j, 1, p] = s
        for p in range(6):
            ids = rowid[pl.ds(128 * p, 128), :]
            c, s = waves_at(ids * lane, count, inverse)
            c1 = jnp.broadcast_to(c[:, 64:65], shape)
            s1 = jnp.broadcast_to(s[:, 64:65], shape)
            c1, s1 = c1 * c1 - s1 * s1, 2.0 * c1 * s1
            table[j, pl.ds(128 * p, 128), pl.ds(0, 128)] = c.astype(jnp.bfloat16)
            table[j, pl.ds(768 + 128 * p, 128), pl.ds(0, 128)] = (-s).astype(jnp.bfloat16)
            table[j, pl.ds(128 * p, 128), pl.ds(128, 128)] = (c * c1 - s * s1).astype(jnp.bfloat16)
            table[j, pl.ds(768 + 128 * p, 128), pl.ds(128, 128)] = (-(s * c1 + c * s1)).astype(jnp.bfloat16)
        return carry

    def step(i, carry):
        slot = lax.rem(i, 5)
        leg_copy(i).wait()
        tables(i, 0)
        for w in range(5):
            m = 5 * i + w
            rows = [spread[k, pl.ds(m, 48, stride=40), :].astype(jnp.bfloat16) for k in range(10)]
            value = jnp.dot(jnp.concatenate(rows, axis=1), leg[slot, w], preferred_element_type=jnp.float32)
            for k in range(2):
                for q in range(6):
                    part = value[8 * q : 8 * q + 8, 128 * k : 128 * k + 128]
                    tall[k, pl.ds(20 * q + lax.rem(m, 20), 8, stride=PLANE), :] = part

        @pl.when(i < 3)
        def _():
            leg_copy(i + 5).start()

        return carry

    def edges(i, carry):
        @pl.when(i >= 3)
        def _():
            leg_copy(i - 3).start()

        side = lax.rem(i, 2)
        band_copy(i).wait()

        def level(l, carry):
            kept = cols[...]
            for n in range(4):
                at = 8 * i + 4 * l + n
                x = band[side, :, 4 * l + n].reshape(256, 256).astype(jnp.float32)
                for k in range(2):
                    wide[n][k] = x[:, 128 * k : 128 * k + 128]
                low[at] = rows_of(wide[n], 0, 16, 16).astype(jnp.bfloat16)
                high[at] = rows_of(wide[n], 15, 16, 16).astype(jnp.bfloat16)
                first = pltpu.roll(x[:, :128], at, 1)
                last = pltpu.roll(x[:, 128:], lax.rem(at + 65, 128), 1)
                kept = jnp.where(lane == at, first, jnp.where(lane == at + 64, last, kept))
            cols[...] = kept
            return carry

        lax.fori_loop(0, 2, level, 0)

        @pl.when(i < 6)
        def _():
            band_copy(i + 2).start()

        return carry

    lax.fori_loop(0, 8, edges, 0)
    edge[...] = cols[...].astype(jnp.bfloat16)
    pl.semaphore_wait(barrier, SRC + DST - 2)

    def halo(k, src, dst, lat, lon):
        return pltpu.make_async_remote_copy(
            src_ref=src, dst_ref=dst, send_sem=sent_h.at[k], recv_sem=came_h.at[k],
            device_id=(lat, lon), device_id_type=MESH,
        )

    to_north = halo(0, high, south_ref, lax.rem(g + 1, SRC), h)
    to_south = halo(1, low, north_ref, lax.rem(g + SRC - 1, SRC), h)
    to_east = halo(2, edge, west_ref, g, lax.rem(h + 1, DST))
    to_west = halo(3, edge, east_ref, g, lax.rem(h + DST - 1, DST))
    none_south = pltpu.make_async_copy(empty, south_ref, own.at[5])
    none_north = pltpu.make_async_copy(empty, north_ref, own.at[6])
    none_west = pltpu.make_async_copy(blank_cols, west_ref, own.at[7])
    none_east = pltpu.make_async_copy(blank_cols, east_ref, own.at[8])
    sides = (
        (g < SRC - 1, to_north, g > 0, none_south),
        (g > 0, to_south, g < SRC - 1, none_north),
        (h < DST - 1, to_east, h > 0, none_west),
        (h > 0, to_west, h < DST - 1, none_east),
    )
    for sends, copy, gets, fill in sides:
        pl.when(sends)(copy.start)
        pl.when(jnp.logical_not(gets))(fill.start)

    def turn(half):
        def pair(i, carry):
            for k in range(2):
                blocks = [tall[k, pl.ds(PLANE * (2 * i + n), 128), :].T for n in range(2)]
                for b in range(8):
                    for rows in range(2):
                        at = 16 * b + 8 * rows
                        both = jnp.concatenate([block[at : at + 8] for block in blocks], axis=0)
                        send_a[8 * k + b, half, rows, pl.ds(16 * i, 16), :] = both.astype(jnp.bfloat16)
            return carry

        lax.fori_loop(0, 4, pair, 0)

    def copy_a(d, k):
        to = band_at(g, *BANDS[d - 1])
        src, dst = ((send_a.at[to, 0], got_a.at[g, 0]), (send_a.at[to, 1, 0], got_a.at[g, 1, 0]),
                    (send_a.at[to, 1, 1], got_a.at[g, 1, 1]))[k]
        return pltpu.make_async_remote_copy(
            src_ref=src, dst_ref=dst, send_sem=sent_a.at[k, d], recv_sem=came_a.at[k, d],
            device_id=(to, h), device_id_type=MESH,
        )

    spec_copy.wait()

    def loosen(i, carry):
        for r in range(4):
            for k in range(10):
                part = spec[4 * i + r, :, 128 * k : 128 * k + 128]
                spread[k, pl.ds(160 * i + 40 * r, 40), :] = part.astype(jnp.float32)
        return carry

    lax.fori_loop(0, 12, loosen, 0)
    lax.fori_loop(0, 4, step, 0)
    turn(0)
    for d in range(1, SRC):
        copy_a(d, 0).start()
    lax.fori_loop(4, 8, step, 0)
    turn(1)
    for k in (1, 2):
        for d in range(1, SRC):
            copy_a(d, k).start()
    mine = pltpu.make_async_copy(send_a.at[g], got_a.at[g], own.at[0])
    mine.start()
    lax.fori_loop(8, 12, tables, 0)
    mine.wait()

    def widen(rows):
        def one(q, carry):
            for half in range(2):
                coef[pl.ds(64 * (2 * q + half), 64), :] = got_a[q, half, rows].astype(jnp.float32)
            return carry

        lax.fori_loop(0, SRC, one, 0)

    def turn_of(j):
        lane = lax.broadcasted_iota(jnp.int32, (8, 128), 1)
        row = lax.rem(j, 8)
        for p in range(6):
            count = min(6, 2 * SRC - 6 * p)
            held = [coef[pl.ds(64 * (6 * p + q) + row, 8, stride=8), :] for q in range(count)]
            for f in range(6):
                value = jnp.zeros((8, 128), jnp.float32)
                for q in range(count):
                    moved = held[q] if q == f else pltpu.roll(held[q], (20 * (q - f)) % 128, 1)
                    value = jnp.where((lane >= 20 * q) & (lane < 20 * q + 20), moved, value)
                line[f // 2, f % 2, p] = value
        for p in range(6):
            for a in range(0, DST, 2):
                parts = []
                for b in range(6):
                    row, f = a + b // 3, b % 3
                    c = phase[j, 0, p, row : row + 1, :]
                    s = phase[j, 1, p, row : row + 1, :]
                    re, im = line[f, 0, p], line[f, 1, p]
                    parts.append((re * c - im * s, re * s + im * c))
                for b in range(0, 6, 2):
                    at = 24 * a + 8 * b
                    for k in range(2):
                        pair = jnp.concatenate([parts[b][k], parts[b + 1][k]], axis=0)
                        turned[at : at + 16, 768 * k + 128 * p : 768 * k + 128 * p + 128] = pair.astype(jnp.bfloat16)
        out = jnp.dot(turned[...], table[j], preferred_element_type=jnp.float32)
        return out * (640.0 ** -0.5)

    def copy_b(d, c):
        to = tile_at(h, *TILES[d - 1])
        return pltpu.make_async_remote_copy(
            src_ref=send_b.at[c, to], dst_ref=out_ref.at[h, pl.ds(96 * c, 96), :],
            send_sem=sent_b.at[c, d], recv_sem=came_b.at[c, d], device_id=(g, to), device_id_type=MESH,
        )

    def copy_own(c):
        return pltpu.make_async_copy(send_b.at[c, h], out_ref.at[h, pl.ds(96 * c, 96), :], own.at[1 + c])

    def quad(c, carry):
        for jj in range(2):
            one = turn_of(4 * c + 2 * jj)
            two = turn_of(4 * c + 2 * jj + 1)
            for a in range(DST):
                both = jnp.concatenate([one[24 * a : 24 * a + 24], two[24 * a : 24 * a + 24]], axis=0)
                send_b[c, a, pl.ds(48 * jj, 48), :] = both.astype(jnp.bfloat16)
        for d in range(1, DST):
            copy_b(d, c).start()
        copy_own(c).start()
        return carry

    for rows in range(2):
        for k in ((0, 1), (2,))[rows]:
            for d in range(1, SRC):
                copy_a(d, k).wait_recv()
        widen(rows)
        lax.fori_loop(2 * rows, 2 * rows + 2, quad, 0)
        if rows == 0:
            lax.fori_loop(12, 16, tables, 0)
    for k in range(3):
        for d in range(1, SRC):
            copy_a(d, k).wait_send()

    def finish(c, carry):
        copy_own(c).wait()
        for d in range(1, DST):
            copy_b(d, c).wait()
        return carry

    lax.fori_loop(0, 4, finish, 0)
    for sends, copy, gets, fill in sides:
        pl.when(sends)(copy.wait_send)
        pl.when(gets)(copy.wait_recv)
        pl.when(jnp.logical_not(gets))(fill.wait)


def winds_of(spectral, legendre, tracers, wave_ids, points):
    vmem = pl.BlockSpec(memory_space=pltpu.VMEM)
    hbm = pl.BlockSpec(memory_space=pl.ANY)
    return pl.pallas_call(
        spectral_kernel,
        in_specs=[hbm, hbm, hbm, vmem, pl.BlockSpec(memory_space=pltpu.SMEM)],
        out_specs=[hbm] * 5,
        out_shape=[
            jax.ShapeDtypeStruct((8, 384, 256), jnp.bfloat16),
            jax.ShapeDtypeStruct((64, 16, 256), jnp.bfloat16),
            jax.ShapeDtypeStruct((64, 16, 256), jnp.bfloat16),
            jax.ShapeDtypeStruct((256, 128), jnp.bfloat16),
            jax.ShapeDtypeStruct((256, 128), jnp.bfloat16),
        ],
        scratch_shapes=[
            pltpu.VMEM((48, 40, 1280), jnp.bfloat16),
            pltpu.VMEM((10, 1920, 128), jnp.float32),
            pltpu.VMEM((5, 5, 1280, 256), jnp.bfloat16),
            pltpu.VMEM((2, 16, 8, 16, 256), jnp.bfloat16),
            pltpu.VMEM((2, 256, 128), jnp.float32),
            pltpu.VMEM((2, 256, 128), jnp.float32),
            pltpu.VMEM((2, 256, 128), jnp.float32),
            pltpu.VMEM((2, 256, 128), jnp.float32),
            pltpu.VMEM((256, 128), jnp.float32),
            pltpu.VMEM((64, 16, 256), jnp.bfloat16),
            pltpu.VMEM((64, 16, 256), jnp.bfloat16),
            pltpu.VMEM((256, 128), jnp.bfloat16),
            pltpu.VMEM((64, 16, 256), jnp.bfloat16),
            pltpu.VMEM((256, 128), jnp.bfloat16),
            pltpu.VMEM((768, 128), jnp.float32),
            pltpu.VMEM((8, 768), jnp.float32),
            pltpu.VMEM((2, 8 * PLANE, 128), jnp.float32),
            pltpu.VMEM((16, 2, 2, 64, 128), jnp.bfloat16),
            pltpu.VMEM((16, 2, 2, 64, 128), jnp.bfloat16),
            pltpu.VMEM((16, 1536, 256), jnp.bfloat16),
            pltpu.VMEM((16, 2, 6, 8, 128), jnp.float32),
            pltpu.VMEM((2048, 128), jnp.float32),
            pltpu.VMEM((3, 2, 6, 8, 128), jnp.float32),
            pltpu.VMEM((192, 1536), jnp.bfloat16),
            pltpu.VMEM((4, 8, 96, 256), jnp.bfloat16),
            pltpu.SemaphoreType.DMA((3, 16)),
            pltpu.SemaphoreType.DMA((3, 16)),
            pltpu.SemaphoreType.DMA((4, 8)),
            pltpu.SemaphoreType.DMA((4, 8)),
            pltpu.SemaphoreType.DMA((9,)),
            pltpu.SemaphoreType.DMA((4,)),
            pltpu.SemaphoreType.DMA((4,)),
            pltpu.SemaphoreType.DMA,
            pltpu.SemaphoreType.DMA((5,)),
            pltpu.SemaphoreType.DMA((2,)),
        ],
        compiler_params=pltpu.CompilerParams(
            collective_id=0, has_side_effects=True, vmem_limit_bytes=60 * 1024 * 1024
        ),
        name="winds",
    )(spectral, legendre, tracers, wave_ids.reshape(5, 128), points)


def rows_of(ref, start, size, stride):
    return jnp.concatenate([ref[k, pl.ds(start, size, stride=stride), :] for k in range(2)], axis=1)


def chem_kernel(
    ids_ref, pts_ref, tr_ref, wind_ref, north_ref, south_ref, east_ref, west_ref, base_ref, temp_ref, *rest
):
    out_ref, got_ref, wide, east, west, mix, *kept = rest
    towers, moved, moved_b = kept[:2], kept[2:4], kept[4:6]
    chosen, sent, came, own = kept[6:]
    step = pl.program_id(0)
    g, tile = lax.axis_index("lat"), lax.axis_index("lon")
    h, part = tile_of_step(tile, step)
    levels = out_ref.shape[1]
    barrier = pltpu.get_barrier_semaphore()

    place = got_ref.at[:, :, :, pl.ds(pl.multiple_of(tile * 256, 256), 256)]

    def send(d):
        to, some = tile_of_step(tile, d)
        rows = pl.ds(4 * some, 4)
        return pltpu.make_async_remote_copy(
            src_ref=chosen.at[to, :, rows], dst_ref=place.at[:, rows], send_sem=sent.at[d], recv_sem=came.at[d],
            device_id=(g, to), device_id_type=MESH,
        )

    @pl.when(step == 0)
    def _():
        for d in range(1, DST):
            pl.semaphore_signal(barrier, inc=1, device_id=(g, lax.rem(tile + d, DST)), device_id_type=MESH)
        east[...] = east_ref[...].astype(jnp.float32)
        west[...] = west_ref[...].astype(jnp.float32)
        row = lax.broadcasted_iota(jnp.int32, (256, 16), 0)
        col = lax.broadcasted_iota(jnp.int32, (256, 16), 1)
        spread = jnp.where(row // 16 == col, 1.0, 0.0).astype(jnp.bfloat16)
        row = lax.broadcasted_iota(jnp.int32, (256, 256), 0)
        col = lax.broadcasted_iota(jnp.int32, (256, 256), 1)
        same = row % 16 == col % 16
        for k, ref in enumerate((base_ref, temp_ref)):
            rows = jnp.dot(spread, ref[...].astype(jnp.bfloat16), preferred_element_type=jnp.float32)
            full = lax.dot_general(
                rows.astype(jnp.bfloat16), spread, (((1,), (1,)), ((), ())), preferred_element_type=jnp.float32
            )
            full = jnp.where(same, full, 0.0).astype(jnp.bfloat16)
            for c in range(0, 16, CHUNK):
                mix[pl.ds(32 * c + 16 * CHUNK * k, 16 * CHUNK), :] = full[16 * c : 16 * (c + CHUNK)]

    for k in range(2):
        wide[k] = wind_ref[0, :, 128 * k : 128 * k + 128].astype(jnp.float32)
    lane = lax.broadcasted_iota(jnp.int32, (16, 128), 1)
    row = lax.broadcasted_iota(jnp.int32, (16, 256), 0)
    limit = jnp.zeros((16, 256), jnp.int32)
    for j in range(16):
        limit = jnp.where(row == j, pts_ref[j], limit)
    column = lax.broadcasted_iota(jnp.int32, (16, 256), 1) + tile * 256
    mask = jnp.where(column < limit, 1.0, 0.0)

    def advect(l, kept, kept_b, tower):
        at = h * 8 + 4 * part + l
        local = 4 * part + l
        u = 0.1 * rows_of(wide, local, 16, 24)
        v = 0.1 * rows_of(wide, 8 + local, 16, 24)
        east_w, west_w = (0.05 - u) * mask, (0.05 + u) * mask
        north_w, south_w = (0.05 - v) * mask, (0.05 + v) * mask
        own_w = 0.8 * mask
        for k in range(2):
            half = slice(128 * k, 128 * k + 128)
            tower[k, pl.ds(0, 16, stride=36), :] = south_ref[l, :, half].astype(jnp.float32)
            tower[k, pl.ds(34, 16, stride=36), :] = north_ref[l, :, half].astype(jnp.float32)
        for t in range(16):
            x = tr_ref[t, l].astype(jnp.float32)
            xl, xr = x[:, :128], x[:, 128:]
            for k, part_x in enumerate((xl, xr)):
                tower[k, pl.ds(36 * t + 2, 16, stride=2), :] = part_x
            he = pltpu.roll(east[pl.ds(16 * t, 16), :], 127 - at, 1)
            hw = pltpu.roll(west[pl.ds(16 * t, 16), :], 64 - at, 1)
            el, er = pltpu.roll(xl, 127, 1), pltpu.roll(xr, 127, 1)
            wl, wr = pltpu.roll(xl, 1, 1), pltpu.roll(xr, 1, 1)
            xe = jnp.concatenate([jnp.where(lane == 127, er, el), jnp.where(lane == 127, he, er)], axis=1)
            xw = jnp.concatenate([jnp.where(lane == 0, hw, wl), jnp.where(lane == 0, wl, wr)], axis=1)
            xn = rows_of(tower, 36 * t + 4, 16, 2)
            xs = rows_of(tower, 36 * t, 16, 2)
            q = own_w * x + east_w * xe + west_w * xw + north_w * xn + south_w * xs
            kept[t] = q
            kept_b[pl.ds(16 * t, 16), :] = q.astype(jnp.bfloat16)

    def settle(l, kept, kept_b):
        temper = rows_of(wide, 16 + 4 * part + l, 16, 24)
        for c in range(0, 16, CHUNK):
            y = jnp.dot(mix[pl.ds(32 * c, 32 * CHUNK), :], kept_b[...], preferred_element_type=jnp.float32)
            for t in range(CHUNK):
                base, heat = y[16 * t : 16 * t + 16], y[16 * (CHUNK + t) : 16 * (CHUNK + t) + 16]
                q = kept[c + t] + base + temper * heat
                kept[c + t] = q
                out_ref[c + t, l] = q.astype(jnp.bfloat16)
        for a in range(4):
            chosen[h, a, 4 * part + l] = kept[ids_ref[a]].astype(jnp.bfloat16)

    def several(i, carry):
        pend = None
        for k in range(UNROLL):
            l = UNROLL * i + k
            now = (l, moved[k % 2], moved_b[k % 2])
            advect(*now, towers[k % 2])
            if pend is not None:
                settle(*pend)
            pend = now
        settle(*pend)
        return carry

    lax.fori_loop(0, levels // UNROLL, several, 0)

    @pl.when(step == 0)
    def _():
        pl.semaphore_wait(barrier, DST - 1)

    @pl.when(step < 14)
    def _():
        send(step).start()

    @pl.when(step == 15)
    def _():
        mine = pltpu.make_async_copy(chosen.at[tile], place, own)
        mine.start()
        mine.wait()
        for d in range(14):
            send(d).wait()


def chemistry(tracers, winds, north, south, east, west, base, temp, ids, points):
    whole = lambda s, i, p: (0, 0)
    hbm = pl.BlockSpec(memory_space=pl.ANY)

    def rows(s, i, p):
        tile, part = tile_of_step(lax.axis_index("lon"), s)
        return (2 * tile + part, 0, 0)

    def cube(s, i, p):
        return (0,) + rows(s, i, p)

    def source(s, i, p):
        return (tile_of_step(lax.axis_index("lon"), s)[0], 0, 0)

    return pl.pallas_call(
        chem_kernel,
        grid_spec=pltpu.PrefetchScalarGridSpec(
            num_scalar_prefetch=2,
            grid=(16,),
            in_specs=[
                pl.BlockSpec((16, 4, 16, 256), cube),
                pl.BlockSpec((1, 384, 256), source),
                pl.BlockSpec((4, 16, 256), rows),
                pl.BlockSpec((4, 16, 256), rows),
                pl.BlockSpec((256, 128), whole),
                pl.BlockSpec((256, 128), whole),
                pl.BlockSpec((16, 16), whole),
                pl.BlockSpec((16, 16), whole),
            ],
            out_specs=[pl.BlockSpec((16, 4, 16, 256), cube), hbm],
            scratch_shapes=[
                pltpu.VMEM((2, 384, 128), jnp.float32),
                pltpu.VMEM((256, 128), jnp.float32),
                pltpu.VMEM((256, 128), jnp.float32),
                pltpu.VMEM((512, 256), jnp.bfloat16),
                pltpu.VMEM((2, 576, 128), jnp.float32),
                pltpu.VMEM((2, 576, 128), jnp.float32),
                pltpu.VMEM((16, 16, 256), jnp.float32),
                pltpu.VMEM((16, 16, 256), jnp.float32),
                pltpu.VMEM((256, 256), jnp.bfloat16),
                pltpu.VMEM((256, 256), jnp.bfloat16),
                pltpu.VMEM((8, 4, 8, 16, 256), jnp.bfloat16),
                pltpu.SemaphoreType.DMA((14,)),
                pltpu.SemaphoreType.DMA((14,)),
                pltpu.SemaphoreType.DMA,
            ],
        ),
        out_shape=[
            jax.ShapeDtypeStruct((16, 64, 16, 256), jnp.bfloat16),
            jax.ShapeDtypeStruct((4, 8, 16, 2048), jnp.bfloat16),
        ],
        compiler_params=pltpu.CompilerParams(collective_id=1, has_side_effects=True),
        name="chemistry",
    )(ids, points, tracers, winds, north, south, east, west, base, temp)


def body(spectral, legendre, wave_ids, points, tracers, react_base, react_temp, active_ids):
    winds, north, south, east, west = winds_of(
        spectral.reshape(48, 40, 1280), legendre, tracers, wave_ids, points
    )
    fresh, active = chemistry(
        tracers, winds, north, south, east, west, react_base, react_temp, active_ids, points
    )
    return (fresh, active.astype(jnp.float32))


def solution(mesh):
    in_specs = (
        P(None, LON, "lat", None),
        P("lat", None, None),
        P(),
        P("lat"),
        P(None, None, "lat", LON),
        P(),
        P(),
        P(),
    )
    out_specs = (P(None, None, "lat", LON), P(None, LON, "lat", None))
    return jax.shard_map(body, mesh=mesh, in_specs=in_specs, out_specs=out_specs, check_vma=False)
```

```python
import functools

import jax
import jax.numpy as jnp
from jax import lax
from jax.experimental import pallas as pl
from jax.experimental.pallas import tpu as pltpu
from jax.sharding import PartitionSpec as P

LON = "lon"


SRC = 16
PLANE = 136
UNROLL = 4
CHUNK = 8
DST = 8
MESH = pl.DeviceIdType.MESH
TILES = ((2, 1), (2, 0), (1, 1), (3, 0), (3, 1), (1, 0), (0, 1))
ORDER = ((2, 1), (0, 1), (2, 0), (1, 1), (3, 1), (1, 0), (3, 0))
BANDS = (
    (1, 2, 0), (1, 2, 1), (0, 1, 0), (1, 0, 0), (0, 3, 1), (1, 1, 0), (0, 2, 0), (1, 3, 1),
    (0, 1, 1), (1, 0, 1), (0, 3, 0), (1, 1, 1), (0, 2, 1), (1, 3, 0), (0, 0, 1),
)
COS = (0.9999992006931535, -19.7389777615569, 64.92855937725766, -85.27036091136767,
       58.78399626476764, -21.059548245283555)
SIN = (6.283184911477688, -41.3415879428884, 81.59989458670537, -76.61384581975258,
       41.339653019987985, -12.465497972860707)


def tile_at(h, dx, dz, back=False):
    dx = (4 - dx) % 4 if back else dx
    return lax.rem(h // 2 + dx, 4) * 2 + lax.rem(lax.rem(h, 2) + dz, 2)


def band_at(g, dz, dy, dc):
    high = lax.rem(g // 8 + dz, 2)
    return high * 8 + lax.rem(lax.rem(g // 2, 4) + dy, 4) * 2 + lax.rem(lax.rem(g, 2) + dc, 2)


def tile_of_step(h, s):
    two = (1 + lax.rem(s, 2)) * (1 + 3 * lax.rem(s // 2, 2)) * (1 + 15 * (s // 4))
    code_x = sum(dx * 4**k for k, (dx, dz) in enumerate(ORDER))
    code_z = sum(dz * 2**k for k, (dx, dz) in enumerate(ORDER))
    x = lax.rem(h // 2 + lax.rem(code_x // (two * two), 4), 4)
    return x * 2 + lax.rem(lax.rem(h, 2) + lax.rem(code_z // two, 2), 2)


def waves_at(product, count, inverse):
    turns = jnp.round(product * inverse)
    t = (product - turns * count) * inverse
    s = t * t
    c = COS[-1]
    for k in COS[-2::-1]:
        c = c * s + k
    d = SIN[-1]
    for k in SIN[-2::-1]:
        d = d * s + k
    return c, d * t


def spectral_kernel(
    spec_ref, leg_ref, tr_ref, ids_ref, pts_ref,
    out_ref, north_ref, south_ref, east_ref, west_ref,
    spec, spread, leg, band, wide_0, wide_1, wide_2, wide_3, cols, low, high, edge, empty, blank_cols,
    rowid, laneid, tall, send_a, got_a, table, phase, coef, line, turned, send_b,
    sent_a, came_a, sent_b, came_b, own, sent_h, came_h, taken, leg_in, band_in,
):
    g, h = lax.axis_index("lat"), lax.axis_index("lon")
    barrier = pltpu.get_barrier_semaphore()
    for d in range(1, SRC):
        pl.semaphore_signal(barrier, inc=1, device_id=(lax.rem(g + d, SRC), h), device_id_type=MESH)
    for d in range(1, DST):
        pl.semaphore_signal(barrier, inc=1, device_id=(g, lax.rem(h + d, DST)), device_id_type=MESH)

    wide = (wide_0, wide_1, wide_2, wide_3)

    def leg_copy(i):
        slot = lax.rem(i, 5)
        return pltpu.make_async_copy(leg_ref.at[pl.ds(5 * i, 5)], leg.at[slot], leg_in.at[slot])

    def band_copy(i):
        slot = lax.rem(i, 2)
        return pltpu.make_async_copy(tr_ref.at[:, pl.ds(8 * i, 8)], band.at[slot], band_in.at[slot])

    spec_copy = pltpu.make_async_copy(spec_ref, spec, taken)
    band_copy(0).start()
    spec_copy.start()
    band_copy(1).start()
    place = lax.broadcasted_iota(jnp.int32, (8, 128), 1)
    for p in range(6):
        at, by = divmod(120 * p, 128)
        ids = jnp.broadcast_to(ids_ref[at : at + 1, :], (8, 128)).astype(jnp.float32)
        if by:
            ids = pltpu.roll(ids, 128 - by, 1)
        if 0 < by and at < 4:
            more = jnp.broadcast_to(ids_ref[at + 1 : at + 2, :], (8, 128)).astype(jnp.float32)
            ids = jnp.where(place < 128 - by, ids, pltpu.roll(more, 128 - by, 1))
        laneid[:, 128 * p : 128 * p + 128] = ids
        rowid[128 * p : 128 * p + 128, :] = jnp.broadcast_to(ids[:1], (128, 128)).T
    tall[...] = jnp.zeros_like(tall)
    empty[...] = jnp.zeros_like(empty)
    blank_cols[...] = jnp.zeros_like(blank_cols)
    cols[...] = jnp.zeros_like(cols)
    lane = lax.broadcasted_iota(jnp.int32, (256, 128), 1)

    shape = (128, 128)

    def tables(j, carry):
        count = jnp.full((1, 1), pts_ref[j], jnp.int32).astype(jnp.float32)
        inverse = 1.0 / count
        far = lax.broadcasted_iota(jnp.int32, (8, 128), 0).astype(jnp.float32) * 256.0
        lane = lax.broadcasted_iota(jnp.int32, shape, 1).astype(jnp.float32)
        for p in range(6):
            ids = laneid[:, pl.ds(128 * p, 128)]
            c, s = waves_at(ids * far, count, inverse)
            phase[j, 0, p] = c
            phase[j, 1, p] = s
        for p in range(6):
            ids = rowid[pl.ds(128 * p, 128), :]
            c, s = waves_at(ids * lane, count, inverse)
            c1 = jnp.broadcast_to(c[:, 64:65], shape)
            s1 = jnp.broadcast_to(s[:, 64:65], shape)
            c1, s1 = c1 * c1 - s1 * s1, 2.0 * c1 * s1
            table[j, pl.ds(128 * p, 128), pl.ds(0, 128)] = c.astype(jnp.bfloat16)
            table[j, pl.ds(768 + 128 * p, 128), pl.ds(0, 128)] = (-s).astype(jnp.bfloat16)
            table[j, pl.ds(128 * p, 128), pl.ds(128, 128)] = (c * c1 - s * s1).astype(jnp.bfloat16)
            table[j, pl.ds(768 + 128 * p, 128), pl.ds(128, 128)] = (-(s * c1 + c * s1)).astype(jnp.bfloat16)
        return carry

    def step(i, carry):
        slot = lax.rem(i, 5)
        leg_copy(i).wait()
        tables(i, 0)
        for w in range(5):
            m = 5 * i + w
            rows = [spread[k, pl.ds(m, 48, stride=40), :].astype(jnp.bfloat16) for k in range(10)]
            value = jnp.dot(jnp.concatenate(rows, axis=1), leg[slot, w], preferred_element_type=jnp.float32)
            for k in range(2):
                for q in range(6):
                    part = value[8 * q : 8 * q + 8, 128 * k : 128 * k + 128]
                    tall[k, pl.ds(20 * q + lax.rem(m, 20), 8, stride=PLANE), :] = part

        @pl.when(i < 3)
        def _():
            leg_copy(i + 5).start()

        return carry

    def edges(i, carry):
        @pl.when(i >= 3)
        def _():
            leg_copy(i - 3).start()

        for n in range(3):
            @pl.when(i == 2 * n + 3)
            def _():
                send_rows(n)

        side = lax.rem(i, 2)
        band_copy(i).wait()

        def level(l, carry):
            kept = cols[...]
            for n in range(4):
                at = 8 * i + 4 * l + n
                x = band[side, :, 4 * l + n].reshape(256, 256).astype(jnp.float32)
                for k in range(2):
                    wide[n][k] = x[:, 128 * k : 128 * k + 128]
                low[at] = rows_of(wide[n], 0, 16, 16).astype(jnp.bfloat16)
                high[at] = rows_of(wide[n], 15, 16, 16).astype(jnp.bfloat16)
                first = pltpu.roll(x[:, :128], at, 1)
                last = pltpu.roll(x[:, 128:], lax.rem(at + 65, 128), 1)
                kept = jnp.where(lane == at, first, jnp.where(lane == at + 64, last, kept))
            cols[...] = kept
            return carry

        lax.fori_loop(0, 2, level, 0)

        @pl.when(i < 6)
        def _():
            band_copy(i + 2).start()

        return carry

    def halo(k, src, dst, lat, lon):
        return pltpu.make_async_remote_copy(
            src_ref=src, dst_ref=dst, send_sem=sent_h.at[k], recv_sem=came_h.at[k],
            device_id=(lat, lon), device_id_type=MESH,
        )

    to_east = halo(0, edge, west_ref, g, lax.rem(h + 1, DST))
    to_west = halo(1, edge, east_ref, g, lax.rem(h + DST - 1, DST))

    def to_north(n):
        rows = pl.ds(16 * n, 16)
        return halo(2 + n, high.at[rows], south_ref.at[rows], lax.rem(g + 1, SRC), h)

    def to_south(n):
        rows = pl.ds(16 * n, 16)
        return halo(6 + n, low.at[rows], north_ref.at[rows], lax.rem(g + SRC - 1, SRC), h)

    def send_rows(n):
        @pl.when(g < SRC - 1)
        def _():
            to_north(n).start()

        @pl.when(g > 0)
        def _():
            to_south(n).start()

    none_south = pltpu.make_async_copy(empty, south_ref, own.at[5])
    none_north = pltpu.make_async_copy(empty, north_ref, own.at[6])
    none_west = pltpu.make_async_copy(blank_cols, west_ref, own.at[7])
    none_east = pltpu.make_async_copy(blank_cols, east_ref, own.at[8])
    fills = ((g == 0, none_south), (g == SRC - 1, none_north), (h == 0, none_west), (h == DST - 1, none_east))
    pl.semaphore_wait(barrier, SRC + DST - 2)
    lax.fori_loop(0, 8, edges, 0)
    edge[...] = cols[...].astype(jnp.bfloat16)
    send_rows(3)
    pl.when(h < DST - 1)(to_east.start)
    pl.when(h > 0)(to_west.start)
    for here, fill in fills:
        pl.when(here)(fill.start)

    def turn(half):
        def pair(i, carry):
            for k in range(2):
                blocks = [tall[k, pl.ds(PLANE * (2 * i + n), 128), :].T for n in range(2)]
                for b in range(8):
                    for rows in range(2):
                        at = 16 * b + 8 * rows
                        both = jnp.concatenate([block[at : at + 8] for block in blocks], axis=0)
                        send_a[8 * k + b, half, rows, pl.ds(16 * i, 16), :] = both.astype(jnp.bfloat16)
            return carry

        lax.fori_loop(0, 4, pair, 0)

    def copy_a(d, k):
        to = band_at(g, *BANDS[d - 1])
        src, dst = ((send_a.at[to, 0], got_a.at[g, 0]), (send_a.at[to, 1, 0], got_a.at[g, 1, 0]),
                    (send_a.at[to, 1, 1], got_a.at[g, 1, 1]))[k]
        return pltpu.make_async_remote_copy(
            src_ref=src, dst_ref=dst, send_sem=sent_a.at[k, d], recv_sem=came_a.at[k, d],
            device_id=(to, h), device_id_type=MESH,
        )

    spec_copy.wait()

    def loosen(i, carry):
        for r in range(4):
            for k in range(10):
                part = spec[4 * i + r, :, 128 * k : 128 * k + 128]
                spread[k, pl.ds(160 * i + 40 * r, 40), :] = part.astype(jnp.float32)
        return carry

    lax.fori_loop(0, 12, loosen, 0)
    lax.fori_loop(0, 4, step, 0)
    turn(0)
    for d in range(1, SRC):
        copy_a(d, 0).start()
    lax.fori_loop(4, 8, step, 0)
    turn(1)
    for k in (1, 2):
        for d in range(1, SRC):
            copy_a(d, k).start()
    mine = pltpu.make_async_copy(send_a.at[g], got_a.at[g], own.at[0])
    mine.start()
    lax.fori_loop(8, 12, tables, 0)
    mine.wait()

    def widen(rows):
        def one(q, carry):
            for half in range(2):
                coef[pl.ds(64 * (2 * q + half), 64), :] = got_a[q, half, rows].astype(jnp.float32)
            return carry

        lax.fori_loop(0, SRC, one, 0)

    def turn_of(j):
        lane = lax.broadcasted_iota(jnp.int32, (8, 128), 1)
        row = lax.rem(j, 8)
        for p in range(6):
            count = min(6, 2 * SRC - 6 * p)
            held = [coef[pl.ds(64 * (6 * p + q) + row, 8, stride=8), :] for q in range(count)]
            for f in range(6):
                value = jnp.zeros((8, 128), jnp.float32)
                for q in range(count):
                    moved = held[q] if q == f else pltpu.roll(held[q], (20 * (q - f)) % 128, 1)
                    value = jnp.where((lane >= 20 * q) & (lane < 20 * q + 20), moved, value)
                line[f // 2, f % 2, p] = value
        for p in range(6):
            for a in range(0, DST, 2):
                parts = []
                for b in range(6):
                    row, f = a + b // 3, b % 3
                    c = phase[j, 0, p, row : row + 1, :]
                    s = phase[j, 1, p, row : row + 1, :]
                    re, im = line[f, 0, p], line[f, 1, p]
                    parts.append((re * c - im * s, re * s + im * c))
                for b in range(0, 6, 2):
                    at = 24 * a + 8 * b
                    for k in range(2):
                        pair = jnp.concatenate([parts[b][k], parts[b + 1][k]], axis=0)
                        turned[at : at + 16, 768 * k + 128 * p : 768 * k + 128 * p + 128] = pair.astype(jnp.bfloat16)
        out = jnp.dot(turned[...], table[j], preferred_element_type=jnp.float32)
        return out * (640.0 ** -0.5)

    def copy_b(d, c):
        to = tile_at(h, *TILES[d - 1])
        return pltpu.make_async_remote_copy(
            src_ref=send_b.at[c, to], dst_ref=out_ref.at[h, pl.ds(96 * c, 96), :],
            send_sem=sent_b.at[c, d], recv_sem=came_b.at[c, d], device_id=(g, to), device_id_type=MESH,
        )

    def copy_own(c):
        return pltpu.make_async_copy(send_b.at[c, h], out_ref.at[h, pl.ds(96 * c, 96), :], own.at[1 + c])

    def quad(c, carry):
        for jj in range(2):
            one = turn_of(4 * c + 2 * jj)
            two = turn_of(4 * c + 2 * jj + 1)
            for a in range(DST):
                both = jnp.concatenate([one[24 * a : 24 * a + 24], two[24 * a : 24 * a + 24]], axis=0)
                send_b[c, a, pl.ds(48 * jj, 48), :] = both.astype(jnp.bfloat16)
        for d in range(1, DST):
            copy_b(d, c).start()
        copy_own(c).start()
        return carry

    for rows in range(2):
        for k in ((0, 1), (2,))[rows]:
            for d in range(1, SRC):
                copy_a(d, k).wait_recv()
        widen(rows)
        lax.fori_loop(2 * rows, 2 * rows + 2, quad, 0)
        if rows == 0:
            lax.fori_loop(12, 16, tables, 0)
    for k in range(3):
        for d in range(1, SRC):
            copy_a(d, k).wait_send()

    def finish(c, carry):
        copy_own(c).wait()
        for d in range(1, DST):
            copy_b(d, c).wait()
        return carry

    lax.fori_loop(0, 4, finish, 0)
    pl.when(h < DST - 1)(to_east.wait_send)
    pl.when(h > 0)(to_west.wait_send)
    pl.when(h > 0)(to_east.wait_recv)
    pl.when(h < DST - 1)(to_west.wait_recv)
    for n in range(4):
        pl.when(g < SRC - 1)(to_north(n).wait_send)
        pl.when(g > 0)(to_south(n).wait_send)
        pl.when(g > 0)(to_north(n).wait_recv)
        pl.when(g < SRC - 1)(to_south(n).wait_recv)
    for here, fill in fills:
        pl.when(here)(fill.wait)


def winds_of(spectral, legendre, tracers, wave_ids, points):
    vmem = pl.BlockSpec(memory_space=pltpu.VMEM)
    hbm = pl.BlockSpec(memory_space=pl.ANY)
    return pl.pallas_call(
        spectral_kernel,
        in_specs=[hbm, hbm, hbm, vmem, pl.BlockSpec(memory_space=pltpu.SMEM)],
        out_specs=[hbm] * 5,
        out_shape=[
            jax.ShapeDtypeStruct((8, 384, 256), jnp.bfloat16),
            jax.ShapeDtypeStruct((64, 16, 256), jnp.bfloat16),
            jax.ShapeDtypeStruct((64, 16, 256), jnp.bfloat16),
            jax.ShapeDtypeStruct((256, 128), jnp.bfloat16),
            jax.ShapeDtypeStruct((256, 128), jnp.bfloat16),
        ],
        scratch_shapes=[
            pltpu.VMEM((48, 40, 1280), jnp.bfloat16),
            pltpu.VMEM((10, 1920, 128), jnp.float32),
            pltpu.VMEM((5, 5, 1280, 256), jnp.bfloat16),
            pltpu.VMEM((2, 16, 8, 16, 256), jnp.bfloat16),
            pltpu.VMEM((2, 256, 128), jnp.float32),
            pltpu.VMEM((2, 256, 128), jnp.float32),
            pltpu.VMEM((2, 256, 128), jnp.float32),
            pltpu.VMEM((2, 256, 128), jnp.float32),
            pltpu.VMEM((256, 128), jnp.float32),
            pltpu.VMEM((64, 16, 256), jnp.bfloat16),
            pltpu.VMEM((64, 16, 256), jnp.bfloat16),
            pltpu.VMEM((256, 128), jnp.bfloat16),
            pltpu.VMEM((64, 16, 256), jnp.bfloat16),
            pltpu.VMEM((256, 128), jnp.bfloat16),
            pltpu.VMEM((768, 128), jnp.float32),
            pltpu.VMEM((8, 768), jnp.float32),
            pltpu.VMEM((2, 8 * PLANE, 128), jnp.float32),
            pltpu.VMEM((16, 2, 2, 64, 128), jnp.bfloat16),
            pltpu.VMEM((16, 2, 2, 64, 128), jnp.bfloat16),
            pltpu.VMEM((16, 1536, 256), jnp.bfloat16),
            pltpu.VMEM((16, 2, 6, 8, 128), jnp.float32),
            pltpu.VMEM((2048, 128), jnp.float32),
            pltpu.VMEM((3, 2, 6, 8, 128), jnp.float32),
            pltpu.VMEM((192, 1536), jnp.bfloat16),
            pltpu.VMEM((4, 8, 96, 256), jnp.bfloat16),
            pltpu.SemaphoreType.DMA((3, 16)),
            pltpu.SemaphoreType.DMA((3, 16)),
            pltpu.SemaphoreType.DMA((4, 8)),
            pltpu.SemaphoreType.DMA((4, 8)),
            pltpu.SemaphoreType.DMA((9,)),
            pltpu.SemaphoreType.DMA((10,)),
            pltpu.SemaphoreType.DMA((10,)),
            pltpu.SemaphoreType.DMA,
            pltpu.SemaphoreType.DMA((5,)),
            pltpu.SemaphoreType.DMA((2,)),
        ],
        compiler_params=pltpu.CompilerParams(
            collective_id=0, has_side_effects=True, vmem_limit_bytes=60 * 1024 * 1024
        ),
        name="winds",
    )(spectral, legendre, tracers, wave_ids.reshape(5, 128), points)


def rows_of(ref, start, size, stride):
    return jnp.concatenate([ref[k, pl.ds(start, size, stride=stride), :] for k in range(2)], axis=1)


def chem_kernel(
    ids_ref, pts_ref, tr_ref, wind_ref, north_ref, south_ref, east_ref, west_ref, base_ref, temp_ref, *rest
):
    out_ref, got_ref, wide, east, west, mix, *kept = rest
    towers, moved, moved_b = kept[:2], kept[2:4], kept[4:6]
    chosen, sent, came, own = kept[6:]
    step = pl.program_id(0)
    g, tile = lax.axis_index("lat"), lax.axis_index("lon")
    h = tile_of_step(tile, step)
    levels = out_ref.shape[1]
    barrier = pltpu.get_barrier_semaphore()

    place = got_ref.at[:, :, :, pl.ds(pl.multiple_of(tile * 256, 256), 256)]

    def send(d, half):
        to = tile_of_step(tile, d)
        rows = pl.ds(4 * half, 4)
        return pltpu.make_async_remote_copy(
            src_ref=chosen.at[to, :, rows], dst_ref=place.at[:, rows],
            send_sem=sent.at[d, half], recv_sem=came.at[d, half],
            device_id=(g, to), device_id_type=MESH,
        )

    @pl.when(step == 0)
    def _():
        for d in range(1, DST):
            pl.semaphore_signal(barrier, inc=1, device_id=(g, lax.rem(tile + d, DST)), device_id_type=MESH)
        east[...] = east_ref[...].astype(jnp.float32)
        west[...] = west_ref[...].astype(jnp.float32)
        row = lax.broadcasted_iota(jnp.int32, (256, 16), 0)
        col = lax.broadcasted_iota(jnp.int32, (256, 16), 1)
        spread = jnp.where(row // 16 == col, 1.0, 0.0).astype(jnp.bfloat16)
        row = lax.broadcasted_iota(jnp.int32, (256, 256), 0)
        col = lax.broadcasted_iota(jnp.int32, (256, 256), 1)
        same = row % 16 == col % 16
        for k, ref in enumerate((base_ref, temp_ref)):
            rows = jnp.dot(spread, ref[...].astype(jnp.bfloat16), preferred_element_type=jnp.float32)
            full = lax.dot_general(
                rows.astype(jnp.bfloat16), spread, (((1,), (1,)), ((), ())), preferred_element_type=jnp.float32
            )
            full = jnp.where(same, full, 0.0).astype(jnp.bfloat16)
            for c in range(0, 16, CHUNK):
                mix[pl.ds(32 * c + 16 * CHUNK * k, 16 * CHUNK), :] = full[16 * c : 16 * (c + CHUNK)]

    for k in range(2):
        wide[k] = wind_ref[0, :, 128 * k : 128 * k + 128].astype(jnp.float32)
    lane = lax.broadcasted_iota(jnp.int32, (16, 128), 1)
    row = lax.broadcasted_iota(jnp.int32, (16, 256), 0)
    limit = jnp.zeros((16, 256), jnp.int32)
    for j in range(16):
        limit = jnp.where(row == j, pts_ref[j], limit)
    column = lax.broadcasted_iota(jnp.int32, (16, 256), 1) + tile * 256
    mask = jnp.where(column < limit, 1.0, 0.0)

    def advect(l, kept, kept_b, tower):
        at = h * 8 + l
        local = l
        u = 0.1 * rows_of(wide, local, 16, 24)
        v = 0.1 * rows_of(wide, 8 + local, 16, 24)
        east_w, west_w = (0.05 - u) * mask, (0.05 + u) * mask
        north_w, south_w = (0.05 - v) * mask, (0.05 + v) * mask
        own_w = 0.8 * mask
        for k in range(2):
            half = slice(128 * k, 128 * k + 128)
            tower[k, pl.ds(0, 16, stride=36), :] = south_ref[l, :, half].astype(jnp.float32)
            tower[k, pl.ds(34, 16, stride=36), :] = north_ref[l, :, half].astype(jnp.float32)
        for t in range(16):
            x = tr_ref[t, l].astype(jnp.float32)
            xl, xr = x[:, :128], x[:, 128:]
            for k, part_x in enumerate((xl, xr)):
                tower[k, pl.ds(36 * t + 2, 16, stride=2), :] = part_x
            he = pltpu.roll(east[pl.ds(16 * t, 16), :], 127 - at, 1)
            hw = pltpu.roll(west[pl.ds(16 * t, 16), :], 64 - at, 1)
            el, er = pltpu.roll(xl, 127, 1), pltpu.roll(xr, 127, 1)
            wl, wr = pltpu.roll(xl, 1, 1), pltpu.roll(xr, 1, 1)
            xe = jnp.concatenate([jnp.where(lane == 127, er, el), jnp.where(lane == 127, he, er)], axis=1)
            xw = jnp.concatenate([jnp.where(lane == 0, hw, wl), jnp.where(lane == 0, wl, wr)], axis=1)
            xn = rows_of(tower, 36 * t + 4, 16, 2)
            xs = rows_of(tower, 36 * t, 16, 2)
            q = own_w * x + east_w * xe + west_w * xw + north_w * xn + south_w * xs
            kept[t] = q
            kept_b[pl.ds(16 * t, 16), :] = q.astype(jnp.bfloat16)

    def settle(l, kept, kept_b):
        temper = rows_of(wide, 16 + l, 16, 24)
        for c in range(0, 16, CHUNK):
            y = jnp.dot(mix[pl.ds(32 * c, 32 * CHUNK), :], kept_b[...], preferred_element_type=jnp.float32)
            for t in range(CHUNK):
                base, heat = y[16 * t : 16 * t + 16], y[16 * (CHUNK + t) : 16 * (CHUNK + t) + 16]
                q = kept[c + t] + base + temper * heat
                kept[c + t] = q
                out_ref[c + t, l] = q.astype(jnp.bfloat16)
        for a in range(4):
            chosen[h, a, l] = kept[ids_ref[a]].astype(jnp.bfloat16)

    def several(i, carry):
        pend = None
        for k in range(UNROLL):
            l = UNROLL * i + k
            now = (l, moved[k % 2], moved_b[k % 2])
            advect(*now, towers[k % 2])
            if pend is not None:
                settle(*pend)
            pend = now
        settle(*pend)

        @pl.when(step + i == 0)
        def _():
            pl.semaphore_wait(barrier, DST - 1)

        @pl.when(step < DST - 1)
        def _():
            send(step, i).start()

        return carry

    lax.fori_loop(0, levels // UNROLL, several, 0)

    @pl.when(step == DST - 1)
    def _():
        mine = pltpu.make_async_copy(chosen.at[tile], place, own)
        mine.start()
        mine.wait()
        for d in range(DST - 1):
            for half in range(2):
                send(d, half).wait()


def chemistry(tracers, winds, north, south, east, west, base, temp, ids, points):
    whole = lambda s, i, p: (0, 0)
    hbm = pl.BlockSpec(memory_space=pl.ANY)

    def rows(s, i, p):
        return (tile_of_step(lax.axis_index("lon"), s), 0, 0)

    def cube(s, i, p):
        return (0,) + rows(s, i, p)

    return pl.pallas_call(
        chem_kernel,
        grid_spec=pltpu.PrefetchScalarGridSpec(
            num_scalar_prefetch=2,
            grid=(8,),
            in_specs=[
                pl.BlockSpec((16, 8, 16, 256), cube),
                pl.BlockSpec((1, 384, 256), rows),
                pl.BlockSpec((8, 16, 256), rows),
                pl.BlockSpec((8, 16, 256), rows),
                pl.BlockSpec((256, 128), whole),
                pl.BlockSpec((256, 128), whole),
                pl.BlockSpec((16, 16), whole),
                pl.BlockSpec((16, 16), whole),
            ],
            out_specs=[pl.BlockSpec((16, 8, 16, 256), cube), hbm],
            scratch_shapes=[
                pltpu.VMEM((2, 384, 128), jnp.float32),
                pltpu.VMEM((256, 128), jnp.float32),
                pltpu.VMEM((256, 128), jnp.float32),
                pltpu.VMEM((512, 256), jnp.bfloat16),
                pltpu.VMEM((2, 576, 128), jnp.float32),
                pltpu.VMEM((2, 576, 128), jnp.float32),
                pltpu.VMEM((16, 16, 256), jnp.float32),
                pltpu.VMEM((16, 16, 256), jnp.float32),
                pltpu.VMEM((256, 256), jnp.bfloat16),
                pltpu.VMEM((256, 256), jnp.bfloat16),
                pltpu.VMEM((8, 4, 8, 16, 256), jnp.bfloat16),
                pltpu.SemaphoreType.DMA((7, 2)),
                pltpu.SemaphoreType.DMA((7, 2)),
                pltpu.SemaphoreType.DMA,
            ],
        ),
        out_shape=[
            jax.ShapeDtypeStruct((16, 64, 16, 256), jnp.bfloat16),
            jax.ShapeDtypeStruct((4, 8, 16, 2048), jnp.bfloat16),
        ],
        compiler_params=pltpu.CompilerParams(collective_id=1, has_side_effects=True),
        name="chemistry",
    )(ids, points, tracers, winds, north, south, east, west, base, temp)


def body(spectral, legendre, wave_ids, points, tracers, react_base, react_temp, active_ids):
    winds, north, south, east, west = winds_of(
        spectral.reshape(48, 40, 1280), legendre, tracers, wave_ids, points
    )
    fresh, active = chemistry(
        tracers, winds, north, south, east, west, react_base, react_temp, active_ids, points
    )
    return (fresh, active.astype(jnp.float32))


def solution(mesh):
    in_specs = (
        P(None, LON, "lat", None),
        P("lat", None, None),
        P(),
        P("lat"),
        P(None, None, "lat", LON),
        P(),
        P(),
        P(),
    )
    out_specs = (P(None, None, "lat", LON), P(None, LON, "lat", None))
    return jax.shard_map(body, mesh=mesh, in_specs=in_specs, out_specs=out_specs, check_vma=False)
```

```python
import functools

import jax
import jax.numpy as jnp
from jax import lax
from jax.experimental import pallas as pl
from jax.experimental.pallas import tpu as pltpu
from jax.sharding import PartitionSpec as P

LON = "lon"


SRC = 16
PLANE = 136
UNROLL = 4
CHUNK = 8
DST = 8
MESH = pl.DeviceIdType.MESH
TILES = ((2, 1), (2, 0), (1, 1), (3, 0), (3, 1), (1, 0), (0, 1))
ORDER = ((2, 1), (0, 1), (2, 0), (1, 1), (3, 1), (1, 0), (3, 0))
BANDS = tuple((dz, dy, dc) for dz in (1, 0) for dy in (2, 1, 3, 0) for dc in (0, 1) if dz + dy + dc)
COS = (0.9999992006931535, -19.7389777615569, 64.92855937725766, -85.27036091136767,
       58.78399626476764, -21.059548245283555)
SIN = (6.283184911477688, -41.3415879428884, 81.59989458670537, -76.61384581975258,
       41.339653019987985, -12.465497972860707)


def tile_at(h, dx, dz, back=False):
    dx = (4 - dx) % 4 if back else dx
    return lax.rem(h // 2 + dx, 4) * 2 + lax.rem(lax.rem(h, 2) + dz, 2)


def band_at(g, dz, dy, dc):
    high = lax.rem(g // 8 + dz, 2)
    return high * 8 + lax.rem(lax.rem(g // 2, 4) + dy, 4) * 2 + lax.rem(lax.rem(g, 2) + dc, 2)


def tile_of_step(h, step):
    late = step // 14
    s = lax.rem(step, 7) * (1 - late) + 7 * late
    part = step // 7 - 2 * late + late * lax.rem(step, 2)
    two = (1 + lax.rem(s, 2)) * (1 + 3 * lax.rem(s // 2, 2)) * (1 + 15 * (s // 4))
    code_x = sum(dx * 4**k for k, (dx, dz) in enumerate(ORDER))
    code_z = sum(dz * 2**k for k, (dx, dz) in enumerate(ORDER))
    x = lax.rem(h // 2 + lax.rem(code_x // (two * two), 4), 4)
    return x * 2 + lax.rem(lax.rem(h, 2) + lax.rem(code_z // two, 2), 2), part


def waves_at(product, count, inverse):
    turns = jnp.round(product * inverse)
    t = (product - turns * count) * inverse
    s = t * t
    c = COS[-1]
    for k in COS[-2::-1]:
        c = c * s + k
    d = SIN[-1]
    for k in SIN[-2::-1]:
        d = d * s + k
    return c, d * t


def spectral_kernel(
    spec_ref, leg_ref, tr_ref, ids_ref, pts_ref,
    out_ref, north_ref, south_ref, east_ref, west_ref,
    spec, spread, leg, band, wide_0, wide_1, wide_2, wide_3, cols, low, high, edge, empty, blank_cols,
    rowid, laneid, tall, send_a, got_a, table, phase, coef, line, turned, send_b,
    sent_a, came_a, sent_b, came_b, own, sent_h, came_h, taken, leg_in, band_in,
):
    g, h = lax.axis_index("lat"), lax.axis_index("lon")
    barrier = pltpu.get_barrier_semaphore()
    for d in range(1, SRC):
        pl.semaphore_signal(barrier, inc=1, device_id=(lax.rem(g + d, SRC), h), device_id_type=MESH)
    for d in range(1, DST):
        pl.semaphore_signal(barrier, inc=1, device_id=(g, lax.rem(h + d, DST)), device_id_type=MESH)

    wide = (wide_0, wide_1, wide_2, wide_3)

    def leg_copy(i):
        slot = lax.rem(i, 5)
        return pltpu.make_async_copy(leg_ref.at[pl.ds(5 * i, 5)], leg.at[slot], leg_in.at[slot])

    def band_copy(i):
        slot = lax.rem(i, 2)
        return pltpu.make_async_copy(tr_ref.at[:, pl.ds(8 * i, 8)], band.at[slot], band_in.at[slot])

    spec_copy = pltpu.make_async_copy(spec_ref, spec, taken)
    band_copy(0).start()
    spec_copy.start()
    band_copy(1).start()
    place = lax.broadcasted_iota(jnp.int32, (8, 128), 1)
    for p in range(6):
        at, by = divmod(120 * p, 128)
        ids = jnp.broadcast_to(ids_ref[at : at + 1, :], (8, 128)).astype(jnp.float32)
        if by:
            ids = pltpu.roll(ids, 128 - by, 1)
        if 0 < by and at < 4:
            more = jnp.broadcast_to(ids_ref[at + 1 : at + 2, :], (8, 128)).astype(jnp.float32)
            ids = jnp.where(place < 128 - by, ids, pltpu.roll(more, 128 - by, 1))
        laneid[:, 128 * p : 128 * p + 128] = ids
        rowid[128 * p : 128 * p + 128, :] = jnp.broadcast_to(ids[:1], (128, 128)).T
    tall[...] = jnp.zeros_like(tall)
    empty[...] = jnp.zeros_like(empty)
    blank_cols[...] = jnp.zeros_like(blank_cols)
    cols[...] = jnp.zeros_like(cols)
    lane = lax.broadcasted_iota(jnp.int32, (256, 128), 1)

    shape = (128, 128)

    def tables(j, carry):
        count = jnp.full((1, 1), pts_ref[j], jnp.int32).astype(jnp.float32)
        inverse = 1.0 / count
        far = lax.broadcasted_iota(jnp.int32, (8, 128), 0).astype(jnp.float32) * 256.0
        lane = lax.broadcasted_iota(jnp.int32, shape, 1).astype(jnp.float32)
        for p in range(6):
            ids = laneid[:, pl.ds(128 * p, 128)]
            c, s = waves_at(ids * far, count, inverse)
            phase[j, 0, p] = c
            phase[j, 1, p] = s
        for p in range(6):
            ids = rowid[pl.ds(128 * p, 128), :]
            c, s = waves_at(ids * lane, count, inverse)
            c1 = jnp.broadcast_to(c[:, 64:65], shape)
            s1 = jnp.broadcast_to(s[:, 64:65], shape)
            c1, s1 = c1 * c1 - s1 * s1, 2.0 * c1 * s1
            table[j, pl.ds(128 * p, 128), pl.ds(0, 128)] = c.astype(jnp.bfloat16)
            table[j, pl.ds(768 + 128 * p, 128), pl.ds(0, 128)] = (-s).astype(jnp.bfloat16)
            table[j, pl.ds(128 * p, 128), pl.ds(128, 128)] = (c * c1 - s * s1).astype(jnp.bfloat16)
            table[j, pl.ds(768 + 128 * p, 128), pl.ds(128, 128)] = (-(s * c1 + c * s1)).astype(jnp.bfloat16)
        return carry

    def step(i, carry):
        slot = lax.rem(i, 5)
        leg_copy(i).wait()
        tables(i, 0)
        for w in range(5):
            m = 5 * i + w
            rows = [spread[k, pl.ds(m, 48, stride=40), :].astype(jnp.bfloat16) for k in range(10)]
            value = jnp.dot(jnp.concatenate(rows, axis=1), leg[slot, w], preferred_element_type=jnp.float32)
            for k in range(2):
                for q in range(6):
                    part = value[8 * q : 8 * q + 8, 128 * k : 128 * k + 128]
                    tall[k, pl.ds(20 * q + lax.rem(m, 20), 8, stride=PLANE), :] = part

        @pl.when(i < 3)
        def _():
            leg_copy(i + 5).start()

        return carry

    def edges(i, carry):
        @pl.when(i >= 3)
        def _():
            leg_copy(i - 3).start()

        for n in range(3):
            @pl.when(i == 2 * n + 3)
            def _():
                send_rows(n)

        side = lax.rem(i, 2)
        band_copy(i).wait()

        def level(l, carry):
            kept = cols[...]
            for n in range(4):
                at = 8 * i + 4 * l + n
                x = band[side, :, 4 * l + n].reshape(256, 256).astype(jnp.float32)
                for k in range(2):
                    wide[n][k] = x[:, 128 * k : 128 * k + 128]
                low[at] = rows_of(wide[n], 0, 16, 16).astype(jnp.bfloat16)
                high[at] = rows_of(wide[n], 15, 16, 16).astype(jnp.bfloat16)
                first = pltpu.roll(x[:, :128], at, 1)
                last = pltpu.roll(x[:, 128:], lax.rem(at + 65, 128), 1)
                kept = jnp.where(lane == at, first, jnp.where(lane == at + 64, last, kept))
            cols[...] = kept
            return carry

        lax.fori_loop(0, 2, level, 0)

        @pl.when(i < 6)
        def _():
            band_copy(i + 2).start()

        return carry

    def halo(k, src, dst, lat, lon):
        return pltpu.make_async_remote_copy(
            src_ref=src, dst_ref=dst, send_sem=sent_h.at[k], recv_sem=came_h.at[k],
            device_id=(lat, lon), device_id_type=MESH,
        )

    to_east = halo(0, edge, west_ref, g, lax.rem(h + 1, DST))
    to_west = halo(1, edge, east_ref, g, lax.rem(h + DST - 1, DST))

    def to_north(n):
        rows = pl.ds(16 * n, 16)
        return halo(2 + n, high.at[rows], south_ref.at[rows], lax.rem(g + 1, SRC), h)

    def to_south(n):
        rows = pl.ds(16 * n, 16)
        return halo(6 + n, low.at[rows], north_ref.at[rows], lax.rem(g + SRC - 1, SRC), h)

    def send_rows(n):
        @pl.when(g < SRC - 1)
        def _():
            to_north(n).start()

        @pl.when(g > 0)
        def _():
            to_south(n).start()

    none_south = pltpu.make_async_copy(empty, south_ref, own.at[5])
    none_north = pltpu.make_async_copy(empty, north_ref, own.at[6])
    none_west = pltpu.make_async_copy(blank_cols, west_ref, own.at[7])
    none_east = pltpu.make_async_copy(blank_cols, east_ref, own.at[8])
    fills = ((g == 0, none_south), (g == SRC - 1, none_north), (h == 0, none_west), (h == DST - 1, none_east))
    pl.semaphore_wait(barrier, SRC + DST - 2)
    lax.fori_loop(0, 8, edges, 0)
    edge[...] = cols[...].astype(jnp.bfloat16)
    send_rows(3)
    pl.when(h < DST - 1)(to_east.start)
    pl.when(h > 0)(to_west.start)
    for here, fill in fills:
        pl.when(here)(fill.start)

    def turn(half):
        def pair(i, carry):
            for k in range(2):
                blocks = [tall[k, pl.ds(PLANE * (2 * i + n), 128), :].T for n in range(2)]
                for b in range(8):
                    for rows in range(2):
                        at = 16 * b + 8 * rows
                        both = jnp.concatenate([block[at : at + 8] for block in blocks], axis=0)
                        send_a[8 * k + b, half, rows, pl.ds(16 * i, 16), :] = both.astype(jnp.bfloat16)
            return carry

        lax.fori_loop(0, 4, pair, 0)

    def copy_a(d, k):
        to = band_at(g, *BANDS[d - 1])
        src, dst = ((send_a.at[to, 0], got_a.at[g, 0]), (send_a.at[to, 1, 0], got_a.at[g, 1, 0]),
                    (send_a.at[to, 1, 1], got_a.at[g, 1, 1]))[k]
        return pltpu.make_async_remote_copy(
            src_ref=src, dst_ref=dst, send_sem=sent_a.at[k, d], recv_sem=came_a.at[k, d],
            device_id=(to, h), device_id_type=MESH,
        )

    spec_copy.wait()

    def loosen(i, carry):
        for r in range(4):
            for k in range(10):
                part = spec[4 * i + r, :, 128 * k : 128 * k + 128]
                spread[k, pl.ds(160 * i + 40 * r, 40), :] = part.astype(jnp.float32)
        return carry

    lax.fori_loop(0, 12, loosen, 0)
    lax.fori_loop(0, 4, step, 0)
    turn(0)
    for d in range(1, SRC):
        copy_a(d, 0).start()
    lax.fori_loop(4, 8, step, 0)
    turn(1)
    for k in (1, 2):
        for d in range(1, SRC):
            copy_a(d, k).start()
    mine = pltpu.make_async_copy(send_a.at[g], got_a.at[g], own.at[0])
    mine.start()
    lax.fori_loop(8, 12, tables, 0)
    mine.wait()

    def widen(rows):
        def one(q, carry):
            for half in range(2):
                coef[pl.ds(64 * (2 * q + half), 64), :] = got_a[q, half, rows].astype(jnp.float32)
            return carry

        lax.fori_loop(0, SRC, one, 0)

    def turn_of(j):
        lane = lax.broadcasted_iota(jnp.int32, (8, 128), 1)
        row = lax.rem(j, 8)
        for p in range(6):
            count = min(6, 2 * SRC - 6 * p)
            held = [coef[pl.ds(64 * (6 * p + q) + row, 8, stride=8), :] for q in range(count)]
            for f in range(6):
                value = jnp.zeros((8, 128), jnp.float32)
                for q in range(count):
                    moved = held[q] if q == f else pltpu.roll(held[q], (20 * (q - f)) % 128, 1)
                    value = jnp.where((lane >= 20 * q) & (lane < 20 * q + 20), moved, value)
                line[f // 2, f % 2, p] = value
        for p in range(6):
            for a in range(0, DST, 2):
                parts = []
                for b in range(6):
                    row, f = a + b // 3, b % 3
                    c = phase[j, 0, p, row : row + 1, :]
                    s = phase[j, 1, p, row : row + 1, :]
                    re, im = line[f, 0, p], line[f, 1, p]
                    parts.append((re * c - im * s, re * s + im * c))
                for b in range(0, 6, 2):
                    at = 24 * a + 8 * b
                    for k in range(2):
                        pair = jnp.concatenate([parts[b][k], parts[b + 1][k]], axis=0)
                        turned[at : at + 16, 768 * k + 128 * p : 768 * k + 128 * p + 128] = pair.astype(jnp.bfloat16)
        out = jnp.dot(turned[...], table[j], preferred_element_type=jnp.float32)
        return out * (640.0 ** -0.5)

    def copy_b(d, c):
        to = tile_at(h, *TILES[d - 1])
        return pltpu.make_async_remote_copy(
            src_ref=send_b.at[c, to], dst_ref=out_ref.at[h, pl.ds(96 * c, 96), :],
            send_sem=sent_b.at[c, d], recv_sem=came_b.at[c, d], device_id=(g, to), device_id_type=MESH,
        )

    def copy_own(c):
        return pltpu.make_async_copy(send_b.at[c, h], out_ref.at[h, pl.ds(96 * c, 96), :], own.at[1 + c])

    def quad(c, carry):
        for jj in range(2):
            one = turn_of(4 * c + 2 * jj)
            two = turn_of(4 * c + 2 * jj + 1)
            for a in range(DST):
                both = jnp.concatenate([one[24 * a : 24 * a + 24], two[24 * a : 24 * a + 24]], axis=0)
                send_b[c, a, pl.ds(48 * jj, 48), :] = both.astype(jnp.bfloat16)
        for d in range(1, DST):
            copy_b(d, c).start()
        copy_own(c).start()
        return carry

    for rows in range(2):
        for k in ((0, 1), (2,))[rows]:
            for d in range(1, SRC):
                copy_a(d, k).wait_recv()
        widen(rows)
        lax.fori_loop(2 * rows, 2 * rows + 2, quad, 0)
        if rows == 0:
            lax.fori_loop(12, 16, tables, 0)
    for k in range(3):
        for d in range(1, SRC):
            copy_a(d, k).wait_send()

    def finish(c, carry):
        copy_own(c).wait()
        for d in range(1, DST):
            copy_b(d, c).wait()
        return carry

    lax.fori_loop(0, 4, finish, 0)
    pl.when(h < DST - 1)(to_east.wait_send)
    pl.when(h > 0)(to_west.wait_send)
    pl.when(h > 0)(to_east.wait_recv)
    pl.when(h < DST - 1)(to_west.wait_recv)
    for n in range(4):
        pl.when(g < SRC - 1)(to_north(n).wait_send)
        pl.when(g > 0)(to_south(n).wait_send)
        pl.when(g > 0)(to_north(n).wait_recv)
        pl.when(g < SRC - 1)(to_south(n).wait_recv)
    for here, fill in fills:
        pl.when(here)(fill.wait)


def winds_of(spectral, legendre, tracers, wave_ids, points):
    vmem = pl.BlockSpec(memory_space=pltpu.VMEM)
    hbm = pl.BlockSpec(memory_space=pl.ANY)
    return pl.pallas_call(
        spectral_kernel,
        in_specs=[hbm, hbm, hbm, vmem, pl.BlockSpec(memory_space=pltpu.SMEM)],
        out_specs=[hbm] * 5,
        out_shape=[
            jax.ShapeDtypeStruct((8, 384, 256), jnp.bfloat16),
            jax.ShapeDtypeStruct((64, 16, 256), jnp.bfloat16),
            jax.ShapeDtypeStruct((64, 16, 256), jnp.bfloat16),
            jax.ShapeDtypeStruct((256, 128), jnp.bfloat16),
            jax.ShapeDtypeStruct((256, 128), jnp.bfloat16),
        ],
        scratch_shapes=[
            pltpu.VMEM((48, 40, 1280), jnp.bfloat16),
            pltpu.VMEM((10, 1920, 128), jnp.float32),
            pltpu.VMEM((5, 5, 1280, 256), jnp.bfloat16),
            pltpu.VMEM((2, 16, 8, 16, 256), jnp.bfloat16),
            pltpu.VMEM((2, 256, 128), jnp.float32),
            pltpu.VMEM((2, 256, 128), jnp.float32),
            pltpu.VMEM((2, 256, 128), jnp.float32),
            pltpu.VMEM((2, 256, 128), jnp.float32),
            pltpu.VMEM((256, 128), jnp.float32),
            pltpu.VMEM((64, 16, 256), jnp.bfloat16),
            pltpu.VMEM((64, 16, 256), jnp.bfloat16),
            pltpu.VMEM((256, 128), jnp.bfloat16),
            pltpu.VMEM((64, 16, 256), jnp.bfloat16),
            pltpu.VMEM((256, 128), jnp.bfloat16),
            pltpu.VMEM((768, 128), jnp.float32),
            pltpu.VMEM((8, 768), jnp.float32),
            pltpu.VMEM((2, 8 * PLANE, 128), jnp.float32),
            pltpu.VMEM((16, 2, 2, 64, 128), jnp.bfloat16),
            pltpu.VMEM((16, 2, 2, 64, 128), jnp.bfloat16),
            pltpu.VMEM((16, 1536, 256), jnp.bfloat16),
            pltpu.VMEM((16, 2, 6, 8, 128), jnp.float32),
            pltpu.VMEM((2048, 128), jnp.float32),
            pltpu.VMEM((3, 2, 6, 8, 128), jnp.float32),
            pltpu.VMEM((192, 1536), jnp.bfloat16),
            pltpu.VMEM((4, 8, 96, 256), jnp.bfloat16),
            pltpu.SemaphoreType.DMA((3, 16)),
            pltpu.SemaphoreType.DMA((3, 16)),
            pltpu.SemaphoreType.DMA((4, 8)),
            pltpu.SemaphoreType.DMA((4, 8)),
            pltpu.SemaphoreType.DMA((9,)),
            pltpu.SemaphoreType.DMA((10,)),
            pltpu.SemaphoreType.DMA((10,)),
            pltpu.SemaphoreType.DMA,
            pltpu.SemaphoreType.DMA((5,)),
            pltpu.SemaphoreType.DMA((2,)),
        ],
        compiler_params=pltpu.CompilerParams(
            collective_id=0, has_side_effects=True, vmem_limit_bytes=60 * 1024 * 1024
        ),
        name="winds",
    )(spectral, legendre, tracers, wave_ids.reshape(5, 128), points)


def rows_of(ref, start, size, stride):
    return jnp.concatenate([ref[k, pl.ds(start, size, stride=stride), :] for k in range(2)], axis=1)


def chem_kernel(
    ids_ref, pts_ref, tr_ref, wind_ref, north_ref, south_ref, east_ref, west_ref, base_ref, temp_ref, *rest
):
    out_ref, got_ref, wide, east, west, mix, *kept = rest
    towers, moved, moved_b = kept[:2], kept[2:4], kept[4:6]
    chosen, sent, came, own = kept[6:]
    step = pl.program_id(0)
    g, tile = lax.axis_index("lat"), lax.axis_index("lon")
    h, part = tile_of_step(tile, step)
    levels = out_ref.shape[1]
    barrier = pltpu.get_barrier_semaphore()

    place = got_ref.at[:, :, :, pl.ds(pl.multiple_of(tile * 256, 256), 256)]

    def send(d):
        to, some = tile_of_step(tile, d)
        rows = pl.ds(4 * some, 4)
        return pltpu.make_async_remote_copy(
            src_ref=chosen.at[to, :, rows], dst_ref=place.at[:, rows], send_sem=sent.at[d], recv_sem=came.at[d],
            device_id=(g, to), device_id_type=MESH,
        )

    @pl.when(step == 0)
    def _():
        for d in range(1, DST):
            pl.semaphore_signal(barrier, inc=1, device_id=(g, lax.rem(tile + d, DST)), device_id_type=MESH)
        east[...] = east_ref[...].astype(jnp.float32)
        west[...] = west_ref[...].astype(jnp.float32)
        row = lax.broadcasted_iota(jnp.int32, (256, 16), 0)
        col = lax.broadcasted_iota(jnp.int32, (256, 16), 1)
        spread = jnp.where(row // 16 == col, 1.0, 0.0).astype(jnp.bfloat16)
        row = lax.broadcasted_iota(jnp.int32, (256, 256), 0)
        col = lax.broadcasted_iota(jnp.int32, (256, 256), 1)
        same = row % 16 == col % 16
        for k, ref in enumerate((base_ref, temp_ref)):
            rows = jnp.dot(spread, ref[...].astype(jnp.bfloat16), preferred_element_type=jnp.float32)
            full = lax.dot_general(
                rows.astype(jnp.bfloat16), spread, (((1,), (1,)), ((), ())), preferred_element_type=jnp.float32
            )
            full = jnp.where(same, full, 0.0).astype(jnp.bfloat16)
            for c in range(0, 16, CHUNK):
                mix[pl.ds(32 * c + 16 * CHUNK * k, 16 * CHUNK), :] = full[16 * c : 16 * (c + CHUNK)]

    for k in range(2):
        wide[k] = wind_ref[0, :, 128 * k : 128 * k + 128].astype(jnp.float32)
    lane = lax.broadcasted_iota(jnp.int32, (16, 128), 1)
    row = lax.broadcasted_iota(jnp.int32, (16, 256), 0)
    limit = jnp.zeros((16, 256), jnp.int32)
    for j in range(16):
        limit = jnp.where(row == j, pts_ref[j], limit)
    column = lax.broadcasted_iota(jnp.int32, (16, 256), 1) + tile * 256
    mask = jnp.where(column < limit, 1.0, 0.0)

    def advect(l, kept, kept_b, tower):
        at = h * 8 + 4 * part + l
        local = 4 * part + l
        u = 0.1 * rows_of(wide, local, 16, 24)
        v = 0.1 * rows_of(wide, 8 + local, 16, 24)
        east_w, west_w = (0.05 - u) * mask, (0.05 + u) * mask
        north_w, south_w = (0.05 - v) * mask, (0.05 + v) * mask
        own_w = 0.8 * mask
        for k in range(2):
            half = slice(128 * k, 128 * k + 128)
            tower[k, pl.ds(0, 16, stride=36), :] = south_ref[l, :, half].astype(jnp.float32)
            tower[k, pl.ds(34, 16, stride=36), :] = north_ref[l, :, half].astype(jnp.float32)
        for t in range(16):
            x = tr_ref[t, l].astype(jnp.float32)
            xl, xr = x[:, :128], x[:, 128:]
            for k, part_x in enumerate((xl, xr)):
                tower[k, pl.ds(36 * t + 2, 16, stride=2), :] = part_x
            he = pltpu.roll(east[pl.ds(16 * t, 16), :], 127 - at, 1)
            hw = pltpu.roll(west[pl.ds(16 * t, 16), :], 64 - at, 1)
            el, er = pltpu.roll(xl, 127, 1), pltpu.roll(xr, 127, 1)
            wl, wr = pltpu.roll(xl, 1, 1), pltpu.roll(xr, 1, 1)
            xe = jnp.concatenate([jnp.where(lane == 127, er, el), jnp.where(lane == 127, he, er)], axis=1)
            xw = jnp.concatenate([jnp.where(lane == 0, hw, wl), jnp.where(lane == 0, wl, wr)], axis=1)
            xn = rows_of(tower, 36 * t + 4, 16, 2)
            xs = rows_of(tower, 36 * t, 16, 2)
            q = own_w * x + east_w * xe + west_w * xw + north_w * xn + south_w * xs
            kept[t] = q
            kept_b[pl.ds(16 * t, 16), :] = q.astype(jnp.bfloat16)

    def settle(l, kept, kept_b):
        temper = rows_of(wide, 16 + 4 * part + l, 16, 24)
        for c in range(0, 16, CHUNK):
            y = jnp.dot(mix[pl.ds(32 * c, 32 * CHUNK), :], kept_b[...], preferred_element_type=jnp.float32)
            for t in range(CHUNK):
                base, heat = y[16 * t : 16 * t + 16], y[16 * (CHUNK + t) : 16 * (CHUNK + t) + 16]
                q = kept[c + t] + base + temper * heat
                kept[c + t] = q
                out_ref[c + t, l] = q.astype(jnp.bfloat16)
        for a in range(4):
            chosen[h, a, 4 * part + l] = kept[ids_ref[a]].astype(jnp.bfloat16)

    def several(i, carry):
        pend = None
        for k in range(UNROLL):
            l = UNROLL * i + k
            now = (l, moved[k % 2], moved_b[k % 2])
            advect(*now, towers[k % 2])
            if pend is not None:
                settle(*pend)
            pend = now
        settle(*pend)
        return carry

    lax.fori_loop(0, levels // UNROLL, several, 0)

    @pl.when(step == 0)
    def _():
        pl.semaphore_wait(barrier, DST - 1)

    @pl.when(step < 14)
    def _():
        send(step).start()

    @pl.when(step == 15)
    def _():
        mine = pltpu.make_async_copy(chosen.at[tile], place, own)
        mine.start()
        mine.wait()
        for d in range(14):
            send(d).wait()


def chemistry(tracers, winds, north, south, east, west, base, temp, ids, points):
    whole = lambda s, i, p: (0, 0)
    hbm = pl.BlockSpec(memory_space=pl.ANY)

    def rows(s, i, p):
        tile, part = tile_of_step(lax.axis_index("lon"), s)
        return (2 * tile + part, 0, 0)

    def cube(s, i, p):
        return (0,) + rows(s, i, p)

    def source(s, i, p):
        return (tile_of_step(lax.axis_index("lon"), s)[0], 0, 0)

    return pl.pallas_call(
        chem_kernel,
        grid_spec=pltpu.PrefetchScalarGridSpec(
            num_scalar_prefetch=2,
            grid=(16,),
            in_specs=[
                pl.BlockSpec((16, 4, 16, 256), cube),
                pl.BlockSpec((1, 384, 256), source),
                pl.BlockSpec((4, 16, 256), rows),
                pl.BlockSpec((4, 16, 256), rows),
                pl.BlockSpec((256, 128), whole),
                pl.BlockSpec((256, 128), whole),
                pl.BlockSpec((16, 16), whole),
                pl.BlockSpec((16, 16), whole),
            ],
            out_specs=[pl.BlockSpec((16, 4, 16, 256), cube), hbm],
            scratch_shapes=[
                pltpu.VMEM((2, 384, 128), jnp.float32),
                pltpu.VMEM((256, 128), jnp.float32),
                pltpu.VMEM((256, 128), jnp.float32),
                pltpu.VMEM((512, 256), jnp.bfloat16),
                pltpu.VMEM((2, 576, 128), jnp.float32),
                pltpu.VMEM((2, 576, 128), jnp.float32),
                pltpu.VMEM((16, 16, 256), jnp.float32),
                pltpu.VMEM((16, 16, 256), jnp.float32),
                pltpu.VMEM((256, 256), jnp.bfloat16),
                pltpu.VMEM((256, 256), jnp.bfloat16),
                pltpu.VMEM((8, 4, 8, 16, 256), jnp.bfloat16),
                pltpu.SemaphoreType.DMA((14,)),
                pltpu.SemaphoreType.DMA((14,)),
                pltpu.SemaphoreType.DMA,
            ],
        ),
        out_shape=[
            jax.ShapeDtypeStruct((16, 64, 16, 256), jnp.bfloat16),
            jax.ShapeDtypeStruct((4, 8, 16, 2048), jnp.bfloat16),
        ],
        compiler_params=pltpu.CompilerParams(collective_id=1, has_side_effects=True),
        name="chemistry",
    )(ids, points, tracers, winds, north, south, east, west, base, temp)


def body(spectral, legendre, wave_ids, points, tracers, react_base, react_temp, active_ids):
    winds, north, south, east, west = winds_of(
        spectral.reshape(48, 40, 1280), legendre, tracers, wave_ids, points
    )
    fresh, active = chemistry(
        tracers, winds, north, south, east, west, react_base, react_temp, active_ids, points
    )
    return (fresh, active.astype(jnp.float32))


def solution(mesh):
    in_specs = (
        P(None, LON, "lat", None),
        P("lat", None, None),
        P(),
        P("lat"),
        P(None, None, "lat", LON),
        P(),
        P(),
        P(),
    )
    out_specs = (P(None, None, "lat", LON), P(None, LON, "lat", None))
    return jax.shard_map(body, mesh=mesh, in_specs=in_specs, out_specs=out_specs, check_vma=False)
```

```python
import functools

import jax
import jax.numpy as jnp
from jax import lax
from jax.experimental import pallas as pl
from jax.experimental.pallas import tpu as pltpu
from jax.sharding import PartitionSpec as P

LON = "lon"


SRC = 16
PLANE = 136
UNROLL = 4
CHUNK = 8
DST = 8
MESH = pl.DeviceIdType.MESH
TILES = ((2, 1), (2, 0), (1, 1), (3, 0), (3, 1), (1, 0), (0, 1))
ORDER = ((2, 0), (0, 1), (2, 1), (1, 0), (3, 1), (1, 1), (3, 0))
BANDS = tuple((dz, dy, dc) for dz in (1, 0) for dy in (2, 1, 3, 0) for dc in (0, 1) if dz + dy + dc)
COS = (0.9999992006931535, -19.7389777615569, 64.92855937725766, -85.27036091136767,
       58.78399626476764, -21.059548245283555)
SIN = (6.283184911477688, -41.3415879428884, 81.59989458670537, -76.61384581975258,
       41.339653019987985, -12.465497972860707)


def tile_at(h, dx, dz, back=False):
    dx = (4 - dx) % 4 if back else dx
    return lax.rem(h // 2 + dx, 4) * 2 + lax.rem(lax.rem(h, 2) + dz, 2)


def band_at(g, dz, dy, dc):
    high = lax.rem(g // 8 + dz, 2)
    return high * 8 + lax.rem(lax.rem(g // 2, 4) + dy, 4) * 2 + lax.rem(lax.rem(g, 2) + dc, 2)


def tile_of_step(h, step):
    late = step // 14
    s = lax.rem(step, 7) * (1 - late) + 7 * late
    part = step // 7 - 2 * late + late * lax.rem(step, 2)
    two = (1 + lax.rem(s, 2)) * (1 + 3 * lax.rem(s // 2, 2)) * (1 + 15 * (s // 4))
    code_x = sum(dx * 4**k for k, (dx, dz) in enumerate(ORDER))
    code_z = sum(dz * 2**k for k, (dx, dz) in enumerate(ORDER))
    x = lax.rem(h // 2 + lax.rem(code_x // (two * two), 4), 4)
    return x * 2 + lax.rem(lax.rem(h, 2) + lax.rem(code_z // two, 2), 2), part


def waves_at(product, count, inverse):
    turns = jnp.round(product * inverse)
    t = (product - turns * count) * inverse
    s = t * t
    c = COS[-1]
    for k in COS[-2::-1]:
        c = c * s + k
    d = SIN[-1]
    for k in SIN[-2::-1]:
        d = d * s + k
    return c, d * t


def spectral_kernel(
    spec_ref, leg_ref, tr_ref, ids_ref, pts_ref,
    out_ref, north_ref, south_ref, east_ref, west_ref,
    spec, spread, leg, band, wide_0, wide_1, wide_2, wide_3, cols, low, high, edge, empty, blank_cols,
    rowid, laneid, tall, send_a, got_a, table, phase, coef, line, turned, send_b,
    sent_a, came_a, sent_b, came_b, own, sent_h, came_h, taken, leg_in, band_in,
):
    g, h = lax.axis_index("lat"), lax.axis_index("lon")
    barrier = pltpu.get_barrier_semaphore()
    for d in range(1, SRC):
        pl.semaphore_signal(barrier, inc=1, device_id=(lax.rem(g + d, SRC), h), device_id_type=MESH)
    for d in range(1, DST):
        pl.semaphore_signal(barrier, inc=1, device_id=(g, lax.rem(h + d, DST)), device_id_type=MESH)

    wide = (wide_0, wide_1, wide_2, wide_3)

    def leg_copy(i):
        slot = lax.rem(i, 5)
        return pltpu.make_async_copy(leg_ref.at[pl.ds(5 * i, 5)], leg.at[slot], leg_in.at[slot])

    def band_copy(i):
        slot = lax.rem(i, 2)
        return pltpu.make_async_copy(tr_ref.at[:, pl.ds(8 * i, 8)], band.at[slot], band_in.at[slot])

    spec_copy = pltpu.make_async_copy(spec_ref, spec, taken)
    band_copy(0).start()
    spec_copy.start()
    band_copy(1).start()
    place = lax.broadcasted_iota(jnp.int32, (8, 128), 1)
    for p in range(6):
        at, by = divmod(120 * p, 128)
        ids = jnp.broadcast_to(ids_ref[at : at + 1, :], (8, 128)).astype(jnp.float32)
        if by:
            ids = pltpu.roll(ids, 128 - by, 1)
        if 0 < by and at < 4:
            more = jnp.broadcast_to(ids_ref[at + 1 : at + 2, :], (8, 128)).astype(jnp.float32)
            ids = jnp.where(place < 128 - by, ids, pltpu.roll(more, 128 - by, 1))
        laneid[:, 128 * p : 128 * p + 128] = ids
        rowid[128 * p : 128 * p + 128, :] = jnp.broadcast_to(ids[:1], (128, 128)).T
    tall[...] = jnp.zeros_like(tall)
    empty[...] = jnp.zeros_like(empty)
    blank_cols[...] = jnp.zeros_like(blank_cols)
    cols[...] = jnp.zeros_like(cols)
    lane = lax.broadcasted_iota(jnp.int32, (256, 128), 1)

    shape = (128, 128)

    def tables(j, carry):
        count = jnp.full((1, 1), pts_ref[j], jnp.int32).astype(jnp.float32)
        inverse = 1.0 / count
        far = lax.broadcasted_iota(jnp.int32, (8, 128), 0).astype(jnp.float32) * 256.0
        lane = lax.broadcasted_iota(jnp.int32, shape, 1).astype(jnp.float32)
        for p in range(6):
            ids = laneid[:, pl.ds(128 * p, 128)]
            c, s = waves_at(ids * far, count, inverse)
            phase[j, 0, p] = c
            phase[j, 1, p] = s
        for p in range(6):
            ids = rowid[pl.ds(128 * p, 128), :]
            c, s = waves_at(ids * lane, count, inverse)
            c1 = jnp.broadcast_to(c[:, 64:65], shape)
            s1 = jnp.broadcast_to(s[:, 64:65], shape)
            c1, s1 = c1 * c1 - s1 * s1, 2.0 * c1 * s1
            table[j, pl.ds(128 * p, 128), pl.ds(0, 128)] = c.astype(jnp.bfloat16)
            table[j, pl.ds(768 + 128 * p, 128), pl.ds(0, 128)] = (-s).astype(jnp.bfloat16)
            table[j, pl.ds(128 * p, 128), pl.ds(128, 128)] = (c * c1 - s * s1).astype(jnp.bfloat16)
            table[j, pl.ds(768 + 128 * p, 128), pl.ds(128, 128)] = (-(s * c1 + c * s1)).astype(jnp.bfloat16)
        return carry

    def step(i, carry):
        slot = lax.rem(i, 5)
        leg_copy(i).wait()
        tables(i, 0)
        for w in range(5):
            m = 5 * i + w
            rows = [spread[k, pl.ds(m, 48, stride=40), :].astype(jnp.bfloat16) for k in range(10)]
            value = jnp.dot(jnp.concatenate(rows, axis=1), leg[slot, w], preferred_element_type=jnp.float32)
            for k in range(2):
                for q in range(6):
                    part = value[8 * q : 8 * q + 8, 128 * k : 128 * k + 128]
                    tall[k, pl.ds(20 * q + lax.rem(m, 20), 8, stride=PLANE), :] = part

        @pl.when(i < 3)
        def _():
            leg_copy(i + 5).start()

        return carry

    def edges(i, carry):
        @pl.when(i >= 3)
        def _():
            leg_copy(i - 3).start()

        for n in range(3):
            @pl.when(i == 2 * n + 3)
            def _():
                send_rows(n)

        side = lax.rem(i, 2)
        band_copy(i).wait()

        def level(l, carry):
            kept = cols[...]
            for n in range(4):
                at = 8 * i + 4 * l + n
                x = band[side, :, 4 * l + n].reshape(256, 256).astype(jnp.float32)
                for k in range(2):
                    wide[n][k] = x[:, 128 * k : 128 * k + 128]
                low[at] = rows_of(wide[n], 0, 16, 16).astype(jnp.bfloat16)
                high[at] = rows_of(wide[n], 15, 16, 16).astype(jnp.bfloat16)
                first = pltpu.roll(x[:, :128], at, 1)
                last = pltpu.roll(x[:, 128:], lax.rem(at + 65, 128), 1)
                kept = jnp.where(lane == at, first, jnp.where(lane == at + 64, last, kept))
            cols[...] = kept
            return carry

        lax.fori_loop(0, 2, level, 0)

        @pl.when(i < 6)
        def _():
            band_copy(i + 2).start()

        return carry

    def halo(k, src, dst, lat, lon):
        return pltpu.make_async_remote_copy(
            src_ref=src, dst_ref=dst, send_sem=sent_h.at[k], recv_sem=came_h.at[k],
            device_id=(lat, lon), device_id_type=MESH,
        )

    to_east = halo(0, edge, west_ref, g, lax.rem(h + 1, DST))
    to_west = halo(1, edge, east_ref, g, lax.rem(h + DST - 1, DST))

    def to_north(n):
        rows = pl.ds(16 * n, 16)
        return halo(2 + n, high.at[rows], south_ref.at[rows], lax.rem(g + 1, SRC), h)

    def to_south(n):
        rows = pl.ds(16 * n, 16)
        return halo(6 + n, low.at[rows], north_ref.at[rows], lax.rem(g + SRC - 1, SRC), h)

    def send_rows(n):
        @pl.when(g < SRC - 1)
        def _():
            to_north(n).start()

        @pl.when(g > 0)
        def _():
            to_south(n).start()

    none_south = pltpu.make_async_copy(empty, south_ref, own.at[5])
    none_north = pltpu.make_async_copy(empty, north_ref, own.at[6])
    none_west = pltpu.make_async_copy(blank_cols, west_ref, own.at[7])
    none_east = pltpu.make_async_copy(blank_cols, east_ref, own.at[8])
    fills = ((g == 0, none_south), (g == SRC - 1, none_north), (h == 0, none_west), (h == DST - 1, none_east))
    pl.semaphore_wait(barrier, SRC + DST - 2)
    lax.fori_loop(0, 8, edges, 0)
    edge[...] = cols[...].astype(jnp.bfloat16)
    send_rows(3)
    pl.when(h < DST - 1)(to_east.start)
    pl.when(h > 0)(to_west.start)
    for here, fill in fills:
        pl.when(here)(fill.start)

    def turn(half):
        def pair(i, carry):
            for k in range(2):
                blocks = [tall[k, pl.ds(PLANE * (2 * i + n), 128), :].T for n in range(2)]
                for b in range(8):
                    for rows in range(2):
                        at = 16 * b + 8 * rows
                        both = jnp.concatenate([block[at : at + 8] for block in blocks], axis=0)
                        send_a[8 * k + b, half, rows, pl.ds(16 * i, 16), :] = both.astype(jnp.bfloat16)
            return carry

        lax.fori_loop(0, 4, pair, 0)

    def copy_a(d, k):
        to = band_at(g, *BANDS[d - 1])
        src, dst = ((send_a.at[to, 0], got_a.at[g, 0]), (send_a.at[to, 1, 0], got_a.at[g, 1, 0]),
                    (send_a.at[to, 1, 1], got_a.at[g, 1, 1]))[k]
        return pltpu.make_async_remote_copy(
            src_ref=src, dst_ref=dst, send_sem=sent_a.at[k, d], recv_sem=came_a.at[k, d],
            device_id=(to, h), device_id_type=MESH,
        )

    spec_copy.wait()

    def loosen(i, carry):
        for r in range(4):
            for k in range(10):
                part = spec[4 * i + r, :, 128 * k : 128 * k + 128]
                spread[k, pl.ds(160 * i + 40 * r, 40), :] = part.astype(jnp.float32)
        return carry

    lax.fori_loop(0, 12, loosen, 0)
    lax.fori_loop(0, 4, step, 0)
    turn(0)
    for d in range(1, SRC):
        copy_a(d, 0).start()
    lax.fori_loop(4, 8, step, 0)
    turn(1)
    for k in (1, 2):
        for d in range(1, SRC):
            copy_a(d, k).start()
    mine = pltpu.make_async_copy(send_a.at[g], got_a.at[g], own.at[0])
    mine.start()
    lax.fori_loop(8, 12, tables, 0)
    mine.wait()

    def widen(rows):
        def one(q, carry):
            for half in range(2):
                coef[pl.ds(64 * (2 * q + half), 64), :] = got_a[q, half, rows].astype(jnp.float32)
            return carry

        lax.fori_loop(0, SRC, one, 0)

    def turn_of(j):
        lane = lax.broadcasted_iota(jnp.int32, (8, 128), 1)
        row = lax.rem(j, 8)
        for p in range(6):
            count = min(6, 2 * SRC - 6 * p)
            held = [coef[pl.ds(64 * (6 * p + q) + row, 8, stride=8), :] for q in range(count)]
            for f in range(6):
                value = jnp.zeros((8, 128), jnp.float32)
                for q in range(count):
                    moved = held[q] if q == f else pltpu.roll(held[q], (20 * (q - f)) % 128, 1)
                    value = jnp.where((lane >= 20 * q) & (lane < 20 * q + 20), moved, value)
                line[f // 2, f % 2, p] = value
        for p in range(6):
            for a in range(0, DST, 2):
                parts = []
                for b in range(6):
                    row, f = a + b // 3, b % 3
                    c = phase[j, 0, p, row : row + 1, :]
                    s = phase[j, 1, p, row : row + 1, :]
                    re, im = line[f, 0, p], line[f, 1, p]
                    parts.append((re * c - im * s, re * s + im * c))
                for b in range(0, 6, 2):
                    at = 24 * a + 8 * b
                    for k in range(2):
                        pair = jnp.concatenate([parts[b][k], parts[b + 1][k]], axis=0)
                        turned[at : at + 16, 768 * k + 128 * p : 768 * k + 128 * p + 128] = pair.astype(jnp.bfloat16)
        out = jnp.dot(turned[...], table[j], preferred_element_type=jnp.float32)
        return out * (640.0 ** -0.5)

    def copy_b(d, c):
        to = tile_at(h, *TILES[d - 1])
        return pltpu.make_async_remote_copy(
            src_ref=send_b.at[c, to], dst_ref=out_ref.at[h, pl.ds(96 * c, 96), :],
            send_sem=sent_b.at[c, d], recv_sem=came_b.at[c, d], device_id=(g, to), device_id_type=MESH,
        )

    def copy_own(c):
        return pltpu.make_async_copy(send_b.at[c, h], out_ref.at[h, pl.ds(96 * c, 96), :], own.at[1 + c])

    def quad(c, carry):
        for jj in range(2):
            one = turn_of(4 * c + 2 * jj)
            two = turn_of(4 * c + 2 * jj + 1)
            for a in range(DST):
                both = jnp.concatenate([one[24 * a : 24 * a + 24], two[24 * a : 24 * a + 24]], axis=0)
                send_b[c, a, pl.ds(48 * jj, 48), :] = both.astype(jnp.bfloat16)
        for d in range(1, DST):
            copy_b(d, c).start()
        copy_own(c).start()
        return carry

    for rows in range(2):
        for k in ((0, 1), (2,))[rows]:
            for d in range(1, SRC):
                copy_a(d, k).wait_recv()
        widen(rows)
        lax.fori_loop(2 * rows, 2 * rows + 2, quad, 0)
        if rows == 0:
            lax.fori_loop(12, 16, tables, 0)
    for k in range(3):
        for d in range(1, SRC):
            copy_a(d, k).wait_send()

    def finish(c, carry):
        copy_own(c).wait()
        for d in range(1, DST):
            copy_b(d, c).wait()
        return carry

    lax.fori_loop(0, 4, finish, 0)
    pl.when(h < DST - 1)(to_east.wait_send)
    pl.when(h > 0)(to_west.wait_send)
    pl.when(h > 0)(to_east.wait_recv)
    pl.when(h < DST - 1)(to_west.wait_recv)
    for n in range(4):
        pl.when(g < SRC - 1)(to_north(n).wait_send)
        pl.when(g > 0)(to_south(n).wait_send)
        pl.when(g > 0)(to_north(n).wait_recv)
        pl.when(g < SRC - 1)(to_south(n).wait_recv)
    for here, fill in fills:
        pl.when(here)(fill.wait)


def winds_of(spectral, legendre, tracers, wave_ids, points):
    vmem = pl.BlockSpec(memory_space=pltpu.VMEM)
    hbm = pl.BlockSpec(memory_space=pl.ANY)
    return pl.pallas_call(
        spectral_kernel,
        in_specs=[hbm, hbm, hbm, vmem, pl.BlockSpec(memory_space=pltpu.SMEM)],
        out_specs=[hbm] * 5,
        out_shape=[
            jax.ShapeDtypeStruct((8, 384, 256), jnp.bfloat16),
            jax.ShapeDtypeStruct((64, 16, 256), jnp.bfloat16),
            jax.ShapeDtypeStruct((64, 16, 256), jnp.bfloat16),
            jax.ShapeDtypeStruct((256, 128), jnp.bfloat16),
            jax.ShapeDtypeStruct((256, 128), jnp.bfloat16),
        ],
        scratch_shapes=[
            pltpu.VMEM((48, 40, 1280), jnp.bfloat16),
            pltpu.VMEM((10, 1920, 128), jnp.float32),
            pltpu.VMEM((5, 5, 1280, 256), jnp.bfloat16),
            pltpu.VMEM((2, 16, 8, 16, 256), jnp.bfloat16),
            pltpu.VMEM((2, 256, 128), jnp.float32),
            pltpu.VMEM((2, 256, 128), jnp.float32),
            pltpu.VMEM((2, 256, 128), jnp.float32),
            pltpu.VMEM((2, 256, 128), jnp.float32),
            pltpu.VMEM((256, 128), jnp.float32),
            pltpu.VMEM((64, 16, 256), jnp.bfloat16),
            pltpu.VMEM((64, 16, 256), jnp.bfloat16),
            pltpu.VMEM((256, 128), jnp.bfloat16),
            pltpu.VMEM((64, 16, 256), jnp.bfloat16),
            pltpu.VMEM((256, 128), jnp.bfloat16),
            pltpu.VMEM((768, 128), jnp.float32),
            pltpu.VMEM((8, 768), jnp.float32),
            pltpu.VMEM((2, 8 * PLANE, 128), jnp.float32),
            pltpu.VMEM((16, 2, 2, 64, 128), jnp.bfloat16),
            pltpu.VMEM((16, 2, 2, 64, 128), jnp.bfloat16),
            pltpu.VMEM((16, 1536, 256), jnp.bfloat16),
            pltpu.VMEM((16, 2, 6, 8, 128), jnp.float32),
            pltpu.VMEM((2048, 128), jnp.float32),
            pltpu.VMEM((3, 2, 6, 8, 128), jnp.float32),
            pltpu.VMEM((192, 1536), jnp.bfloat16),
            pltpu.VMEM((4, 8, 96, 256), jnp.bfloat16),
            pltpu.SemaphoreType.DMA((3, 16)),
            pltpu.SemaphoreType.DMA((3, 16)),
            pltpu.SemaphoreType.DMA((4, 8)),
            pltpu.SemaphoreType.DMA((4, 8)),
            pltpu.SemaphoreType.DMA((9,)),
            pltpu.SemaphoreType.DMA((10,)),
            pltpu.SemaphoreType.DMA((10,)),
            pltpu.SemaphoreType.DMA,
            pltpu.SemaphoreType.DMA((5,)),
            pltpu.SemaphoreType.DMA((2,)),
        ],
        compiler_params=pltpu.CompilerParams(
            collective_id=0, has_side_effects=True, vmem_limit_bytes=60 * 1024 * 1024
        ),
        name="winds",
    )(spectral, legendre, tracers, wave_ids.reshape(5, 128), points)


def rows_of(ref, start, size, stride):
    return jnp.concatenate([ref[k, pl.ds(start, size, stride=stride), :] for k in range(2)], axis=1)


def chem_kernel(
    ids_ref, pts_ref, tr_ref, wind_ref, north_ref, south_ref, east_ref, west_ref, base_ref, temp_ref, *rest
):
    out_ref, got_ref, wide, east, west, mix, *kept = rest
    towers, moved, moved_b = kept[:2], kept[2:4], kept[4:6]
    chosen, sent, came, own = kept[6:]
    step = pl.program_id(0)
    g, tile = lax.axis_index("lat"), lax.axis_index("lon")
    h, part = tile_of_step(tile, step)
    levels = out_ref.shape[1]
    barrier = pltpu.get_barrier_semaphore()

    place = got_ref.at[:, :, :, pl.ds(pl.multiple_of(tile * 256, 256), 256)]

    def send(d):
        to, some = tile_of_step(tile, d)
        rows = pl.ds(4 * some, 4)
        return pltpu.make_async_remote_copy(
            src_ref=chosen.at[to, :, rows], dst_ref=place.at[:, rows], send_sem=sent.at[d], recv_sem=came.at[d],
            device_id=(g, to), device_id_type=MESH,
        )

    @pl.when(step == 0)
    def _():
        for d in range(1, DST):
            pl.semaphore_signal(barrier, inc=1, device_id=(g, lax.rem(tile + d, DST)), device_id_type=MESH)
        east[...] = east_ref[...].astype(jnp.float32)
        west[...] = west_ref[...].astype(jnp.float32)
        row = lax.broadcasted_iota(jnp.int32, (256, 16), 0)
        col = lax.broadcasted_iota(jnp.int32, (256, 16), 1)
        spread = jnp.where(row // 16 == col, 1.0, 0.0).astype(jnp.bfloat16)
        row = lax.broadcasted_iota(jnp.int32, (256, 256), 0)
        col = lax.broadcasted_iota(jnp.int32, (256, 256), 1)
        same = row % 16 == col % 16
        for k, ref in enumerate((base_ref, temp_ref)):
            rows = jnp.dot(spread, ref[...].astype(jnp.bfloat16), preferred_element_type=jnp.float32)
            full = lax.dot_general(
                rows.astype(jnp.bfloat16), spread, (((1,), (1,)), ((), ())), preferred_element_type=jnp.float32
            )
            full = jnp.where(same, full, 0.0).astype(jnp.bfloat16)
            for c in range(0, 16, CHUNK):
                mix[pl.ds(32 * c + 16 * CHUNK * k, 16 * CHUNK), :] = full[16 * c : 16 * (c + CHUNK)]

    for k in range(2):
        wide[k] = wind_ref[0, :, 128 * k : 128 * k + 128].astype(jnp.float32)
    lane = lax.broadcasted_iota(jnp.int32, (16, 128), 1)
    row = lax.broadcasted_iota(jnp.int32, (16, 256), 0)
    limit = jnp.zeros((16, 256), jnp.int32)
    for j in range(16):
        limit = jnp.where(row == j, pts_ref[j], limit)
    column = lax.broadcasted_iota(jnp.int32, (16, 256), 1) + tile * 256
    mask = jnp.where(column < limit, 1.0, 0.0)

    def advect(l, kept, kept_b, tower):
        at = h * 8 + 4 * part + l
        local = 4 * part + l
        u = 0.1 * rows_of(wide, local, 16, 24)
        v = 0.1 * rows_of(wide, 8 + local, 16, 24)
        east_w, west_w = (0.05 - u) * mask, (0.05 + u) * mask
        north_w, south_w = (0.05 - v) * mask, (0.05 + v) * mask
        own_w = 0.8 * mask
        for k in range(2):
            half = slice(128 * k, 128 * k + 128)
            tower[k, pl.ds(0, 16, stride=36), :] = south_ref[l, :, half].astype(jnp.float32)
            tower[k, pl.ds(34, 16, stride=36), :] = north_ref[l, :, half].astype(jnp.float32)
        for t in range(16):
            x = tr_ref[t, l].astype(jnp.float32)
            xl, xr = x[:, :128], x[:, 128:]
            for k, part_x in enumerate((xl, xr)):
                tower[k, pl.ds(36 * t + 2, 16, stride=2), :] = part_x
            he = pltpu.roll(east[pl.ds(16 * t, 16), :], 127 - at, 1)
            hw = pltpu.roll(west[pl.ds(16 * t, 16), :], 64 - at, 1)
            el, er = pltpu.roll(xl, 127, 1), pltpu.roll(xr, 127, 1)
            wl, wr = pltpu.roll(xl, 1, 1), pltpu.roll(xr, 1, 1)
            xe = jnp.concatenate([jnp.where(lane == 127, er, el), jnp.where(lane == 127, he, er)], axis=1)
            xw = jnp.concatenate([jnp.where(lane == 0, hw, wl), jnp.where(lane == 0, wl, wr)], axis=1)
            xn = rows_of(tower, 36 * t + 4, 16, 2)
            xs = rows_of(tower, 36 * t, 16, 2)
            q = own_w * x + east_w * xe + west_w * xw + north_w * xn + south_w * xs
            kept[t] = q
            kept_b[pl.ds(16 * t, 16), :] = q.astype(jnp.bfloat16)

    def settle(l, kept, kept_b):
        temper = rows_of(wide, 16 + 4 * part + l, 16, 24)
        for c in range(0, 16, CHUNK):
            y = jnp.dot(mix[pl.ds(32 * c, 32 * CHUNK), :], kept_b[...], preferred_element_type=jnp.float32)
            for t in range(CHUNK):
                base, heat = y[16 * t : 16 * t + 16], y[16 * (CHUNK + t) : 16 * (CHUNK + t) + 16]
                q = kept[c + t] + base + temper * heat
                kept[c + t] = q
                out_ref[c + t, l] = q.astype(jnp.bfloat16)
        for a in range(4):
            chosen[h, a, 4 * part + l] = kept[ids_ref[a]].astype(jnp.bfloat16)

    def several(i, carry):
        pend = None
        for k in range(UNROLL):
            l = UNROLL * i + k
            now = (l, moved[k % 2], moved_b[k % 2])
            advect(*now, towers[k % 2])
            if pend is not None:
                settle(*pend)
            pend = now
        settle(*pend)
        return carry

    lax.fori_loop(0, levels // UNROLL, several, 0)

    @pl.when(step == 0)
    def _():
        pl.semaphore_wait(barrier, DST - 1)

    @pl.when(step < 14)
    def _():
        send(step).start()

    @pl.when(step == 15)
    def _():
        mine = pltpu.make_async_copy(chosen.at[tile], place, own)
        mine.start()
        mine.wait()
        for d in range(14):
            send(d).wait()


def chemistry(tracers, winds, north, south, east, west, base, temp, ids, points):
    whole = lambda s, i, p: (0, 0)
    hbm = pl.BlockSpec(memory_space=pl.ANY)

    def rows(s, i, p):
        tile, part = tile_of_step(lax.axis_index("lon"), s)
        return (2 * tile + part, 0, 0)

    def cube(s, i, p):
        return (0,) + rows(s, i, p)

    def source(s, i, p):
        return (tile_of_step(lax.axis_index("lon"), s)[0], 0, 0)

    return pl.pallas_call(
        chem_kernel,
        grid_spec=pltpu.PrefetchScalarGridSpec(
            num_scalar_prefetch=2,
            grid=(16,),
            in_specs=[
                pl.BlockSpec((16, 4, 16, 256), cube),
                pl.BlockSpec((1, 384, 256), source),
                pl.BlockSpec((4, 16, 256), rows),
                pl.BlockSpec((4, 16, 256), rows),
                pl.BlockSpec((256, 128), whole),
                pl.BlockSpec((256, 128), whole),
                pl.BlockSpec((16, 16), whole),
                pl.BlockSpec((16, 16), whole),
            ],
            out_specs=[pl.BlockSpec((16, 4, 16, 256), cube), hbm],
            scratch_shapes=[
                pltpu.VMEM((2, 384, 128), jnp.float32),
                pltpu.VMEM((256, 128), jnp.float32),
                pltpu.VMEM((256, 128), jnp.float32),
                pltpu.VMEM((512, 256), jnp.bfloat16),
                pltpu.VMEM((2, 576, 128), jnp.float32),
                pltpu.VMEM((2, 576, 128), jnp.float32),
                pltpu.VMEM((16, 16, 256), jnp.float32),
                pltpu.VMEM((16, 16, 256), jnp.float32),
                pltpu.VMEM((256, 256), jnp.bfloat16),
                pltpu.VMEM((256, 256), jnp.bfloat16),
                pltpu.VMEM((8, 4, 8, 16, 256), jnp.bfloat16),
                pltpu.SemaphoreType.DMA((14,)),
                pltpu.SemaphoreType.DMA((14,)),
                pltpu.SemaphoreType.DMA,
            ],
        ),
        out_shape=[
            jax.ShapeDtypeStruct((16, 64, 16, 256), jnp.bfloat16),
            jax.ShapeDtypeStruct((4, 8, 16, 2048), jnp.bfloat16),
        ],
        compiler_params=pltpu.CompilerParams(collective_id=1, has_side_effects=True),
        name="chemistry",
    )(ids, points, tracers, winds, north, south, east, west, base, temp)


def body(spectral, legendre, wave_ids, points, tracers, react_base, react_temp, active_ids):
    winds, north, south, east, west = winds_of(
        spectral.reshape(48, 40, 1280), legendre, tracers, wave_ids, points
    )
    fresh, active = chemistry(
        tracers, winds, north, south, east, west, react_base, react_temp, active_ids, points
    )
    return (fresh, active.astype(jnp.float32))


def solution(mesh):
    in_specs = (
        P(None, LON, "lat", None),
        P("lat", None, None),
        P(),
        P("lat"),
        P(None, None, "lat", LON),
        P(),
        P(),
        P(),
    )
    out_specs = (P(None, None, "lat", LON), P(None, LON, "lat", None))
    return jax.shard_map(body, mesh=mesh, in_specs=in_specs, out_specs=out_specs, check_vma=False)
```
